256 devices in a mesh: gx: 8 (over y, core), gy: 32 (over x, z).
Axes of the slice: x: 4, y: 4, z: 8, core: 2. Of those that a mesh axis runs over, the one named last changes fastest.
Arguments:
- flow_field: float32 [16, 256, 256, 128], P(None, 'gx', 'gy'), may hold values from -6 to 6
- cotangent: float32 [16, 256, 256, 128], P(None, 'gx', 'gy'), may hold values from -6 to 6
- mode_weights: float32 [4, 16, 16, 256], replicated, may hold values from -3 to 3
- point_weights: float32 [16, 16], replicated, may hold values from -1.5 to 1.5
- point_bias: float32 [16], replicated, may hold values from -3 to 3
Outputs:
- output_field: float32 [16, 256, 256, 128], P(None, 'gx', 'gy')
- grad_field: float32 [16, 256, 256, 128], P(None, 'gx', 'gy')
- grad_modes: float32 [4, 16, 16, 256], replicated
- grad_point: float32 [16, 16], replicated
- grad_bias: float32 [16], replicated
The draws below stay inside these ranges and needn't reach their ends.
All inputs are finite; a program needn't handle non-finite values.
Results may differ from the reference program's by a relative error of at most 0.00024.
Values sent between devices are 32-bit elements; how exact they have to be, the bound alone decides.
No kernel may reach another device: no remote copies, remote signals or barrier semaphores. Data moves between devices by JAX's collectives and lax.ppermute only.
A program may use at most 128 MiB of HBM per device.

```python
import math
import jax
import jax.numpy as jnp
from jax import lax

CH = 16
NX = 256
NY = 256
NZ = 128
MX = 16
MY = 16


def shard_levels(stream_key, shape, split, least, high):
    def one(dim, shards_of):
        steps = jax.random.uniform(jax.random.fold_in(jax.random.fold_in(stream_key, 6), dim), (shards_of,), jnp.float32, least / len(split), high / len(split))
        return jnp.repeat(jnp.exp(steps), shape[dim] // shards_of).reshape((-1,) + (1,) * (len(shape) - dim - 1))

    factor_of = one(*split[0])
    for cut in split[1:]:
        factor_of = factor_of * one(*cut)
    return factor_of


def bell_draw(stream_key, extent, deviation, bound, split=(), kind=jnp.bfloat16):
    array = jax.random.normal(stream_key, extent, jnp.float32) * deviation
    if len(split) > 0:
        array = shard_levels(stream_key, extent, split, -0.22, 0.18) * array
    return jnp.clip(array, min=-bound, max=bound).astype(kind)


def setup_inputs(seed: int = 0) -> dict:
    key_of = jax.random.split(jax.random.key(seed), 6)
    flow_field = bell_draw(key_of[0], (CH, NX, NY, NZ), 1.0, 6.0, ((1, 8), (2, 32)), jnp.float32)
    cotangent = bell_draw(key_of[1], (CH, NX, NY, NZ), 1.0, 6.0, ((1, 8), (2, 32)), jnp.float32)
    mode_weights = bell_draw(key_of[2], (4, CH, CH, MX * MY), 0.5, 3.0, (), jnp.float32)
    point_weights = bell_draw(key_of[3], (CH, CH), CH ** -0.5, 1.5, (), jnp.float32)
    point_bias = bell_draw(key_of[4], (CH,), 0.5, 3.0, (), jnp.float32)
    return {"flow_field": flow_field, "cotangent": cotangent, "mode_weights": mode_weights, "point_weights": point_weights, "point_bias": point_bias}


LOW_PASS = [0.23037781330885523, 0.7148465705525415, 0.6308807679295904, -0.02798376941698385, -0.18703481171888114, 0.030841381835986965, 0.032883011666982945, -0.010597401784997278]
HIGH_PASS = [(-1) ** position * LOW_PASS[7 - position] for position in range(8)]
GELU_SCALE = 0.7978845608028654
GELU_CUBE = 0.044715

def filter_table(filter_taps, out_count, in_count, periodic):
    row_index = lax.broadcasted_iota(jnp.int32, (out_count, in_count), 0)
    col_index = lax.broadcasted_iota(jnp.int32, (out_count, in_count), 1)
    offset = col_index - 2 * row_index
    if periodic:
        offset = offset % in_count
    matrix = jnp.zeros((out_count, in_count), jnp.float32)
    for position in range(8):
        matrix = matrix + filter_taps[position] * (offset == position).astype(jnp.float32)
    return matrix

def along_x(matrix, signal):
    return jnp.einsum('kr,abry->abky', matrix, signal, precision=lax.Precision.HIGHEST)

def along_y(matrix, signal):
    return jnp.einsum('kr,abxr->abxk', matrix, signal, precision=lax.Precision.HIGHEST)

def low_low(signal):
    extent_x, extent_y = (signal.shape[2], signal.shape[3])
    signal = along_x(filter_table(LOW_PASS, extent_x // 2, extent_x, True), signal)
    return along_y(filter_table(LOW_PASS, extent_y // 2, extent_y, True), signal)

def low_low_back(signal):
    extent_x, extent_y = (signal.shape[2], signal.shape[3])
    signal = along_x(filter_table(LOW_PASS, extent_x, 2 * extent_x, True).T, signal)
    return along_y(filter_table(LOW_PASS, extent_y, 2 * extent_y, True).T, signal)

def four_bands(signal):
    extent_x, extent_y = (signal.shape[2], signal.shape[3])
    low_x = along_x(filter_table(LOW_PASS, extent_x // 2, extent_x, True), signal)
    high_x = along_x(filter_table(HIGH_PASS, extent_x // 2, extent_x, True), signal)
    low_y = filter_table(LOW_PASS, extent_y // 2, extent_y, True)
    high_y = filter_table(HIGH_PASS, extent_y // 2, extent_y, True)
    return jnp.stack([along_y(low_y, low_x), along_y(low_y, high_x), along_y(high_y, low_x), along_y(high_y, high_x)])

def join_bands(changes):
    modes_x, modes_y = (changes.shape[3], changes.shape[4])
    low_x = filter_table(LOW_PASS, modes_x, 2 * modes_x, True).T
    high_x = filter_table(HIGH_PASS, modes_x, 2 * modes_x, True).T
    low_y = filter_table(LOW_PASS, modes_y, 2 * modes_y, True).T
    high_y = filter_table(HIGH_PASS, modes_y, 2 * modes_y, True).T
    from_low = along_y(low_y, changes[0]) + along_y(high_y, changes[2])
    from_high = along_y(low_y, changes[1]) + along_y(high_y, changes[3])
    return along_x(low_x, from_low) + along_x(high_x, from_high)

def descend(signal):
    for repeat in range(3):
        signal = low_low(signal)
    return four_bands(signal)

def ascend(changes):
    delta_level = join_bands(changes)
    for repeat in range(3):
        delta_level = low_low_back(delta_level)
    return delta_level

def mix_forward(wave_bands, mode_weights):
    return jnp.einsum('bzixy,bioxy->bzoxy', wave_bands, mode_weights, precision=lax.Precision.HIGHEST)

def mix_back(wave_bands, mode_weights):
    return jnp.einsum('bzoxy,bioxy->bzixy', wave_bands, mode_weights, precision=lax.Precision.HIGHEST)

def gelu_parts(signal):
    tangent = jnp.tanh(GELU_SCALE * (signal + GELU_CUBE * signal * signal * signal))
    activated = 0.5 * signal * (1.0 + tangent)
    gelu_slope = 0.5 * (1.0 + tangent) + 0.5 * signal * (1.0 - tangent * tangent) * GELU_SCALE * (1.0 + 3.0 * GELU_CUBE * signal * signal)
    return (activated, gelu_slope)

def reference(flow_field, cotangent, mode_weights, point_weights, point_bias):
    planes_flow = jnp.transpose(flow_field, (3, 0, 1, 2))
    planes_cot = jnp.transpose(cotangent, (3, 0, 1, 2))
    weights_grid = mode_weights.reshape(4, CH, CH, MX, MY)

    def one_plane(plane_pair):
        field_plane = plane_pair[0][None]
        cot_plane = plane_pair[1][None]
        bands_flow = descend(field_plane)
        spectral = field_plane + ascend(mix_forward(bands_flow, weights_grid) - bands_flow)
        pointwise = jnp.einsum('io,zixy->zoxy', point_weights, field_plane, precision=lax.Precision.HIGHEST)
        before_gelu = spectral + pointwise + point_bias[None, :, None, None]
        activated, gelu_slope = gelu_parts(before_gelu)
        grad_inner = cot_plane * gelu_slope
        bands_grad = descend(grad_inner)
        point_back = jnp.einsum('io,zoxy->zixy', point_weights, grad_inner, precision=lax.Precision.HIGHEST)
        grad_plane = grad_inner + ascend(mix_back(bands_grad, weights_grid) - bands_grad) + point_back
        mode_term = jnp.einsum('bzixy,bzoxy->bioxy', bands_flow, bands_grad, precision=lax.Precision.HIGHEST)
        point_term = jnp.einsum('zixy,zoxy->io', field_plane, grad_inner, precision=lax.Precision.HIGHEST)
        bias_term = lax.optimization_barrier(jnp.sum(grad_inner, axis=(0, 2, 3)))
        return (activated[0], grad_plane[0], mode_term, point_term, bias_term)
    per_plane = lax.map(one_plane, (planes_flow, planes_cot))
    cell_count = NZ * NX * NY
    grad_modes = (lax.optimization_barrier(jnp.sum(per_plane[2], 0)) / math.sqrt(NZ)).reshape(4, CH, CH, MX * MY)
    grad_point = lax.optimization_barrier(jnp.sum(per_plane[3], 0)) / math.sqrt(cell_count)
    grad_bias = lax.optimization_barrier(jnp.sum(per_plane[4], 0)) / math.sqrt(cell_count)
    output_field = jnp.transpose(per_plane[0], (1, 2, 3, 0))
    grad_field = jnp.transpose(per_plane[1], (1, 2, 3, 0))
    return (output_field, grad_field, grad_modes, grad_point, grad_bias)
```

```python
import math

import jax
import jax.numpy as jnp
import numpy as np
from jax import lax
from jax.experimental import pallas as pl
from jax.experimental.pallas import tpu as pltpu
from jax.sharding import PartitionSpec as P

LOW_PASS = [
    0.23037781330885523,
    0.7148465705525415,
    0.6308807679295904,
    -0.02798376941698385,
    -0.18703481171888114,
    0.030841381835986965,
    0.032883011666982945,
    -0.010597401784997278,
]
HIGH_PASS = [(-1) ** position * LOW_PASS[7 - position] for position in range(8)]
GELU_SCALE = 0.7978845608028654
GELU_CUBE = 0.044715


def triple_low():
    taps = np.zeros(50)
    for p, hp in enumerate(LOW_PASS):
        for q, hq in enumerate(LOW_PASS):
            for r, hr in enumerate(LOW_PASS):
                taps[p + 2 * q + 4 * r] += hp * hq * hr
    return [float(t) for t in taps]


TRIPLE = triple_low()
HIGHEST = lax.Precision.HIGHEST
F32 = jnp.float32
VMEM = pltpu.CompilerParams(vmem_limit_bytes=56 * 1024 * 1024)


def tap(position, coef):
    at = position + 48 - 8 * coef
    return TRIPLE[at] if 0 <= at < 50 else None


def y_table():
    table = np.zeros((32, 8, 128), np.float32)
    for slab in range(32):
        for b in range(7):
            ky = (slab - 6 + b) % 32
            for mode in range(16):
                at = (ky - 2 * mode) % 32
                if at < 8:
                    table[slab, b, mode] = LOW_PASS[at]
                    table[slab, b, 16 + mode] = HIGH_PASS[at]
    return table.reshape(256, 128)


def gather_sum(pairs):
    total = None
    for weight, value in pairs:
        term = value * weight
        total = term if total is None else total + term
    return total


def swap_blocks(rows):
    lane = lax.broadcasted_iota(jnp.int32, (8, 128), 1)
    rows = list(rows)
    for bit in range(3):
        width = 16 << bit
        upper = (lane & width) != 0
        for lo in range(8):
            if lo & (1 << bit):
                continue
            hi = lo | (1 << bit)
            first, second = rows[lo], rows[hi]
            rows[lo] = jnp.where(upper, pltpu.roll(second, width, 1), first)
            rows[hi] = jnp.where(upper, second, pltpu.roll(first, 128 - width, 1))
    return rows


def partial_columns(x_scr, p_scr):
    def body(a, carry):
        cols = [x_scr[a, y] for y in range(8)]
        for b in range(7):
            pairs = [(tap(y, b), cols[y]) for y in range(8) if tap(y, b) is not None]
            p_scr[pl.ds(pl.multiple_of((a * 7 + b) * 16, 16), 16), :] = gather_sum(pairs)
        return carry

    lax.fori_loop(0, 10, body, 0)
    p_scr[pl.ds(1120, 32), :] = jnp.zeros((32, 128), F32)


def pack_planes(p_scr, s_ref):
    def body(octet, carry):
        for half in range(2):
            rows = [p_scr[pl.ds(octet * 128 + half * 8 + c, 8, stride=16), :] for c in range(8)]
            rows = swap_blocks(rows)
            for group in range(8):
                s_ref[group, half, pl.ds(pl.multiple_of(octet * 8, 8), 8), :] = rows[group]
        return carry

    lax.fori_loop(0, 9, body, 0)


def unpack_planes(r_ref, d_scr):
    def body(octet, carry):
        for half in range(2):
            rows = [
                r_ref[group, half, pl.ds(pl.multiple_of(octet * 8, 8), 8), :] for group in range(8)
            ]
            rows = swap_blocks(rows)
            for c in range(8):
                d_scr[pl.ds(octet * 128 + half * 8 + c, 8, stride=16), :] = rows[c]
        return carry

    lax.fori_loop(0, 9, body, 0)


def lift_columns(d_scr, e_scr):
    def body(a, carry):
        coefs = [d_scr[pl.ds(pl.multiple_of((a * 7 + b) * 16, 16), 16), :] for b in range(7)]
        for y in range(8):
            pairs = [(tap(y, b), coefs[b]) for b in range(7) if tap(y, b) is not None]
            e_scr[y, a] = gather_sum(pairs)
        return carry

    lax.fori_loop(0, 10, body, 0)


def analyse_kernel(flow_ref, s_ref, f_ref, x_scr, p_scr):
    def body(y, carry):
        sums = [None] * 10
        for x in range(32):
            value = flow_ref[pl.ds(x * 8 + y, 16, stride=256), :]
            f_ref[y, x * 16 : (x + 1) * 16, :] = value
            for a in range(10):
                weight = tap(x, a)
                if weight is not None:
                    term = value * weight
                    sums[a] = term if sums[a] is None else sums[a] + term
        for a in range(10):
            x_scr[a, y] = sums[a]
        return carry

    lax.fori_loop(0, 8, body, 0)
    partial_columns(x_scr, p_scr)
    pack_planes(p_scr, s_ref)


def rows_body(r_ref, l_scr, v_ref):
    def collect(q, carry):
        one = (q + 1) % 8
        two = (q + 2) % 8
        for t in range(4):
            for half in range(2):
                total = r_ref[q, half, 7 * (6 + t) : 7 * (6 + t) + 8, :]
                total = total + r_ref[one, half, 7 * (2 + t) : 7 * (2 + t) + 8, :]
                if t >= 2:
                    total = total + r_ref[two, half, 7 * (t - 2) : 7 * (t - 2) + 8, :]
                l_scr[q * 4 + t, half] = total
        return carry

    lax.fori_loop(0, 8, collect, 0)

    def bands(mode, carry):
        for half in range(2):
            parts = [l_scr[(2 * mode + n) % 32, half] for n in range(8)]
            v_ref[mode, half] = gather_sum(list(zip(LOW_PASS, parts)))
            v_ref[mode + 16, half] = gather_sum(list(zip(HIGH_PASS, parts)))
        return carry

    lax.fori_loop(0, 16, bands, 0)


def rows_kernel(r_ref, v_ref, l_scr):
    rows_body(r_ref, l_scr, v_ref)


def rows_grad_kernel(r_ref, v_ref, bias_ref, l_scr):
    rows_body(r_ref, l_scr, v_ref)
    first = r_ref[0, 0, 70:71, :]
    second = r_ref[0, 0, 71:72, :]
    bias = r_ref[0, 1, 70:71, :]
    for i in range(1, 8):
        first = first + r_ref[i, 0, 70:71, :]
        second = second + r_ref[i, 0, 71:72, :]
        bias = bias + r_ref[i, 1, 70:71, :]

    def put(coef, carry):
        v_ref[coef, 0, 7:8, :] = first
        v_ref[coef, 1, 7:8, :] = second
        return carry

    lax.fori_loop(0, 32, put, 0)
    bias_ref[...] = jnp.broadcast_to(bias, (8, 128))


def weights_kernel(index_ref, w_ref, o_ref):
    slab = index_ref[0]
    high = slab // 16
    mode = slab % 16
    right = mode // 8
    shift = (8 - mode % 8) * 16
    lane = lax.broadcasted_iota(jnp.int32, (256, 128), 1)
    low_y = jnp.where(right == 0, w_ref[high, :, 0:128], w_ref[high, :, 128:256])
    high_y = jnp.where(right == 0, w_ref[high + 2, :, 0:128], w_ref[high + 2, :, 128:256])
    low_y = pltpu.roll(low_y, shift % 128, 1)
    high_y = pltpu.roll(high_y, (shift + 16) % 128, 1)
    o_ref[...] = jnp.where(lane < 16, low_y, jnp.where(lane < 32, high_y, 0.0))


def column_bands(v_ref, q_ref, half):
    value = v_ref[:, half].reshape(256, 128)
    return lax.dot_general(
        value.T, q_ref[...], (((1,), (0,)), ((), ())), precision=HIGHEST,
        preferred_element_type=F32,
    )


def column_changes(d_scr, q_ref, o_ref):
    for half in range(2):
        value = lax.dot_general(
            q_ref[...], d_scr[half * 128 : (half + 1) * 128, :], (((1,), (1,)), ((), ())),
            precision=HIGHEST, preferred_element_type=F32,
        )
        o_ref[:, half] = value.reshape(32, 8, 128)


def mix_kernel(v_ref, q_ref, w_ref, o_ref, y_ref, d_scr):
    for half in range(2):
        y_ref[half * 128 : (half + 1) * 128, :] = column_bands(v_ref, q_ref, half)

    def body(o, carry):
        total = -y_ref[pl.ds(pl.multiple_of(o * 16, 16), 16), :]
        for i in range(16):
            total = total + y_ref[i * 16 : (i + 1) * 16, :] * w_ref[pl.ds(i * 16 + o, 1), :]
        d_scr[pl.ds(pl.multiple_of(o * 16, 16), 16), :] = total
        return carry

    lax.fori_loop(0, 16, body, 0)
    column_changes(d_scr, q_ref, o_ref)


def mix_grad_kernel(v_ref, q_ref, w_ref, y_ref, bias_ref, o_ref, g_ref, p_ref, b_scr, d_scr):
    for half in range(2):
        b_scr[half * 128 : (half + 1) * 128, :] = column_bands(v_ref, q_ref, half)

    def body(i, carry):
        flow = y_ref[pl.ds(pl.multiple_of(i * 16, 16), 16), :]
        total = -b_scr[pl.ds(pl.multiple_of(i * 16, 16), 16), :]
        for o in range(16):
            grad = b_scr[o * 16 : (o + 1) * 16, :]
            total = total + grad * w_ref[pl.ds(i * 16 + o, 1), :]
            g_ref[pl.ds(i * 16 + o, 1), :] = jnp.sum(flow * grad, axis=0, keepdims=True)
        d_scr[pl.ds(pl.multiple_of(i * 16, 16), 16), :] = total
        return carry

    lax.fori_loop(0, 16, body, 0)
    column_changes(d_scr, q_ref, o_ref)
    bias = bias_ref[0:1, :]
    first = v_ref[0, 0, 7:8, :]
    second = v_ref[0, 1, 7:8, :]
    for slab in range(32):
        o_ref[slab, 0, 7:8, :] = bias
        if slab > 0:
            first = first + v_ref[slab, 0, 7:8, :]
            second = second + v_ref[slab, 1, 7:8, :]
    p_ref[...] = jnp.zeros((8, 128), F32)
    p_ref[0:1, :] = first
    p_ref[1:2, :] = second


def spread_body(v_ref, l_scr, s_ref):
    def lift(mode, carry):
        for half in range(2):
            low = [v_ref[(mode + 16 - d) % 16, half] for d in range(4)]
            high = [v_ref[16 + (mode + 16 - d) % 16, half] for d in range(4)]
            for p in range(2):
                pairs = [(LOW_PASS[2 * d + p], low[d]) for d in range(4)]
                pairs += [(HIGH_PASS[2 * d + p], high[d]) for d in range(4)]
                l_scr[2 * mode + p, half] = gather_sum(pairs)
        return carry

    lax.fori_loop(0, 16, lift, 0)

    def send(i, carry):
        for half in range(2):
            s_ref[i, half, 64:72, :] = jnp.zeros((8, 128), F32)
            for a in range(10):
                s_ref[i, half, 7 * a : 7 * a + 8, :] = l_scr[(4 * i + 26 + a) % 32, half]
        return carry

    lax.fori_loop(0, 8, send, 0)


def spread_kernel(v_ref, s_ref, l_scr):
    spread_body(v_ref, l_scr, s_ref)


def spread_grad_kernel(v_ref, s_ref, bias_ref, l_scr):
    spread_body(v_ref, l_scr, s_ref)
    bias = v_ref[0, 0, 7:8, :]
    for slab in range(1, 32):
        bias = bias + v_ref[slab, 0, 7:8, :]
    bias_ref[...] = jnp.broadcast_to(bias, (8, 128))


def side_by_side(values):
    return jnp.concatenate(values, axis=1)


def centre_kernel(
    r_ref, f_ref, c_ref, w_ref, bias_ref, out_ref, g_ref, s_ref,
    d_scr, e_scr, pw_scr, x_scr, p_scr, sum_scr, pt_scr,
):
    unpack_planes(r_ref, d_scr)
    lift_columns(d_scr, e_scr)
    sum_scr[...] = jnp.zeros((16, 128), F32)
    pt_scr[...] = jnp.zeros((16, 16), F32)

    def body(y, carry):
        for part in range(4):
            fields = side_by_side(
                [f_ref[y, x * 16 : (x + 1) * 16, :] for x in range(part * 8, part * 8 + 8)]
            )
            pw_scr[:, part * 1024 : (part + 1) * 1024] = lax.dot_general(
                w_ref[...], fields, (((1,), (0,)), ((), ())), precision=HIGHEST,
                preferred_element_type=F32,
            )
        changes = [e_scr[y, a] for a in range(10)]
        bias = bias_ref[...]
        sums = [None] * 10
        total = sum_scr[...]
        for x in range(32):
            pairs = [(tap(x, a), changes[a]) for a in range(10) if tap(x, a) is not None]
            value = f_ref[y, x * 16 : (x + 1) * 16, :] + gather_sum(pairs)
            value = value + pw_scr[:, x * 128 : (x + 1) * 128] + bias
            square = value * value
            tangent = jnp.tanh(GELU_SCALE * (value + GELU_CUBE * square * value))
            half_up = 0.5 * (1.0 + tangent)
            out_ref[pl.ds(x * 8 + y, 16, stride=256), :] = value * half_up
            slope = half_up + (0.5 * GELU_SCALE) * value * (1.0 - tangent * tangent) * (
                1.0 + (3.0 * GELU_CUBE) * square
            )
            grad = c_ref[pl.ds(x * 8 + y, 16, stride=256), :] * slope
            g_ref[y, x * 16 : (x + 1) * 16, :] = grad
            total = total + grad
            for a in range(10):
                weight = tap(x, a)
                if weight is not None:
                    term = grad * weight
                    sums[a] = term if sums[a] is None else sums[a] + term
        sum_scr[...] = total
        for a in range(10):
            x_scr[a, y] = sums[a]
        point = pt_scr[...]
        for part in range(4):
            span = range(part * 8, part * 8 + 8)
            point = point + lax.dot_general(
                side_by_side([f_ref[y, x * 16 : (x + 1) * 16, :] for x in span]),
                side_by_side([g_ref[y, x * 16 : (x + 1) * 16, :] for x in span]),
                (((1,), (1,)), ((), ())), precision=HIGHEST, preferred_element_type=F32,
            )
        pt_scr[...] = point
        return carry

    lax.fori_loop(0, 8, body, 0)
    partial_columns(x_scr, p_scr)
    pack_planes(p_scr, s_ref)
    lane = lax.broadcasted_iota(jnp.int32, (16, 128), 1)
    row = lax.broadcasted_iota(jnp.int32, (16, 128), 0)
    repeat = (lane % 16 == row).astype(F32)
    wide = lax.dot_general(
        pt_scr[...], repeat, (((1,), (0,)), ((), ())), precision=HIGHEST,
        preferred_element_type=F32,
    )
    wide = jnp.where(lane // 16 == row % 8, wide, 0.0)
    first = jnp.sum(wide[0:8], axis=0, keepdims=True)
    second = jnp.sum(wide[8:16], axis=0, keepdims=True)
    totals = jnp.sum(sum_scr[...], axis=1, keepdims=True)
    bias_row = jnp.sum(jnp.where(lane == row, totals, 0.0), axis=0, keepdims=True)
    for group in range(8):
        s_ref[group, 0, 70:71, :] = first
        s_ref[group, 0, 71:72, :] = second
        s_ref[group, 1, 70:71, :] = bias_row


def finish_kernel(r_ref, g_ref, w_ref, out_ref, d_scr, e_scr, pw_scr):
    unpack_planes(r_ref, d_scr)
    lift_columns(d_scr, e_scr)

    def body(y, carry):
        for part in range(4):
            grads = side_by_side(
                [g_ref[y, x * 16 : (x + 1) * 16, :] for x in range(part * 8, part * 8 + 8)]
            )
            pw_scr[:, part * 1024 : (part + 1) * 1024] = lax.dot_general(
                w_ref[...], grads, (((1,), (0,)), ((), ())), precision=HIGHEST,
                preferred_element_type=F32,
            )
        changes = [e_scr[y, a] for a in range(10)]
        for x in range(32):
            pairs = [(tap(x, a), changes[a]) for a in range(10) if tap(x, a) is not None]
            value = g_ref[y, x * 16 : (x + 1) * 16, :] + gather_sum(pairs)
            value = value + pw_scr[:, x * 128 : (x + 1) * 128]
            out_ref[pl.ds(x * 8 + y, 16, stride=256), :] = value
        return carry

    lax.fori_loop(0, 8, body, 0)


def modes_sum_kernel(g_ref, o_ref):
    total = g_ref[0]
    for i in range(1, 8):
        total = total + g_ref[i]
    lane = lax.broadcasted_iota(jnp.int32, (8, 128), 1)
    packed = jnp.zeros((8, 128), F32)
    for k in range(4):
        rows = total[k * 8 : (k + 1) * 8, :]
        if k > 0:
            rows = pltpu.roll(rows, 32 * k, 1)
        packed = jnp.where(lane // 32 == k, rows, packed)

    def put(slab, carry):
        o_ref[slab] = packed
        return carry

    lax.fori_loop(0, 32, put, 0)


def modes_place_kernel(m_ref, o_ref):
    for high in range(2):
        for right in range(2):
            rows = [m_ref[high * 16 + right * 8 + m] for m in range(8)]
            rows = swap_blocks(rows)
            for k in range(4):
                for up in range(2):
                    for copy in range(8):
                        o_ref[
                            copy, high + 2 * up, k * 8 : (k + 1) * 8,
                            right * 128 : (right + 1) * 128,
                        ] = rows[2 * k + up]


def call(kernel, out_shapes, scratch=(), smem_first=False, n_in=1):
    single = not isinstance(out_shapes, list)
    shapes = [out_shapes] if single else out_shapes
    structs = [jax.ShapeDtypeStruct(s, F32) for s in shapes]
    specs = [pl.BlockSpec(memory_space=pltpu.VMEM)] * n_in
    if smem_first:
        specs[0] = pl.BlockSpec(memory_space=pltpu.SMEM)
    return pl.pallas_call(
        kernel,
        out_shape=structs[0] if single else structs,
        in_specs=specs,
        scratch_shapes=[pltpu.VMEM(s, F32) for s in scratch],
        compiler_params=VMEM,
    )


def local(flow_field, cotangent, mode_weights, point_weights, point_bias):
    swap_x = lambda v: lax.all_to_all(v, "gx", 0, 0, tiled=False)
    swap_y = lambda v: lax.all_to_all(v, "gy", 0, 0, tiled=False)
    packed = (8, 2, 72, 128)
    coefs = (32, 2, 8, 128)
    cells = (8, 512, 128)
    work_x = [(10, 8, 16, 128), (1152, 128)]
    work_lift = [(1152, 128), (8, 10, 16, 128), (16, 4096)]
    rows3 = [(32, 2, 8, 128)]
    table = jnp.asarray(y_table())
    slab = lax.axis_index("gy").astype(jnp.int32).reshape(1)

    weights = call(weights_kernel, (256, 128), smem_first=True, n_in=2)(
        slab, mode_weights.reshape(4, 256, 256)
    )
    sent, fields = call(analyse_kernel, [packed, cells], work_x)(flow_field.reshape(4096, 128))
    got = call(rows_kernel, coefs, rows3)(swap_x(sent))
    back, bands_flow = call(mix_kernel, [coefs, (256, 128)], [(256, 128)], n_in=3)(
        swap_y(got), table, weights
    )
    spread = call(spread_kernel, packed, rows3)(swap_y(back))
    output_field, grads, sent = call(
        centre_kernel, [(4096, 128), cells, packed],
        work_lift + work_x + [(16, 128), (16, 16)], n_in=5,
    )(
        swap_x(spread), fields, cotangent.reshape(4096, 128), point_weights.T,
        jnp.broadcast_to(point_bias[:, None], (16, 128)),
    )
    got, bias_part = call(rows_grad_kernel, [coefs, (8, 128)], rows3)(swap_x(sent))
    back, mode_part, point_total = call(
        mix_grad_kernel, [coefs, (256, 128), (8, 128)], [(256, 128)] * 2, n_in=5
    )(swap_y(got), table, weights, bands_flow, bias_part)
    spread, bias_total = call(spread_grad_kernel, [packed, (8, 128)], rows3)(swap_y(back))
    grad_field = call(finish_kernel, (4096, 128), work_lift, n_in=3)(
        swap_x(spread), grads, point_weights
    )
    part = call(modes_sum_kernel, (32, 8, 128))(swap_x(mode_part.reshape(8, 32, 128)))
    placed = call(modes_place_kernel, (8, 4, 32, 256))(swap_y(part))
    modes = jnp.transpose(swap_x(placed), (1, 0, 2, 3)).reshape(4, 16, 16, 256)

    planes = flow_field.shape[3]
    cell_count = planes * 256 * 256
    return (
        output_field.reshape(flow_field.shape),
        grad_field.reshape(flow_field.shape),
        modes / math.sqrt(planes),
        point_total[0:2].reshape(16, 16) / math.sqrt(cell_count),
        bias_total[0, :16] / math.sqrt(cell_count),
    )


def solution(mesh):
    in_specs = (P(None, "gx", "gy", None), P(None, "gx", "gy", None), P(), P(), P())
    out_specs = (P(None, "gx", "gy", None), P(None, "gx", "gy", None), P(), P(), P())
    return jax.shard_map(local, mesh=mesh, in_specs=in_specs, out_specs=out_specs, check_vma=False)
```

```python
import math

import jax
import jax.numpy as jnp
import ml_dtypes
import numpy as np
from jax import lax
from jax.experimental import pallas as pl
from jax.experimental.pallas import tpu as pltpu
from jax.sharding import PartitionSpec as P

LOW_PASS = [
    0.23037781330885523,
    0.7148465705525415,
    0.6308807679295904,
    -0.02798376941698385,
    -0.18703481171888114,
    0.030841381835986965,
    0.032883011666982945,
    -0.010597401784997278,
]
HIGH_PASS = [(-1) ** position * LOW_PASS[7 - position] for position in range(8)]
GELU_SCALE = 0.7978845608028654
GELU_CUBE = 0.044715


def triple_low():
    taps = np.zeros(50)
    for p, hp in enumerate(LOW_PASS):
        for q, hq in enumerate(LOW_PASS):
            for r, hr in enumerate(LOW_PASS):
                taps[p + 2 * q + 4 * r] += hp * hq * hr
    return [float(t) for t in taps]


TRIPLE = triple_low()
HIGHEST = lax.Precision.HIGHEST
F32 = jnp.float32
BF16 = jnp.bfloat16


def cell_tables():
    table = np.zeros((80, 256))
    for a in range(10):
        for b in range(7):
            for x in range(32):
                for y in range(8):
                    at_x, at_y = x + 48 - 8 * a, y + 48 - 8 * b
                    if 0 <= at_x < 50 and 0 <= at_y < 50:
                        table[a * 7 + b, x * 8 + y] = TRIPLE[at_x] * TRIPLE[at_y]
    table = table.astype(np.float32)
    high = table.astype(ml_dtypes.bfloat16)
    low = (table - high.astype(np.float32)).astype(ml_dtypes.bfloat16)
    down = np.concatenate([high, low])
    pad = np.zeros((256, 16), ml_dtypes.bfloat16)
    up = np.concatenate([high.T, low.T, high.T, pad], 1)
    return down, up


def y_table():
    table = np.zeros((32, 8, 128), np.float32)
    for slab in range(32):
        for b in range(7):
            ky = (slab - 6 + b) % 32
            for mode in range(16):
                at = (ky - 2 * mode) % 32
                if at < 8:
                    table[slab, b, mode] = LOW_PASS[at]
                    table[slab, b, 16 + mode] = HIGH_PASS[at]
    return table.reshape(256, 128)


def gather_sum(pairs):
    total = None
    for weight, value in pairs:
        term = value * weight
        total = term if total is None else total + term
    return total


def swap_blocks(rows):
    lane = lax.broadcasted_iota(jnp.int32, (8, 128), 1)
    rows = list(rows)
    for bit in range(3):
        width = 16 << bit
        upper = (lane & width) != 0
        for lo in range(8):
            if lo & (1 << bit):
                continue
            hi = lo | (1 << bit)
            first, second = rows[lo], rows[hi]
            rows[lo] = jnp.where(upper, pltpu.roll(second, width, 1), first)
            rows[hi] = jnp.where(upper, second, pltpu.roll(first, 128 - width, 1))
    return rows


def split(value):
    high = value.astype(BF16)
    return high, (value - high.astype(F32)).astype(BF16)


def dot(left, right):
    return lax.dot_general(left, right, (((1,), (0,)), ((), ())), preferred_element_type=F32)


def exact_dot(left, right):
    return lax.dot_general(
        left, right, (((1,), (0,)), ((), ())), precision=HIGHEST, preferred_element_type=F32
    )


def side_by_side(values):
    return jnp.concatenate(values, axis=1)


def analyse_pair(field, pair, down_ref, p_scr):
    high, low = split(side_by_side([field[2 * pair], field[2 * pair + 1]]))
    wide = dot(down_ref[...], high)
    total = wide[0:80] + wide[80:160] + dot(down_ref[0:80, :], low)
    p_scr[2 * pair] = total[:, 0:128]
    p_scr[2 * pair + 1] = total[:, 128:256]


def pack_planes(p_scr, s_ref):
    def body(octet, carry):
        at = pl.ds(pl.multiple_of(octet * 8, 8), 8)
        for half in range(2):
            rows = swap_blocks([p_scr[half * 8 + c, at, :] for c in range(8)])
            for group in range(8):
                s_ref[group, half, at, :] = rows[group]
        return carry

    lax.fori_loop(0, 9, body, 0, unroll=True)


def unpack_planes(r_ref, d_scr):
    def body(octet, carry):
        at = pl.ds(pl.multiple_of(octet * 8, 8), 8)
        for half in range(2):
            rows = swap_blocks([r_ref[group, half, at, :] for group in range(8)])
            for c in range(8):
                d_scr[half * 8 + c, at, :] = rows[c]
        return carry

    lax.fori_loop(0, 9, body, 0, unroll=True)
    for c in range(16):
        d_scr[c, 72:80, :] = jnp.zeros((8, 128), F32)


def lift_pair(d_scr, pair, up_ref):
    high, low = split(side_by_side([d_scr[2 * pair], d_scr[2 * pair + 1]]))
    stacked = jnp.concatenate([high, high, low, jnp.zeros((16, 256), BF16)], axis=0)
    return dot(up_ref[...], stacked)


def analyse_kernel(flow_hbm, down_ref, s_ref, f_scr, p_scr, sems):
    copies = [
        pltpu.make_async_copy(flow_hbm.at[pl.ds(4 * k, 4)], f_scr.at[pl.ds(4 * k, 4)], sems.at[k])
        for k in range(4)
    ]
    for copy in copies:
        copy.start()
    for pair in range(8):
        if pair % 2 == 0:
            copies[pair // 2].wait()
        analyse_pair(f_scr, pair, down_ref, p_scr)
    pack_planes(p_scr, s_ref)


def rows_body(r_ref, l_scr, v_ref):
    def collect(q, carry):
        one = (q + 1) % 8
        two = (q + 2) % 8
        for t in range(4):
            for half in range(2):
                total = r_ref[q, half, 7 * (6 + t) : 7 * (6 + t) + 8, :]
                total = total + r_ref[one, half, 7 * (2 + t) : 7 * (2 + t) + 8, :]
                if t >= 2:
                    total = total + r_ref[two, half, 7 * (t - 2) : 7 * (t - 2) + 8, :]
                l_scr[q * 4 + t, half] = total
        return carry

    lax.fori_loop(0, 8, collect, 0)

    def bands(mode, carry):
        for half in range(2):
            parts = [l_scr[(2 * mode + n) % 32, half] for n in range(8)]
            v_ref[mode, half] = gather_sum(list(zip(LOW_PASS, parts)))
            v_ref[mode + 16, half] = gather_sum(list(zip(HIGH_PASS, parts)))
        return carry

    lax.fori_loop(0, 16, bands, 0)


def rows_kernel(r_ref, v_ref, l_scr):
    rows_body(r_ref, l_scr, v_ref)


def rows_grad_kernel(r_ref, v_ref, bias_ref, l_scr):
    rows_body(r_ref, l_scr, v_ref)
    first = r_ref[0, 0, 70:71, :]
    second = r_ref[0, 0, 71:72, :]
    bias = r_ref[0, 1, 70:71, :]
    for i in range(1, 8):
        first = first + r_ref[i, 0, 70:71, :]
        second = second + r_ref[i, 0, 71:72, :]
        bias = bias + r_ref[i, 1, 70:71, :]

    def put(coef, carry):
        v_ref[coef, 0, 7:8, :] = first
        v_ref[coef, 1, 7:8, :] = second
        return carry

    lax.fori_loop(0, 32, put, 0)
    bias_ref[...] = jnp.broadcast_to(bias, (8, 128))


def weights_kernel(index_ref, w_ref, pw_ref, o_ref, forward_ref, back_ref):
    slab = index_ref[0]
    high = slab // 16
    mode = slab % 16
    right = mode // 8
    shift = (8 - mode % 8) * 16
    lane = lax.broadcasted_iota(jnp.int32, (256, 128), 1)
    low_y = jnp.where(right == 0, w_ref[high, :, 0:128], w_ref[high, :, 128:256])
    high_y = jnp.where(right == 0, w_ref[high + 2, :, 0:128], w_ref[high + 2, :, 128:256])
    low_y = pltpu.roll(low_y, shift % 128, 1)
    high_y = pltpu.roll(high_y, (shift + 16) % 128, 1)
    o_ref[...] = jnp.where(lane < 16, low_y, jnp.where(lane < 32, high_y, 0.0))
    same_y = iota(128, 128, 0) % 8 == iota(128, 128, 1) % 8
    rows = (iota(128, 16, 0) // 8 == iota(128, 16, 1)).astype(F32)
    cols = (iota(16, 128, 1) // 8 == iota(16, 128, 0)).astype(F32)
    point = pw_ref[...]
    for ref, matrix in ((forward_ref, point.T), (back_ref, point)):
        wide = jnp.where(same_y, exact_dot(exact_dot(rows, matrix), cols), 0.0)
        upper, lower = split(wide)
        ref[...] = side_by_side([upper, lower, upper])


def iota(rows, cols, axis):
    return lax.broadcasted_iota(jnp.int32, (rows, cols), axis)


def column_bands(v_ref, q_ref, half):
    value = v_ref[:, half].reshape(256, 128)
    return lax.dot_general(
        value.T, q_ref[...], (((1,), (0,)), ((), ())), precision=HIGHEST,
        preferred_element_type=F32,
    )


def column_changes(d_scr, q_ref, o_ref):
    for half in range(2):
        value = lax.dot_general(
            q_ref[...], d_scr[half * 128 : (half + 1) * 128, :], (((1,), (1,)), ((), ())),
            precision=HIGHEST, preferred_element_type=F32,
        )
        o_ref[:, half] = value.reshape(32, 8, 128)


def mix_kernel(v_ref, q_ref, w_ref, o_ref, y_ref, d_scr):
    for half in range(2):
        y_ref[half * 128 : (half + 1) * 128, :] = column_bands(v_ref, q_ref, half)

    def body(o, carry):
        total = -y_ref[pl.ds(pl.multiple_of(o * 16, 16), 16), :]
        for i in range(16):
            total = total + y_ref[i * 16 : (i + 1) * 16, :] * w_ref[pl.ds(i * 16 + o, 1), :]
        d_scr[pl.ds(pl.multiple_of(o * 16, 16), 16), :] = total
        return carry

    lax.fori_loop(0, 16, body, 0)
    column_changes(d_scr, q_ref, o_ref)


def mix_grad_kernel(v_ref, q_ref, w_ref, y_ref, bias_ref, o_ref, g_ref, p_ref, b_scr, d_scr):
    for half in range(2):
        b_scr[half * 128 : (half + 1) * 128, :] = column_bands(v_ref, q_ref, half)

    def body(i, carry):
        flow = y_ref[pl.ds(pl.multiple_of(i * 16, 16), 16), :]
        total = -b_scr[pl.ds(pl.multiple_of(i * 16, 16), 16), :]
        for o in range(16):
            grad = b_scr[o * 16 : (o + 1) * 16, :]
            total = total + grad * w_ref[pl.ds(i * 16 + o, 1), :]
            g_ref[pl.ds(i * 16 + o, 1), :] = jnp.sum(flow * grad, axis=0, keepdims=True)
        d_scr[pl.ds(pl.multiple_of(i * 16, 16), 16), :] = total
        return carry

    lax.fori_loop(0, 16, body, 0)
    column_changes(d_scr, q_ref, o_ref)
    bias = bias_ref[0:1, :]
    first = v_ref[0, 0, 7:8, :]
    second = v_ref[0, 1, 7:8, :]
    for slab in range(32):
        o_ref[slab, 0, 7:8, :] = bias
        if slab > 0:
            first = first + v_ref[slab, 0, 7:8, :]
            second = second + v_ref[slab, 1, 7:8, :]
    p_ref[...] = jnp.zeros((8, 128), F32)
    p_ref[0:1, :] = first
    p_ref[1:2, :] = second


def spread_body(v_ref, l_scr, s_ref):
    def lift(mode, carry):
        for half in range(2):
            low = [v_ref[(mode + 16 - d) % 16, half] for d in range(4)]
            high = [v_ref[16 + (mode + 16 - d) % 16, half] for d in range(4)]
            for p in range(2):
                pairs = [(LOW_PASS[2 * d + p], low[d]) for d in range(4)]
                pairs += [(HIGH_PASS[2 * d + p], high[d]) for d in range(4)]
                l_scr[2 * mode + p, half] = gather_sum(pairs)
        return carry

    lax.fori_loop(0, 16, lift, 0)

    def send(i, carry):
        for half in range(2):
            s_ref[i, half, 64:72, :] = jnp.zeros((8, 128), F32)
            for a in range(10):
                s_ref[i, half, 7 * a : 7 * a + 8, :] = l_scr[(4 * i + 26 + a) % 32, half]
        return carry

    lax.fori_loop(0, 8, send, 0)


def spread_kernel(v_ref, s_ref, l_scr):
    spread_body(v_ref, l_scr, s_ref)


def spread_grad_kernel(v_ref, s_ref, bias_ref, l_scr):
    spread_body(v_ref, l_scr, s_ref)
    bias = v_ref[0, 0, 7:8, :]
    for slab in range(1, 32):
        bias = bias + v_ref[slab, 0, 7:8, :]
    bias_ref[...] = jnp.broadcast_to(bias, (8, 128))


def point_mix(w_ref, first, second):
    high, low = split(side_by_side([first, second]))
    return dot(w_ref[...], jnp.concatenate([high, high, low], axis=0)), high, low


def centre_kernel(
    r_ref, flow_hbm, cot_hbm, w_ref, bias_ref, down_ref, up_ref, out_hbm, g_hbm, s_ref,
    f_scr, c_scr, v_scr, g_scr, d_scr, p_scr, sum_scr, pt_scr, sems,
):
    load_flow = pltpu.make_async_copy(flow_hbm, f_scr, sems.at[0])
    load_cot = pltpu.make_async_copy(cot_hbm, c_scr, sems.at[1])
    load_flow.start()
    load_cot.start()
    unpack_planes(r_ref, d_scr)
    sum_scr[...] = jnp.zeros((128, 128), F32)
    pt_scr[...] = jnp.zeros((128, 128), F32)
    load_flow.wait()
    for pair in range(8):
        change = lift_pair(d_scr, pair, up_ref)
        for k in range(2):
            c = 2 * pair + k
            v_scr[c] = f_scr[c] + (change[:, 128 * k : 128 * k + 128] + bias_ref[c])
    load_cot.wait()
    stores = []
    for chunk in range(4):

        def body(step, carry):
            start = pl.multiple_of((chunk * 4 + step) * 16, 16)
            spans = [pl.ds(start, 8), pl.ds(pl.multiple_of(start + 8, 8), 8)]
            fields = [f_scr[:, span, :].reshape(128, 128) for span in spans]
            mixed, f_high, f_low = point_mix(w_ref, fields[0], fields[1])
            grads = []
            for k in range(2):
                value = v_scr[:, spans[k], :].reshape(128, 128) + mixed[:, 128 * k : 128 * k + 128]
                square = value * value
                tangent = jnp.tanh(value * (GELU_SCALE + (GELU_SCALE * GELU_CUBE) * square))
                half_up = 0.5 + 0.5 * tangent
                v_scr[:, spans[k], :] = (value * half_up).reshape(16, 8, 128)
                bend = value * ((0.5 * GELU_SCALE) + (1.5 * GELU_SCALE * GELU_CUBE) * square)
                slope = half_up + bend * (1.0 - tangent * tangent)
                grad = c_scr[:, spans[k], :].reshape(128, 128) * slope
                g_scr[:, spans[k], :] = grad.reshape(16, 8, 128)
                grads.append(grad)
            sum_scr[...] += grads[0] + grads[1]
            g_high, g_low = split(side_by_side(grads))
            pt_scr[...] += lax.dot_general(
                side_by_side([f_high, f_low, f_high]), side_by_side([g_high, g_high, g_low]),
                (((1,), (1,)), ((), ())), preferred_element_type=F32,
            )
            return carry

        lax.fori_loop(0, 4, body, 0, unroll=True)
        part = pl.ds(chunk * 64, 64)
        for k, (scr, hbm) in enumerate(((v_scr, out_hbm), (g_scr, g_hbm))):
            store = pltpu.make_async_copy(
                scr.at[:, part], hbm.at[:, part], sems.at[2 + 2 * chunk + k]
            )
            store.start()
            stores.append(store)
    for pair in range(8):
        analyse_pair(g_scr, pair, down_ref, p_scr)
    pack_planes(p_scr, s_ref)
    same_y = iota(128, 128, 0) % 8 == iota(128, 128, 1) % 8
    gather = (iota(16, 128, 1) // 8 == iota(16, 128, 0)).astype(F32)
    fold = (iota(128, 128, 0) // 8 == iota(128, 128, 1) % 16).astype(F32)
    wide = exact_dot(exact_dot(gather, jnp.where(same_y, pt_scr[...], 0.0)), fold)
    lane, row = iota(16, 128, 1), iota(16, 128, 0)
    wide = jnp.where(lane // 16 == row % 8, wide, 0.0)
    first = jnp.sum(wide[0:8], axis=0, keepdims=True)
    second = jnp.sum(wide[8:16], axis=0, keepdims=True)
    totals = jnp.sum(exact_dot(gather, sum_scr[...]), axis=1, keepdims=True)
    bias_row = jnp.sum(jnp.where(lane == row, totals, 0.0), axis=0, keepdims=True)
    for group in range(8):
        s_ref[group, 0, 70:71, :] = first
        s_ref[group, 0, 71:72, :] = second
        s_ref[group, 1, 70:71, :] = bias_row
    for store in stores:
        store.wait()


def finish_kernel(r_ref, g_hbm, w_ref, up_ref, out_hbm, g_scr, v_scr, d_scr, sems):
    load = pltpu.make_async_copy(g_hbm, g_scr, sems.at[0])
    load.start()
    unpack_planes(r_ref, d_scr)
    load.wait()
    for pair in range(8):
        change = lift_pair(d_scr, pair, up_ref)
        for k in range(2):
            v_scr[2 * pair + k] = g_scr[2 * pair + k] + change[:, 128 * k : 128 * k + 128]
    stores = []
    for chunk in range(4):

        def body(step, carry):
            start = pl.multiple_of((chunk * 4 + step) * 16, 16)
            spans = [pl.ds(start, 8), pl.ds(pl.multiple_of(start + 8, 8), 8)]
            fields = [g_scr[:, span, :].reshape(128, 128) for span in spans]
            mixed = point_mix(w_ref, fields[0], fields[1])[0]
            for k in range(2):
                value = v_scr[:, spans[k], :].reshape(128, 128) + mixed[:, 128 * k : 128 * k + 128]
                v_scr[:, spans[k], :] = value.reshape(16, 8, 128)
            return carry

        lax.fori_loop(0, 4, body, 0, unroll=True)
        part = pl.ds(chunk * 64, 64)
        store = pltpu.make_async_copy(v_scr.at[:, part], out_hbm.at[:, part], sems.at[1 + chunk])
        store.start()
        stores.append(store)
    for store in stores:
        store.wait()


def modes_sum_kernel(g_ref, o_ref):
    total = g_ref[0]
    for i in range(1, 8):
        total = total + g_ref[i]
    lane = lax.broadcasted_iota(jnp.int32, (8, 128), 1)
    packed = jnp.zeros((8, 128), F32)
    for k in range(4):
        rows = total[k * 8 : (k + 1) * 8, :]
        if k > 0:
            rows = pltpu.roll(rows, 32 * k, 1)
        packed = jnp.where(lane // 32 == k, rows, packed)

    def put(slab, carry):
        o_ref[slab] = packed
        return carry

    lax.fori_loop(0, 32, put, 0)


def modes_place_kernel(m_ref, o_ref):
    for high in range(2):
        for right in range(2):
            rows = [m_ref[high * 16 + right * 8 + m] for m in range(8)]
            rows = swap_blocks(rows)
            for k in range(4):
                for up in range(2):
                    for copy in range(8):
                        o_ref[
                            copy, high + 2 * up, k * 8 : (k + 1) * 8,
                            right * 128 : (right + 1) * 128,
                        ] = rows[2 * k + up]


def call(kernel, ins, outs, scratch=(), sems=0, mib=8):
    spaces = {"v": pltpu.VMEM, "s": pltpu.SMEM, "a": pltpu.HBM}
    structs = [jax.ShapeDtypeStruct(o[0], o[2] if len(o) > 2 else F32) for o in outs]
    scratches = [pltpu.VMEM(shape, F32) for shape in scratch]
    if sems:
        scratches.append(pltpu.SemaphoreType.DMA((sems,)))
    return pl.pallas_call(
        kernel,
        out_shape=structs,
        in_specs=[pl.BlockSpec(memory_space=spaces[k]) for k in ins],
        out_specs=[pl.BlockSpec(memory_space=spaces[o[1]]) for o in outs],
        scratch_shapes=scratches,
        compiler_params=pltpu.CompilerParams(vmem_limit_bytes=mib * 1024 * 1024),
    )


def local(flow_field, cotangent, mode_weights, point_weights, point_bias):
    swap_x = lambda v: lax.all_to_all(v, "gx", 0, 0, tiled=False)
    swap_y = lambda v: lax.all_to_all(v, "gy", 0, 0, tiled=False)
    packed = ((8, 2, 72, 128), "v")
    coefs = ((32, 2, 8, 128), "v")
    square = ((256, 128), "v")
    row = ((8, 128), "v")
    cells = (16, 256, 128)
    parts = (16, 80, 128)
    rows3 = [(32, 2, 8, 128)]
    table = jnp.asarray(y_table())
    down, up = (jnp.asarray(t) for t in cell_tables())
    slab = lax.axis_index("gy").astype(jnp.int32).reshape(1)
    flow_cells = flow_field.reshape(cells)
    kron = ((128, 384), "v", BF16)

    weights, mix_forward, mix_back = call(weights_kernel, "svv", [square, kron, kron])(
        slab, mode_weights.reshape(4, 256, 256), point_weights
    )
    (sent,) = call(analyse_kernel, "av", [packed], [cells, parts], 4, 58)(flow_cells, down)
    (got,) = call(rows_kernel, "v", [coefs], rows3)(swap_x(sent))
    back, bands_flow = call(mix_kernel, "vvv", [coefs, square], [(256, 128)])(
        swap_y(got), table, weights
    )
    (spread,) = call(spread_kernel, "v", [packed], rows3)(swap_y(back))
    output_field, grads, sent = call(
        centre_kernel, "vaavsvv", [(cells, "a"), (cells, "a"), packed],
        [cells] * 4 + [parts] * 2 + [(128, 128)] * 2, 10, 58,
    )(
        swap_x(spread), flow_cells, cotangent.reshape(cells), mix_forward, point_bias, down, up
    )
    got, bias_part = call(rows_grad_kernel, "v", [coefs, row], rows3)(swap_x(sent))
    back, mode_part, point_total = call(
        mix_grad_kernel, "vvvvv", [coefs, square, row], [(256, 128)] * 2
    )(swap_y(got), table, weights, bands_flow, bias_part)
    spread, bias_total = call(spread_grad_kernel, "v", [packed, row], rows3)(swap_y(back))
    (grad_field,) = call(
        finish_kernel, "vavv", [(cells, "a")], [cells] * 2 + [parts], 5, 58
    )(swap_x(spread), grads, mix_back, up)
    (part,) = call(modes_sum_kernel, "v", [((32, 8, 128), "v")])(
        swap_x(mode_part.reshape(8, 32, 128))
    )
    (placed,) = call(modes_place_kernel, "v", [((8, 4, 32, 256), "v")])(swap_y(part))
    modes = jnp.transpose(swap_x(placed), (1, 0, 2, 3)).reshape(4, 16, 16, 256)

    planes = flow_field.shape[3]
    cell_count = planes * 256 * 256
    return (
        output_field.reshape(flow_field.shape),
        grad_field.reshape(flow_field.shape),
        modes / math.sqrt(planes),
        point_total[0:2].reshape(16, 16) / math.sqrt(cell_count),
        bias_total[0, :16] / math.sqrt(cell_count),
    )


def solution(mesh):
    in_specs = (P(None, "gx", "gy", None), P(None, "gx", "gy", None), P(), P(), P())
    out_specs = (P(None, "gx", "gy", None), P(None, "gx", "gy", None), P(), P(), P())
    return jax.shard_map(local, mesh=mesh, in_specs=in_specs, out_specs=out_specs, check_vma=False)
```

```python
import math

import jax
import jax.numpy as jnp
import ml_dtypes
import numpy as np
from jax import lax
from jax.experimental import pallas as pl
from jax.experimental.pallas import tpu as pltpu
from jax.sharding import PartitionSpec as P

LOW_PASS = [
    0.23037781330885523,
    0.7148465705525415,
    0.6308807679295904,
    -0.02798376941698385,
    -0.18703481171888114,
    0.030841381835986965,
    0.032883011666982945,
    -0.010597401784997278,
]
HIGH_PASS = [(-1) ** position * LOW_PASS[7 - position] for position in range(8)]
GELU_SCALE = 0.7978845608028654
GELU_CUBE = 0.044715


def triple_low():
    taps = np.zeros(50)
    for p, hp in enumerate(LOW_PASS):
        for q, hq in enumerate(LOW_PASS):
            for r, hr in enumerate(LOW_PASS):
                taps[p + 2 * q + 4 * r] += hp * hq * hr
    return [float(t) for t in taps]


TRIPLE = triple_low()
HIGHEST = lax.Precision.HIGHEST
F32 = jnp.float32
BF16 = jnp.bfloat16


def cell_tables():
    table = np.zeros((80, 256))
    for a in range(10):
        for b in range(7):
            for x in range(32):
                for y in range(8):
                    at_x, at_y = x + 48 - 8 * a, y + 48 - 8 * b
                    if 0 <= at_x < 50 and 0 <= at_y < 50:
                        table[a * 7 + b, x * 8 + y] = TRIPLE[at_x] * TRIPLE[at_y]
    table = table.astype(np.float32)
    high = table.astype(ml_dtypes.bfloat16)
    low = (table - high.astype(np.float32)).astype(ml_dtypes.bfloat16)
    down = np.concatenate([high, low])
    pad = np.zeros((256, 16), ml_dtypes.bfloat16)
    up = np.concatenate([high.T, low.T, high.T, pad], 1)
    return down, up


def y_table():
    table = np.zeros((32, 8, 128), np.float32)
    for slab in range(32):
        for b in range(7):
            ky = (slab - 6 + b) % 32
            for mode in range(16):
                at = (ky - 2 * mode) % 32
                if at < 8:
                    table[slab, b, mode] = LOW_PASS[at]
                    table[slab, b, 16 + mode] = HIGH_PASS[at]
    return table.reshape(256, 128)


def gather_sum(pairs):
    total = None
    for weight, value in pairs:
        term = value * weight
        total = term if total is None else total + term
    return total


def swap_blocks(rows):
    lane = lax.broadcasted_iota(jnp.int32, (8, 128), 1)
    rows = list(rows)
    for bit in range(3):
        width = 16 << bit
        upper = (lane & width) != 0
        for lo in range(8):
            if lo & (1 << bit):
                continue
            hi = lo | (1 << bit)
            first, second = rows[lo], rows[hi]
            rows[lo] = jnp.where(upper, pltpu.roll(second, width, 1), first)
            rows[hi] = jnp.where(upper, second, pltpu.roll(first, 128 - width, 1))
    return rows


def split(value):
    high = value.astype(BF16)
    return high, (value - high.astype(F32)).astype(BF16)


def dot(left, right):
    return lax.dot_general(left, right, (((1,), (0,)), ((), ())), preferred_element_type=F32)


def exact_dot(left, right):
    return lax.dot_general(
        left, right, (((1,), (0,)), ((), ())), precision=HIGHEST, preferred_element_type=F32
    )


def side_by_side(values):
    return jnp.concatenate(values, axis=1)


def analyse_pair(field, pair, down_ref, p_scr):
    high, low = split(side_by_side([field[2 * pair], field[2 * pair + 1]]))
    wide = dot(down_ref[...], high)
    total = wide[0:80] + wide[80:160] + dot(down_ref[0:80, :], low)
    p_scr[2 * pair] = total[:, 0:128]
    p_scr[2 * pair + 1] = total[:, 128:256]


def pack_planes(p_scr, s_ref):
    def body(octet, carry):
        at = pl.ds(pl.multiple_of(octet * 8, 8), 8)
        for half in range(2):
            rows = swap_blocks([p_scr[half * 8 + c, at, :] for c in range(8)])
            for group in range(8):
                s_ref[group, half, at, :] = rows[group]
        return carry

    lax.fori_loop(0, 9, body, 0, unroll=True)


def unpack_planes(r_ref, d_scr):
    def body(octet, carry):
        at = pl.ds(pl.multiple_of(octet * 8, 8), 8)
        for half in range(2):
            rows = swap_blocks([r_ref[group, half, at, :] for group in range(8)])
            for c in range(8):
                d_scr[half * 8 + c, at, :] = rows[c]
        return carry

    lax.fori_loop(0, 9, body, 0, unroll=True)
    for c in range(16):
        d_scr[c, 72:80, :] = jnp.zeros((8, 128), F32)


def lift_pair(d_scr, pair, up_ref):
    high, low = split(side_by_side([d_scr[2 * pair], d_scr[2 * pair + 1]]))
    stacked = jnp.concatenate([high, high, low, jnp.zeros((16, 256), BF16)], axis=0)
    return dot(up_ref[...], stacked)


def analyse_kernel(flow_hbm, down_ref, s_ref, f_scr, p_scr, sems):
    copies = [
        pltpu.make_async_copy(flow_hbm.at[pl.ds(4 * k, 4)], f_scr.at[pl.ds(4 * k, 4)], sems.at[k])
        for k in range(4)
    ]
    for copy in copies:
        copy.start()
    for pair in range(8):
        if pair % 2 == 0:
            copies[pair // 2].wait()
        analyse_pair(f_scr, pair, down_ref, p_scr)
    pack_planes(p_scr, s_ref)


def rows_body(r_ref, l_scr, v_ref):
    def collect(q, carry):
        one = (q + 1) % 8
        two = (q + 2) % 8
        for t in range(4):
            for half in range(2):
                total = r_ref[q, half, 7 * (6 + t) : 7 * (6 + t) + 8, :]
                total = total + r_ref[one, half, 7 * (2 + t) : 7 * (2 + t) + 8, :]
                if t >= 2:
                    total = total + r_ref[two, half, 7 * (t - 2) : 7 * (t - 2) + 8, :]
                l_scr[q * 4 + t, half] = total
        return carry

    lax.fori_loop(0, 8, collect, 0)

    def bands(mode, carry):
        for half in range(2):
            parts = [l_scr[(2 * mode + n) % 32, half] for n in range(8)]
            v_ref[mode, half] = gather_sum(list(zip(LOW_PASS, parts)))
            v_ref[mode + 16, half] = gather_sum(list(zip(HIGH_PASS, parts)))
        return carry

    lax.fori_loop(0, 16, bands, 0)


def rows_kernel(r_ref, v_ref, l_scr):
    rows_body(r_ref, l_scr, v_ref)


def rows_grad_kernel(r_ref, v_ref, bias_ref, l_scr):
    rows_body(r_ref, l_scr, v_ref)
    first = r_ref[0, 0, 70:71, :]
    second = r_ref[0, 0, 71:72, :]
    bias = r_ref[0, 1, 70:71, :]
    for i in range(1, 8):
        first = first + r_ref[i, 0, 70:71, :]
        second = second + r_ref[i, 0, 71:72, :]
        bias = bias + r_ref[i, 1, 70:71, :]

    def put(coef, carry):
        v_ref[coef, 0, 7:8, :] = first
        v_ref[coef, 1, 7:8, :] = second
        return carry

    lax.fori_loop(0, 32, put, 0)
    bias_ref[...] = jnp.broadcast_to(bias, (8, 128))


def weights_kernel(index_ref, w_ref, pw_ref, o_ref, forward_ref, back_ref):
    slab = index_ref[0]
    high = slab // 16
    mode = slab % 16
    right = mode // 8
    shift = (8 - mode % 8) * 16
    lane = lax.broadcasted_iota(jnp.int32, (256, 128), 1)
    low_y = jnp.where(right == 0, w_ref[high, :, 0:128], w_ref[high, :, 128:256])
    high_y = jnp.where(right == 0, w_ref[high + 2, :, 0:128], w_ref[high + 2, :, 128:256])
    low_y = pltpu.roll(low_y, shift % 128, 1)
    high_y = pltpu.roll(high_y, (shift + 16) % 128, 1)
    o_ref[...] = jnp.where(lane < 16, low_y, jnp.where(lane < 32, high_y, 0.0))
    same_y = iota(128, 128, 0) % 8 == iota(128, 128, 1) % 8
    rows = (iota(128, 16, 0) // 8 == iota(128, 16, 1)).astype(F32)
    cols = (iota(16, 128, 1) // 8 == iota(16, 128, 0)).astype(F32)
    point = pw_ref[...]
    for ref, matrix in ((forward_ref, point.T), (back_ref, point)):
        wide = jnp.where(same_y, exact_dot(exact_dot(rows, matrix), cols), 0.0)
        upper, lower = split(wide)
        ref[...] = side_by_side([upper, lower, upper])


def iota(rows, cols, axis):
    return lax.broadcasted_iota(jnp.int32, (rows, cols), axis)


def column_bands(v_ref, q_ref, half):
    value = v_ref[:, half].reshape(256, 128)
    return lax.dot_general(
        value.T, q_ref[...], (((1,), (0,)), ((), ())), precision=HIGHEST,
        preferred_element_type=F32,
    )


def column_changes(d_scr, q_ref, o_ref):
    for half in range(2):
        value = lax.dot_general(
            q_ref[...], d_scr[half * 128 : (half + 1) * 128, :], (((1,), (1,)), ((), ())),
            precision=HIGHEST, preferred_element_type=F32,
        )
        o_ref[:, half] = value.reshape(32, 8, 128)


def mix_kernel(v_ref, q_ref, w_ref, o_ref, y_ref, d_scr):
    for half in range(2):
        y_ref[half * 128 : (half + 1) * 128, :] = column_bands(v_ref, q_ref, half)

    def body(o, carry):
        total = -y_ref[pl.ds(pl.multiple_of(o * 16, 16), 16), :]
        for i in range(16):
            total = total + y_ref[i * 16 : (i + 1) * 16, :] * w_ref[pl.ds(i * 16 + o, 1), :]
        d_scr[pl.ds(pl.multiple_of(o * 16, 16), 16), :] = total
        return carry

    lax.fori_loop(0, 16, body, 0)
    column_changes(d_scr, q_ref, o_ref)


def grad_bands_kernel(v_ref, q_ref, y_ref, b_ref, g_ref, p_ref, g_scr):
    for half in range(2):
        b_ref[half * 128 : (half + 1) * 128, :] = column_bands(v_ref, q_ref, half)

    def body(i, carry):
        flow = y_ref[pl.ds(pl.multiple_of(i * 16, 16), 16), :]
        for o in range(16):
            grad = b_ref[o * 16 : (o + 1) * 16, :]
            g_scr[pl.ds(i * 16 + o, 1), :] = jnp.sum(flow * grad, axis=0, keepdims=True)
        return carry

    lax.fori_loop(0, 16, body, 0)
    lane = lax.broadcasted_iota(jnp.int32, (8, 128), 1)
    for group in range(8):
        packed = g_scr[group * 32 : group * 32 + 8, :]
        for k in range(1, 4):
            rows = g_scr[group * 32 + k * 8 : group * 32 + k * 8 + 8, :]
            packed = jnp.where(lane // 32 == k, pltpu.roll(rows, 32 * k, 1), packed)
        g_ref[group] = packed
    first = v_ref[0, 0, 7:8, :]
    second = v_ref[0, 1, 7:8, :]
    for slab in range(1, 32):
        first = first + v_ref[slab, 0, 7:8, :]
        second = second + v_ref[slab, 1, 7:8, :]
    p_ref[...] = jnp.zeros((8, 128), F32)
    p_ref[0:1, :] = first
    p_ref[1:2, :] = second


def mix_grad_kernel(b_ref, q_ref, w_ref, bias_ref, o_ref, d_scr):
    def body(i, carry):
        total = -b_ref[pl.ds(pl.multiple_of(i * 16, 16), 16), :]
        for o in range(16):
            total = total + b_ref[o * 16 : (o + 1) * 16, :] * w_ref[pl.ds(i * 16 + o, 1), :]
        d_scr[pl.ds(pl.multiple_of(i * 16, 16), 16), :] = total
        return carry

    lax.fori_loop(0, 16, body, 0)
    column_changes(d_scr, q_ref, o_ref)
    for slab in range(32):
        o_ref[slab, 0, 7:8, :] = bias_ref[0:1, :]


def join_kernel(v_ref, g_ref, o_ref):
    total = g_ref[0]
    for i in range(1, 8):
        total = total + g_ref[i]
    total = total * (1.0 / math.sqrt(128.0))
    for slab in range(32):
        o_ref[slab, 0:2] = v_ref[slab]
        o_ref[slab, 2] = total


def spread_body(v_ref, l_scr, s_ref):
    def lift(mode, carry):
        for half in range(2):
            low = [v_ref[(mode + 16 - d) % 16, half] for d in range(4)]
            high = [v_ref[16 + (mode + 16 - d) % 16, half] for d in range(4)]
            for p in range(2):
                pairs = [(LOW_PASS[2 * d + p], low[d]) for d in range(4)]
                pairs += [(HIGH_PASS[2 * d + p], high[d]) for d in range(4)]
                l_scr[2 * mode + p, half] = gather_sum(pairs)
        return carry

    lax.fori_loop(0, 16, lift, 0)

    def send(i, carry):
        for half in range(2):
            s_ref[i, half, 64:72, :] = jnp.zeros((8, 128), F32)
            for a in range(10):
                s_ref[i, half, 7 * a : 7 * a + 8, :] = l_scr[(4 * i + 26 + a) % 32, half]
        return carry

    lax.fori_loop(0, 8, send, 0)


def spread_kernel(v_ref, s_ref, l_scr):
    spread_body(v_ref, l_scr, s_ref)


def spread_grad_kernel(v_ref, s_ref, bias_ref, l_scr):
    spread_body(v_ref, l_scr, s_ref)
    bias = v_ref[0, 0, 7:8, :]
    for slab in range(1, 32):
        bias = bias + v_ref[slab, 0, 7:8, :]
    bias_ref[...] = jnp.broadcast_to(bias, (8, 128))


def point_mix(w_ref, first, second):
    high, low = split(side_by_side([first, second]))
    return dot(w_ref[...], jnp.concatenate([high, high, low], axis=0)), high, low


def centre_kernel(
    r_ref, flow_hbm, cot_hbm, w_ref, bias_ref, down_ref, up_ref, out_hbm, g_hbm, s_ref,
    f_scr, c_scr, v_scr, g_scr, d_scr, p_scr, sum_scr, pt_scr, sems,
):
    load_flow = pltpu.make_async_copy(flow_hbm, f_scr, sems.at[0])
    load_cot = pltpu.make_async_copy(cot_hbm, c_scr, sems.at[1])
    load_flow.start()
    load_cot.start()
    unpack_planes(r_ref, d_scr)
    sum_scr[...] = jnp.zeros((128, 128), F32)
    pt_scr[...] = jnp.zeros((128, 128), F32)
    load_flow.wait()
    for pair in range(8):
        change = lift_pair(d_scr, pair, up_ref)
        for k in range(2):
            c = 2 * pair + k
            v_scr[c] = f_scr[c] + (change[:, 128 * k : 128 * k + 128] + bias_ref[c])
    load_cot.wait()
    stores = []
    for chunk in range(4):

        def body(step, carry):
            start = pl.multiple_of((chunk * 4 + step) * 16, 16)
            spans = [pl.ds(start, 8), pl.ds(pl.multiple_of(start + 8, 8), 8)]
            fields = [f_scr[:, span, :].reshape(128, 128) for span in spans]
            mixed, f_high, f_low = point_mix(w_ref, fields[0], fields[1])
            grads = []
            for k in range(2):
                value = v_scr[:, spans[k], :].reshape(128, 128) + mixed[:, 128 * k : 128 * k + 128]
                square = value * value
                tangent = jnp.tanh(value * (GELU_SCALE + (GELU_SCALE * GELU_CUBE) * square))
                half_up = 0.5 + 0.5 * tangent
                v_scr[:, spans[k], :] = (value * half_up).reshape(16, 8, 128)
                bend = value * ((0.5 * GELU_SCALE) + (1.5 * GELU_SCALE * GELU_CUBE) * square)
                slope = half_up + bend * (1.0 - tangent * tangent)
                grad = c_scr[:, spans[k], :].reshape(128, 128) * slope
                g_scr[:, spans[k], :] = grad.reshape(16, 8, 128)
                grads.append(grad)
            sum_scr[...] += grads[0] + grads[1]
            g_high, g_low = split(side_by_side(grads))
            pt_scr[...] += lax.dot_general(
                side_by_side([f_high, f_low, f_high]), side_by_side([g_high, g_high, g_low]),
                (((1,), (1,)), ((), ())), preferred_element_type=F32,
            )
            return carry

        lax.fori_loop(0, 4, body, 0, unroll=True)
        part = pl.ds(chunk * 64, 64)
        for k, (scr, hbm) in enumerate(((v_scr, out_hbm), (g_scr, g_hbm))):
            store = pltpu.make_async_copy(
                scr.at[:, part], hbm.at[:, part], sems.at[2 + 2 * chunk + k]
            )
            store.start()
            stores.append(store)
    for pair in range(8):
        analyse_pair(g_scr, pair, down_ref, p_scr)
    pack_planes(p_scr, s_ref)
    same_y = iota(128, 128, 0) % 8 == iota(128, 128, 1) % 8
    gather = (iota(16, 128, 1) // 8 == iota(16, 128, 0)).astype(F32)
    fold = (iota(128, 128, 0) // 8 == iota(128, 128, 1) % 16).astype(F32)
    wide = exact_dot(exact_dot(gather, jnp.where(same_y, pt_scr[...], 0.0)), fold)
    lane, row = iota(16, 128, 1), iota(16, 128, 0)
    wide = jnp.where(lane // 16 == row % 8, wide, 0.0)
    first = jnp.sum(wide[0:8], axis=0, keepdims=True)
    second = jnp.sum(wide[8:16], axis=0, keepdims=True)
    totals = jnp.sum(exact_dot(gather, sum_scr[...]), axis=1, keepdims=True)
    bias_row = jnp.sum(jnp.where(lane == row, totals, 0.0), axis=0, keepdims=True)
    for group in range(8):
        s_ref[group, 0, 70:71, :] = first
        s_ref[group, 0, 71:72, :] = second
        s_ref[group, 1, 70:71, :] = bias_row
    for store in stores:
        store.wait()


def finish_kernel(r_ref, g_hbm, w_ref, up_ref, out_hbm, g_scr, v_scr, d_scr, sems):
    load = pltpu.make_async_copy(g_hbm, g_scr, sems.at[0])
    load.start()
    unpack_planes(r_ref, d_scr)
    load.wait()
    for pair in range(8):
        change = lift_pair(d_scr, pair, up_ref)
        for k in range(2):
            v_scr[2 * pair + k] = g_scr[2 * pair + k] + change[:, 128 * k : 128 * k + 128]
    stores = []
    for chunk in range(4):

        def body(step, carry):
            start = pl.multiple_of((chunk * 4 + step) * 16, 16)
            spans = [pl.ds(start, 8), pl.ds(pl.multiple_of(start + 8, 8), 8)]
            fields = [g_scr[:, span, :].reshape(128, 128) for span in spans]
            mixed = point_mix(w_ref, fields[0], fields[1])[0]
            for k in range(2):
                value = v_scr[:, spans[k], :].reshape(128, 128) + mixed[:, 128 * k : 128 * k + 128]
                v_scr[:, spans[k], :] = value.reshape(16, 8, 128)
            return carry

        lax.fori_loop(0, 4, body, 0, unroll=True)
        part = pl.ds(chunk * 64, 64)
        store = pltpu.make_async_copy(v_scr.at[:, part], out_hbm.at[:, part], sems.at[1 + chunk])
        store.start()
        stores.append(store)
    for store in stores:
        store.wait()


def modes_place_kernel(m_ref, o_ref):
    for high in range(2):
        for right in range(2):
            rows = [m_ref[high * 16 + right * 8 + m, 2] for m in range(8)]
            rows = swap_blocks(rows)
            for k in range(4):
                for up in range(2):
                    for copy in range(8):
                        o_ref[
                            copy, high + 2 * up, k * 8 : (k + 1) * 8,
                            right * 128 : (right + 1) * 128,
                        ] = rows[2 * k + up]


def call(kernel, ins, outs, scratch=(), sems=0, mib=8):
    spaces = {"v": pltpu.VMEM, "s": pltpu.SMEM, "a": pltpu.HBM}
    structs = [jax.ShapeDtypeStruct(o[0], o[2] if len(o) > 2 else F32) for o in outs]
    scratches = [pltpu.VMEM(shape, F32) for shape in scratch]
    if sems:
        scratches.append(pltpu.SemaphoreType.DMA((sems,)))
    return pl.pallas_call(
        kernel,
        out_shape=structs,
        in_specs=[pl.BlockSpec(memory_space=spaces[k]) for k in ins],
        out_specs=[pl.BlockSpec(memory_space=spaces[o[1]]) for o in outs],
        scratch_shapes=scratches,
        compiler_params=pltpu.CompilerParams(vmem_limit_bytes=mib * 1024 * 1024),
    )


def local(flow_field, cotangent, mode_weights, point_weights, point_bias):
    swap_x = lambda v: lax.all_to_all(v, "gx", 0, 0, tiled=False)
    swap_y = lambda v: lax.all_to_all(v, "gy", 0, 0, tiled=False)
    packed = ((8, 2, 72, 128), "v")
    coefs = ((32, 2, 8, 128), "v")
    square = ((256, 128), "v")
    row = ((8, 128), "v")
    cells = (16, 256, 128)
    parts = (16, 80, 128)
    rows3 = [(32, 2, 8, 128)]
    table = jnp.asarray(y_table())
    down, up = (jnp.asarray(t) for t in cell_tables())
    slab = lax.axis_index("gy").astype(jnp.int32).reshape(1)
    flow_cells = flow_field.reshape(cells)
    kron = ((128, 384), "v", BF16)

    weights, mix_forward, mix_back = call(weights_kernel, "svv", [square, kron, kron])(
        slab, mode_weights.reshape(4, 256, 256), point_weights
    )
    (sent,) = call(analyse_kernel, "av", [packed], [cells, parts], 4, 58)(flow_cells, down)
    (got,) = call(rows_kernel, "v", [coefs], rows3)(swap_x(sent))
    back, bands_flow = call(mix_kernel, "vvv", [coefs, square], [(256, 128)])(
        swap_y(got), table, weights
    )
    (spread,) = call(spread_kernel, "v", [packed], rows3)(swap_y(back))
    output_field, grads, sent = call(
        centre_kernel, "vaavsvv", [(cells, "a"), (cells, "a"), packed],
        [cells] * 4 + [parts] * 2 + [(128, 128)] * 2, 10, 58,
    )(
        swap_x(spread), flow_cells, cotangent.reshape(cells), mix_forward, point_bias, down, up
    )
    got, bias_part = call(rows_grad_kernel, "v", [coefs, row], rows3)(swap_x(sent))
    bands_grad, mode_part, point_total = call(
        grad_bands_kernel, "vvv", [square, ((8, 8, 128), "v"), row], [(256, 128)]
    )(swap_y(got), table, bands_flow)
    (back,) = call(mix_grad_kernel, "vvvv", [coefs], [(256, 128)])(
        bands_grad, table, weights, bias_part
    )
    (joined,) = call(join_kernel, "vv", [((32, 3, 8, 128), "v")])(back, swap_x(mode_part))
    joined = swap_y(joined)
    spread, bias_total = call(spread_grad_kernel, "v", [packed, row], rows3)(joined)
    (grad_field,) = call(
        finish_kernel, "vavv", [(cells, "a")], [cells] * 2 + [parts], 5, 58
    )(swap_x(spread), grads, mix_back, up)
    (placed,) = call(modes_place_kernel, "v", [((8, 4, 32, 256), "v")])(joined)
    modes = jnp.transpose(swap_x(placed), (1, 0, 2, 3)).reshape(4, 16, 16, 256)

    cell_count = flow_field.shape[3] * 256 * 256
    return (
        output_field.reshape(flow_field.shape),
        grad_field.reshape(flow_field.shape),
        modes,
        point_total[0:2].reshape(16, 16) / math.sqrt(cell_count),
        bias_total[0, :16] / math.sqrt(cell_count),
    )


def solution(mesh):
    in_specs = (P(None, "gx", "gy", None), P(None, "gx", "gy", None), P(), P(), P())
    out_specs = (P(None, "gx", "gy", None), P(None, "gx", "gy", None), P(), P(), P())
    return jax.shard_map(local, mesh=mesh, in_specs=in_specs, out_specs=out_specs, check_vma=False)
```

```python
import math

import jax
import jax.numpy as jnp
import ml_dtypes
import numpy as np
from jax import lax
from jax.experimental import pallas as pl
from jax.experimental.pallas import tpu as pltpu
from jax.sharding import PartitionSpec as P

LOW_PASS = [
    0.23037781330885523,
    0.7148465705525415,
    0.6308807679295904,
    -0.02798376941698385,
    -0.18703481171888114,
    0.030841381835986965,
    0.032883011666982945,
    -0.010597401784997278,
]
HIGH_PASS = [(-1) ** position * LOW_PASS[7 - position] for position in range(8)]
GELU_SCALE = 0.7978845608028654
GELU_CUBE = 0.044715


def triple_low():
    taps = np.zeros(50)
    for p, hp in enumerate(LOW_PASS):
        for q, hq in enumerate(LOW_PASS):
            for r, hr in enumerate(LOW_PASS):
                taps[p + 2 * q + 4 * r] += hp * hq * hr
    return [float(t) for t in taps]


TRIPLE = triple_low()
HIGHEST = lax.Precision.HIGHEST
F32 = jnp.float32
BF16 = jnp.bfloat16


def cell_tables():
    table = np.zeros((80, 256))
    for a in range(10):
        for b in range(7):
            for x in range(32):
                for y in range(8):
                    at_x, at_y = x + 48 - 8 * a, y + 48 - 8 * b
                    if 0 <= at_x < 50 and 0 <= at_y < 50:
                        table[a * 7 + b, x * 8 + y] = TRIPLE[at_x] * TRIPLE[at_y]
    table = table.astype(np.float32)
    high = table.astype(ml_dtypes.bfloat16)
    low = (table - high.astype(np.float32)).astype(ml_dtypes.bfloat16)
    down = np.concatenate([high, low])
    pad = np.zeros((256, 16), ml_dtypes.bfloat16)
    up = np.concatenate([high.T, low.T, high.T, pad], 1)
    return down, up


def y_table():
    table = np.zeros((32, 8, 128), np.float32)
    for slab in range(32):
        for b in range(7):
            ky = (slab - 6 + b) % 32
            for mode in range(16):
                at = (ky - 2 * mode) % 32
                if at < 8:
                    table[slab, b, mode] = LOW_PASS[at]
                    table[slab, b, 16 + mode] = HIGH_PASS[at]
    return table.reshape(256, 128)


def gather_sum(pairs):
    total = None
    for weight, value in pairs:
        term = value * weight
        total = term if total is None else total + term
    return total


def swap_blocks(rows):
    lane = lax.broadcasted_iota(jnp.int32, (8, 128), 1)
    rows = list(rows)
    for bit in range(3):
        width = 16 << bit
        upper = (lane & width) != 0
        for lo in range(8):
            if lo & (1 << bit):
                continue
            hi = lo | (1 << bit)
            first, second = rows[lo], rows[hi]
            rows[lo] = jnp.where(upper, pltpu.roll(second, width, 1), first)
            rows[hi] = jnp.where(upper, second, pltpu.roll(first, 128 - width, 1))
    return rows


def split(value):
    high = value.astype(BF16)
    return high, (value - high.astype(F32)).astype(BF16)


def dot(left, right):
    return lax.dot_general(left, right, (((1,), (0,)), ((), ())), preferred_element_type=F32)


def exact_dot(left, right):
    return lax.dot_general(
        left, right, (((1,), (0,)), ((), ())), precision=HIGHEST, preferred_element_type=F32
    )


def side_by_side(values):
    return jnp.concatenate(values, axis=1)


def analyse_pair(field, pair, down_ref, p_scr):
    high, low = split(side_by_side([field[2 * pair], field[2 * pair + 1]]))
    wide = dot(down_ref[...], high)
    total = wide[0:80] + wide[80:160] + dot(down_ref[0:80, :], low)
    p_scr[2 * pair] = total[:, 0:128]
    p_scr[2 * pair + 1] = total[:, 128:256]


def pack_planes(p_scr, s_ref):
    def body(octet, carry):
        at = pl.ds(pl.multiple_of(octet * 8, 8), 8)
        for half in range(2):
            rows = swap_blocks([p_scr[half * 8 + c, at, :] for c in range(8)])
            for group in range(8):
                s_ref[group, half, at, :] = rows[group]
        return carry

    lax.fori_loop(0, 9, body, 0, unroll=True)


def unpack_planes(r_ref, d_scr):
    def body(octet, carry):
        at = pl.ds(pl.multiple_of(octet * 8, 8), 8)
        for half in range(2):
            rows = swap_blocks([r_ref[group, half, at, :] for group in range(8)])
            for c in range(8):
                d_scr[half * 8 + c, at, :] = rows[c]
        return carry

    lax.fori_loop(0, 9, body, 0, unroll=True)
    for c in range(16):
        d_scr[c, 72:80, :] = jnp.zeros((8, 128), F32)


def lift_pair(d_scr, pair, up_ref):
    high, low = split(side_by_side([d_scr[2 * pair], d_scr[2 * pair + 1]]))
    stacked = jnp.concatenate([high, high, low, jnp.zeros((16, 256), BF16)], axis=0)
    return dot(up_ref[...], stacked)


def analyse_kernel(flow_hbm, down_ref, s_ref, f_scr, p_scr, sems):
    copies = [
        pltpu.make_async_copy(flow_hbm.at[pl.ds(4 * k, 4)], f_scr.at[pl.ds(4 * k, 4)], sems.at[k])
        for k in range(4)
    ]
    for copy in copies:
        copy.start()
    for pair in range(8):
        if pair % 2 == 0:
            copies[pair // 2].wait()
        analyse_pair(f_scr, pair, down_ref, p_scr)
    pack_planes(p_scr, s_ref)


def rows_body(r_ref, l_scr, v_ref):
    def collect(q, carry):
        one = (q + 1) % 8
        two = (q + 2) % 8
        for t in range(4):
            for half in range(2):
                total = r_ref[q, half, 7 * (6 + t) : 7 * (6 + t) + 8, :]
                total = total + r_ref[one, half, 7 * (2 + t) : 7 * (2 + t) + 8, :]
                if t >= 2:
                    total = total + r_ref[two, half, 7 * (t - 2) : 7 * (t - 2) + 8, :]
                l_scr[q * 4 + t, half] = total
        return carry

    lax.fori_loop(0, 8, collect, 0)

    def bands(mode, carry):
        for half in range(2):
            parts = [l_scr[(2 * mode + n) % 32, half] for n in range(8)]
            v_ref[mode, half] = gather_sum(list(zip(LOW_PASS, parts)))
            v_ref[mode + 16, half] = gather_sum(list(zip(HIGH_PASS, parts)))
        return carry

    lax.fori_loop(0, 16, bands, 0)


def rows_kernel(r_ref, v_ref, l_scr):
    rows_body(r_ref, l_scr, v_ref)


def rows_grad_kernel(r_ref, v_ref, bias_ref, l_scr):
    rows_body(r_ref, l_scr, v_ref)
    first = r_ref[0, 0, 70:71, :]
    second = r_ref[0, 0, 71:72, :]
    bias = r_ref[0, 1, 70:71, :]
    for i in range(1, 8):
        first = first + r_ref[i, 0, 70:71, :]
        second = second + r_ref[i, 0, 71:72, :]
        bias = bias + r_ref[i, 1, 70:71, :]

    def put(coef, carry):
        v_ref[coef, 0, 7:8, :] = first
        v_ref[coef, 1, 7:8, :] = second
        return carry

    lax.fori_loop(0, 32, put, 0)
    bias_ref[...] = jnp.broadcast_to(bias, (8, 128))


def weights_kernel(index_ref, w_ref, pw_ref, o_ref, forward_ref, back_ref):
    slab = index_ref[0]
    high = slab // 16
    mode = slab % 16
    right = mode // 8
    shift = (8 - mode % 8) * 16
    lane = lax.broadcasted_iota(jnp.int32, (256, 128), 1)
    low_y = jnp.where(right == 0, w_ref[high, :, 0:128], w_ref[high, :, 128:256])
    high_y = jnp.where(right == 0, w_ref[high + 2, :, 0:128], w_ref[high + 2, :, 128:256])
    low_y = pltpu.roll(low_y, shift % 128, 1)
    high_y = pltpu.roll(high_y, (shift + 16) % 128, 1)
    o_ref[...] = jnp.where(lane < 16, low_y, jnp.where(lane < 32, high_y, 0.0))
    same_y = iota(128, 128, 0) % 8 == iota(128, 128, 1) % 8
    rows = (iota(128, 16, 0) // 8 == iota(128, 16, 1)).astype(F32)
    cols = (iota(16, 128, 1) // 8 == iota(16, 128, 0)).astype(F32)
    point = pw_ref[...]
    for ref, matrix in ((forward_ref, point.T), (back_ref, point)):
        wide = jnp.where(same_y, exact_dot(exact_dot(rows, matrix), cols), 0.0)
        upper, lower = split(wide)
        ref[...] = side_by_side([upper, lower, upper])


def iota(rows, cols, axis):
    return lax.broadcasted_iota(jnp.int32, (rows, cols), axis)


def column_bands(v_ref, q_ref, half):
    value = v_ref[:, half].reshape(256, 128)
    return lax.dot_general(
        value.T, q_ref[...], (((1,), (0,)), ((), ())), precision=HIGHEST,
        preferred_element_type=F32,
    )


def column_changes(d_scr, q_ref, o_ref):
    for half in range(2):
        value = lax.dot_general(
            q_ref[...], d_scr[half * 128 : (half + 1) * 128, :], (((1,), (1,)), ((), ())),
            precision=HIGHEST, preferred_element_type=F32,
        )
        o_ref[:, half] = value.reshape(32, 8, 128)


def mix_kernel(v_ref, q_ref, w_ref, o_ref, y_ref, d_scr):
    for half in range(2):
        y_ref[half * 128 : (half + 1) * 128, :] = column_bands(v_ref, q_ref, half)

    def body(o, carry):
        total = -y_ref[pl.ds(pl.multiple_of(o * 16, 16), 16), :]
        for i in range(16):
            total = total + y_ref[i * 16 : (i + 1) * 16, :] * w_ref[pl.ds(i * 16 + o, 1), :]
        d_scr[pl.ds(pl.multiple_of(o * 16, 16), 16), :] = total
        return carry

    lax.fori_loop(0, 16, body, 0)
    column_changes(d_scr, q_ref, o_ref)


def grad_bands_kernel(v_ref, q_ref, y_ref, b_ref, g_ref, p_ref, g_scr):
    for half in range(2):
        b_ref[half * 128 : (half + 1) * 128, :] = column_bands(v_ref, q_ref, half)

    def body(i, carry):
        flow = y_ref[pl.ds(pl.multiple_of(i * 16, 16), 16), :]
        for o in range(16):
            grad = b_ref[o * 16 : (o + 1) * 16, :]
            g_scr[pl.ds(i * 16 + o, 1), :] = jnp.sum(flow * grad, axis=0, keepdims=True)
        return carry

    lax.fori_loop(0, 16, body, 0)
    lane = lax.broadcasted_iota(jnp.int32, (8, 128), 1)
    for group in range(8):
        packed = g_scr[group * 32 : group * 32 + 8, :]
        for k in range(1, 4):
            rows = g_scr[group * 32 + k * 8 : group * 32 + k * 8 + 8, :]
            packed = jnp.where(lane // 32 == k, pltpu.roll(rows, 32 * k, 1), packed)
        for copy in range(8):
            g_ref[copy, group] = packed
    first = v_ref[0, 0, 7:8, :]
    second = v_ref[0, 1, 7:8, :]
    for slab in range(1, 32):
        first = first + v_ref[slab, 0, 7:8, :]
        second = second + v_ref[slab, 1, 7:8, :]
    p_ref[...] = jnp.zeros((8, 128), F32)
    p_ref[0:1, :] = first
    p_ref[1:2, :] = second


def mix_grad_kernel(b_ref, q_ref, w_ref, bias_ref, o_ref, d_scr):
    def body(i, carry):
        total = -b_ref[pl.ds(pl.multiple_of(i * 16, 16), 16), :]
        for o in range(16):
            total = total + b_ref[o * 16 : (o + 1) * 16, :] * w_ref[pl.ds(i * 16 + o, 1), :]
        d_scr[pl.ds(pl.multiple_of(i * 16, 16), 16), :] = total
        return carry

    lax.fori_loop(0, 16, body, 0)
    column_changes(d_scr, q_ref, o_ref)
    for slab in range(32):
        o_ref[slab, 0, 7:8, :] = bias_ref[0:1, :]


def join_kernel(v_ref, g_ref, o_ref):
    for quarter in range(4):
        totals = []
        for group in (2 * quarter, 2 * quarter + 1):
            total = g_ref[0, group]
            for i in range(1, 8):
                total = total + g_ref[i, group]
            totals.append(total * (1.0 / math.sqrt(128.0)))
        for slab in range(8 * quarter, 8 * quarter + 8):
            o_ref[slab, 0:2] = v_ref[slab]
            o_ref[slab, 2] = totals[0]
            o_ref[slab, 3] = totals[1]


def spread_body(v_ref, l_scr, s_ref):
    def lift(mode, carry):
        for half in range(2):
            low = [v_ref[(mode + 16 - d) % 16, half] for d in range(4)]
            high = [v_ref[16 + (mode + 16 - d) % 16, half] for d in range(4)]
            for p in range(2):
                pairs = [(LOW_PASS[2 * d + p], low[d]) for d in range(4)]
                pairs += [(HIGH_PASS[2 * d + p], high[d]) for d in range(4)]
                l_scr[2 * mode + p, half] = gather_sum(pairs)
        return carry

    lax.fori_loop(0, 16, lift, 0)

    def send(i, carry):
        for half in range(2):
            s_ref[i, half, 64:72, :] = jnp.zeros((8, 128), F32)
            for a in range(10):
                s_ref[i, half, 7 * a : 7 * a + 8, :] = l_scr[(4 * i + 26 + a) % 32, half]
        return carry

    lax.fori_loop(0, 8, send, 0)


def spread_kernel(v_ref, s_ref, l_scr):
    spread_body(v_ref, l_scr, s_ref)


def spread_grad_kernel(v_ref, s_ref, bias_ref, l_scr):
    spread_body(v_ref, l_scr, s_ref)
    bias = v_ref[0, 0, 7:8, :]
    for slab in range(1, 32):
        bias = bias + v_ref[slab, 0, 7:8, :]
    bias_ref[...] = jnp.broadcast_to(bias, (8, 128))


def point_mix(w_ref, first, second):
    high, low = split(side_by_side([first, second]))
    return dot(w_ref[...], jnp.concatenate([high, high, low], axis=0)), high, low


def centre_kernel(
    r_ref, flow_hbm, cot_hbm, w_ref, bias_ref, down_ref, up_ref, out_hbm, g_hbm, s_ref,
    f_scr, c_scr, v_scr, g_scr, d_scr, p_scr, sum_scr, pt_scr, sems,
):
    load_flow = pltpu.make_async_copy(flow_hbm, f_scr, sems.at[0])
    load_cot = pltpu.make_async_copy(cot_hbm, c_scr, sems.at[1])
    load_flow.start()
    load_cot.start()
    unpack_planes(r_ref, d_scr)
    sum_scr[...] = jnp.zeros((128, 128), F32)
    pt_scr[...] = jnp.zeros((128, 128), F32)
    load_flow.wait()
    for pair in range(8):
        change = lift_pair(d_scr, pair, up_ref)
        for k in range(2):
            c = 2 * pair + k
            v_scr[c] = f_scr[c] + (change[:, 128 * k : 128 * k + 128] + bias_ref[c])
    load_cot.wait()
    stores = []
    for chunk in range(4):

        def body(step, carry):
            start = pl.multiple_of((chunk * 4 + step) * 16, 16)
            spans = [pl.ds(start, 8), pl.ds(pl.multiple_of(start + 8, 8), 8)]
            fields = [f_scr[:, span, :].reshape(128, 128) for span in spans]
            mixed, f_high, f_low = point_mix(w_ref, fields[0], fields[1])
            grads = []
            for k in range(2):
                value = v_scr[:, spans[k], :].reshape(128, 128) + mixed[:, 128 * k : 128 * k + 128]
                square = value * value
                tangent = jnp.tanh(value * (GELU_SCALE + (GELU_SCALE * GELU_CUBE) * square))
                half_up = 0.5 + 0.5 * tangent
                v_scr[:, spans[k], :] = (value * half_up).reshape(16, 8, 128)
                bend = value * ((0.5 * GELU_SCALE) + (1.5 * GELU_SCALE * GELU_CUBE) * square)
                slope = half_up + bend * (1.0 - tangent * tangent)
                grad = c_scr[:, spans[k], :].reshape(128, 128) * slope
                g_scr[:, spans[k], :] = grad.reshape(16, 8, 128)
                grads.append(grad)
            sum_scr[...] += grads[0] + grads[1]
            g_high, g_low = split(side_by_side(grads))
            pt_scr[...] += lax.dot_general(
                side_by_side([f_high, f_low, f_high]), side_by_side([g_high, g_high, g_low]),
                (((1,), (1,)), ((), ())), preferred_element_type=F32,
            )
            return carry

        lax.fori_loop(0, 4, body, 0, unroll=True)
        part = pl.ds(chunk * 64, 64)
        for k, (scr, hbm) in enumerate(((v_scr, out_hbm), (g_scr, g_hbm))):
            store = pltpu.make_async_copy(
                scr.at[:, part], hbm.at[:, part], sems.at[2 + 2 * chunk + k]
            )
            store.start()
            stores.append(store)
    for pair in range(8):
        analyse_pair(g_scr, pair, down_ref, p_scr)
    pack_planes(p_scr, s_ref)
    same_y = iota(128, 128, 0) % 8 == iota(128, 128, 1) % 8
    gather = (iota(16, 128, 1) // 8 == iota(16, 128, 0)).astype(F32)
    fold = (iota(128, 128, 0) // 8 == iota(128, 128, 1) % 16).astype(F32)
    wide = exact_dot(exact_dot(gather, jnp.where(same_y, pt_scr[...], 0.0)), fold)
    lane, row = iota(16, 128, 1), iota(16, 128, 0)
    wide = jnp.where(lane // 16 == row % 8, wide, 0.0)
    first = jnp.sum(wide[0:8], axis=0, keepdims=True)
    second = jnp.sum(wide[8:16], axis=0, keepdims=True)
    totals = jnp.sum(exact_dot(gather, sum_scr[...]), axis=1, keepdims=True)
    bias_row = jnp.sum(jnp.where(lane == row, totals, 0.0), axis=0, keepdims=True)
    for group in range(8):
        s_ref[group, 0, 70:71, :] = first
        s_ref[group, 0, 71:72, :] = second
        s_ref[group, 1, 70:71, :] = bias_row
    for store in stores:
        store.wait()


def finish_kernel(r_ref, g_hbm, w_ref, up_ref, out_hbm, g_scr, v_scr, d_scr, sems):
    load = pltpu.make_async_copy(g_hbm, g_scr, sems.at[0])
    load.start()
    unpack_planes(r_ref, d_scr)
    load.wait()
    for pair in range(8):
        change = lift_pair(d_scr, pair, up_ref)
        for k in range(2):
            v_scr[2 * pair + k] = g_scr[2 * pair + k] + change[:, 128 * k : 128 * k + 128]
    stores = []
    for chunk in range(4):

        def body(step, carry):
            start = pl.multiple_of((chunk * 4 + step) * 16, 16)
            spans = [pl.ds(start, 8), pl.ds(pl.multiple_of(start + 8, 8), 8)]
            fields = [g_scr[:, span, :].reshape(128, 128) for span in spans]
            mixed = point_mix(w_ref, fields[0], fields[1])[0]
            for k in range(2):
                value = v_scr[:, spans[k], :].reshape(128, 128) + mixed[:, 128 * k : 128 * k + 128]
                v_scr[:, spans[k], :] = value.reshape(16, 8, 128)
            return carry

        lax.fori_loop(0, 4, body, 0, unroll=True)
        part = pl.ds(chunk * 64, 64)
        store = pltpu.make_async_copy(v_scr.at[:, part], out_hbm.at[:, part], sems.at[1 + chunk])
        store.start()
        stores.append(store)
    for store in stores:
        store.wait()


def modes_place_kernel(m_ref, o_ref):
    for high in range(2):
        for right in range(2):
            for group in range(2):
                rows = [m_ref[high * 16 + right * 8 + m, 2 + group] for m in range(8)]
                rows = swap_blocks(rows)
                for k in range(4):
                    at = group * 32 + k * 8
                    for up in range(2):
                        o_ref[
                            high + 2 * up, at : at + 8, right * 128 : (right + 1) * 128
                        ] = rows[2 * k + up]


def gather_kernel(index_ref, first, second, third, fourth, out_hbm, sems):
    copies = []
    for k, part in enumerate((first, second, third, fourth)):
        owner = (index_ref[0] // 8 + 4 - k) % 4
        to = out_hbm.at[:, pl.ds(pl.multiple_of(owner * 64, 64), 64), :]
        copies.append(pltpu.make_async_copy(part, to, sems.at[k]))
    for copy in copies:
        copy.start()
    for copy in copies:
        copy.wait()


def call(kernel, ins, outs, scratch=(), sems=0, mib=8):
    spaces = {"v": pltpu.VMEM, "s": pltpu.SMEM, "a": pltpu.HBM}
    structs = [jax.ShapeDtypeStruct(o[0], o[2] if len(o) > 2 else F32) for o in outs]
    scratches = [pltpu.VMEM(shape, F32) for shape in scratch]
    if sems:
        scratches.append(pltpu.SemaphoreType.DMA((sems,)))
    return pl.pallas_call(
        kernel,
        out_shape=structs,
        in_specs=[pl.BlockSpec(memory_space=spaces[k]) for k in ins],
        out_specs=[pl.BlockSpec(memory_space=spaces[o[1]]) for o in outs],
        scratch_shapes=scratches,
        compiler_params=pltpu.CompilerParams(vmem_limit_bytes=mib * 1024 * 1024),
    )


def local(flow_field, cotangent, mode_weights, point_weights, point_bias):
    swap_x = lambda v: lax.all_to_all(v, "gx", 0, 0, tiled=False)
    swap_y = lambda v: lax.all_to_all(v, "gy", 0, 0, tiled=False)
    packed = ((8, 2, 72, 128), "v")
    coefs = ((32, 2, 8, 128), "v")
    square = ((256, 128), "v")
    row = ((8, 128), "v")
    cells = (16, 256, 128)
    parts = (16, 80, 128)
    rows3 = [(32, 2, 8, 128)]
    table = jnp.asarray(y_table())
    down, up = (jnp.asarray(t) for t in cell_tables())
    slab = lax.axis_index("gy").astype(jnp.int32).reshape(1)
    flow_cells = flow_field.reshape(cells)
    kron = ((128, 384), "v", BF16)

    weights, mix_forward, mix_back = call(weights_kernel, "svv", [square, kron, kron])(
        slab, mode_weights.reshape(4, 256, 256), point_weights
    )
    (sent,) = call(analyse_kernel, "av", [packed], [cells, parts], 4, 58)(flow_cells, down)
    (got,) = call(rows_kernel, "v", [coefs], rows3)(swap_x(sent))
    back, bands_flow = call(mix_kernel, "vvv", [coefs, square], [(256, 128)])(
        swap_y(got), table, weights
    )
    (spread,) = call(spread_kernel, "v", [packed], rows3)(swap_y(back))
    output_field, grads, sent = call(
        centre_kernel, "vaavsvv", [(cells, "a"), (cells, "a"), packed],
        [cells] * 4 + [parts] * 2 + [(128, 128)] * 2, 10, 52,
    )(
        swap_x(spread), flow_cells, cotangent.reshape(cells), mix_forward, point_bias, down, up
    )
    got, bias_part = call(rows_grad_kernel, "v", [coefs, row], rows3)(swap_x(sent))
    bands_grad, mode_part, point_total = call(
        grad_bands_kernel, "vvv", [square, ((8, 8, 8, 128), "v"), row], [(256, 128)]
    )(swap_y(got), table, bands_flow)
    (back,) = call(mix_grad_kernel, "vvvv", [coefs], [(256, 128)])(
        bands_grad, table, weights, bias_part
    )
    (joined,) = call(join_kernel, "vv", [((32, 4, 8, 128), "v")])(back, swap_x(mode_part))
    joined = swap_y(joined)
    spread, bias_total = call(spread_grad_kernel, "v", [packed, row], rows3)(joined)
    (grad_field,) = call(
        finish_kernel, "vavv", [(cells, "a")], [cells] * 2 + [parts], 5, 52
    )(swap_x(spread), grads, mix_back, up)
    (placed,) = call(modes_place_kernel, "v", [((4, 64, 256), "v")])(joined)
    shifted = [
        lax.ppermute(placed, "gy", [(j, (j + 8 * k) % 32) for j in range(32)]) for k in (1, 2, 3)
    ]
    slab, grad_field = lax.optimization_barrier((slab, grad_field))
    (modes,) = call(gather_kernel, "saaaa", [((4, 256, 256), "a")], (), 4)(slab, placed, *shifted)

    cell_count = flow_field.shape[3] * 256 * 256
    return (
        output_field.reshape(flow_field.shape),
        grad_field.reshape(flow_field.shape),
        modes.reshape(4, 16, 16, 256),
        point_total[0:2].reshape(16, 16) / math.sqrt(cell_count),
        bias_total[0, :16] / math.sqrt(cell_count),
    )


def solution(mesh):
    in_specs = (P(None, "gx", "gy", None), P(None, "gx", "gy", None), P(), P(), P())
    out_specs = (P(None, "gx", "gy", None), P(None, "gx", "gy", None), P(), P(), P())
    return jax.shard_map(local, mesh=mesh, in_specs=in_specs, out_specs=out_specs, check_vma=False)
```

```python
import math

import jax
import jax.numpy as jnp
import ml_dtypes
import numpy as np
from jax import lax
from jax.experimental import pallas as pl
from jax.experimental.pallas import tpu as pltpu
from jax.sharding import PartitionSpec as P

LOW_PASS = [
    0.23037781330885523,
    0.7148465705525415,
    0.6308807679295904,
    -0.02798376941698385,
    -0.18703481171888114,
    0.030841381835986965,
    0.032883011666982945,
    -0.010597401784997278,
]
HIGH_PASS = [(-1) ** position * LOW_PASS[7 - position] for position in range(8)]
GELU_SCALE = 0.7978845608028654
GELU_CUBE = 0.044715


def triple_low():
    taps = np.zeros(50)
    for p, hp in enumerate(LOW_PASS):
        for q, hq in enumerate(LOW_PASS):
            for r, hr in enumerate(LOW_PASS):
                taps[p + 2 * q + 4 * r] += hp * hq * hr
    return [float(t) for t in taps]


TRIPLE = triple_low()
HIGHEST = lax.Precision.HIGHEST
F32 = jnp.float32
BF16 = jnp.bfloat16


def cell_tables():
    table = np.zeros((80, 256))
    for a in range(10):
        for b in range(7):
            for x in range(32):
                for y in range(8):
                    at_x, at_y = x + 48 - 8 * a, y + 48 - 8 * b
                    if 0 <= at_x < 50 and 0 <= at_y < 50:
                        table[a * 7 + b, x * 8 + y] = TRIPLE[at_x] * TRIPLE[at_y]
    table = table.astype(np.float32)
    high = table.astype(ml_dtypes.bfloat16)
    low = (table - high.astype(np.float32)).astype(ml_dtypes.bfloat16)
    down = np.concatenate([high, low])
    pad = np.zeros((256, 16), ml_dtypes.bfloat16)
    up = np.concatenate([high.T, low.T, high.T, pad], 1)
    return down, up


def y_table():
    table = np.zeros((32, 8, 128), np.float32)
    for slab in range(32):
        for b in range(7):
            ky = (slab - 6 + b) % 32
            for mode in range(16):
                at = (ky - 2 * mode) % 32
                if at < 8:
                    table[slab, b, mode] = LOW_PASS[at]
                    table[slab, b, 16 + mode] = HIGH_PASS[at]
    return table.reshape(256, 128)


def gather_sum(pairs):
    total = None
    for weight, value in pairs:
        term = value * weight
        total = term if total is None else total + term
    return total


def swap_blocks(rows):
    lane = lax.broadcasted_iota(jnp.int32, (8, 128), 1)
    rows = [rows[0]] + [pltpu.roll(rows[c], 16 * c, 1) for c in range(1, 8)]
    for bit in range(3):
        step = 1 << bit
        chosen = (lane & (16 * step)) != 0
        rows = [jnp.where(chosen, rows[(m + step) % 8], rows[m]) for m in range(8)]
    rows = [rows[(8 - k) % 8] for k in range(8)]
    return [rows[0]] + [pltpu.roll(rows[k], 128 - 16 * k, 1) for k in range(1, 8)]


def split(value):
    high = value.astype(BF16)
    return high, (value - high.astype(F32)).astype(BF16)


def dot(left, right):
    return lax.dot_general(left, right, (((1,), (0,)), ((), ())), preferred_element_type=F32)


def exact_dot(left, right):
    return lax.dot_general(
        left, right, (((1,), (0,)), ((), ())), precision=HIGHEST, preferred_element_type=F32
    )


def side_by_side(values):
    return jnp.concatenate(values, axis=1)


def analyse_pair(field, pair, down_ref, p_scr):
    high, low = split(side_by_side([field[2 * pair], field[2 * pair + 1]]))
    wide = dot(down_ref[...], high)
    total = wide[0:80] + wide[80:160] + dot(down_ref[0:80, :], low)
    p_scr[2 * pair] = total[:, 0:128]
    p_scr[2 * pair + 1] = total[:, 128:256]


def pack_planes(p_scr, s_ref):
    def body(octet, carry):
        at = pl.ds(pl.multiple_of(octet * 8, 8), 8)
        for half in range(2):
            rows = swap_blocks([p_scr[half * 8 + c, at, :] for c in range(8)])
            for group in range(8):
                s_ref[group, half, at, :] = rows[group]
        return carry

    lax.fori_loop(0, 9, body, 0, unroll=True)


def unpack_planes(r_ref, d_scr):
    def body(octet, carry):
        at = pl.ds(pl.multiple_of(octet * 8, 8), 8)
        for half in range(2):
            rows = swap_blocks([r_ref[group, half, at, :] for group in range(8)])
            for c in range(8):
                d_scr[half * 8 + c, at, :] = rows[c]
        return carry

    lax.fori_loop(0, 9, body, 0, unroll=True)
    for c in range(16):
        d_scr[c, 72:80, :] = jnp.zeros((8, 128), F32)


def lift_pair(d_scr, pair, up_ref):
    high, low = split(side_by_side([d_scr[2 * pair], d_scr[2 * pair + 1]]))
    stacked = jnp.concatenate([high, high, low, jnp.zeros((16, 256), BF16)], axis=0)
    return dot(up_ref[...], stacked)


def analyse_kernel(flow_hbm, down_ref, s_ref, f_scr, p_scr, sems):
    copies = [
        pltpu.make_async_copy(flow_hbm.at[pl.ds(4 * k, 4)], f_scr.at[pl.ds(4 * k, 4)], sems.at[k])
        for k in range(4)
    ]
    for copy in copies:
        copy.start()
    for pair in range(8):
        if pair % 2 == 0:
            copies[pair // 2].wait()
        analyse_pair(f_scr, pair, down_ref, p_scr)
    pack_planes(p_scr, s_ref)


def rows_body(r_ref, l_scr, v_ref):
    def collect(q, carry):
        one = (q + 1) % 8
        two = (q + 2) % 8
        for t in range(4):
            for half in range(2):
                total = r_ref[q, half, 7 * (6 + t) : 7 * (6 + t) + 8, :]
                total = total + r_ref[one, half, 7 * (2 + t) : 7 * (2 + t) + 8, :]
                if t >= 2:
                    total = total + r_ref[two, half, 7 * (t - 2) : 7 * (t - 2) + 8, :]
                l_scr[q * 4 + t, half] = total
        return carry

    lax.fori_loop(0, 8, collect, 0)

    def bands(mode, carry):
        for half in range(2):
            parts = [l_scr[(2 * mode + n) % 32, half] for n in range(8)]
            v_ref[mode, half] = gather_sum(list(zip(LOW_PASS, parts)))
            v_ref[mode + 16, half] = gather_sum(list(zip(HIGH_PASS, parts)))
        return carry

    lax.fori_loop(0, 16, bands, 0)


def rows_kernel(r_ref, v_ref, l_scr):
    rows_body(r_ref, l_scr, v_ref)


def rows_grad_kernel(r_ref, v_ref, bias_ref, l_scr):
    rows_body(r_ref, l_scr, v_ref)
    first = r_ref[0, 0, 70:71, :]
    second = r_ref[0, 0, 71:72, :]
    bias = r_ref[0, 1, 70:71, :]
    for i in range(1, 8):
        first = first + r_ref[i, 0, 70:71, :]
        second = second + r_ref[i, 0, 71:72, :]
        bias = bias + r_ref[i, 1, 70:71, :]

    def put(coef, carry):
        v_ref[coef, 0, 7:8, :] = first
        v_ref[coef, 1, 7:8, :] = second
        return carry

    lax.fori_loop(0, 32, put, 0)
    bias_ref[...] = jnp.broadcast_to(bias, (8, 128))


def weights_kernel(index_ref, w_ref, pw_ref, o_ref, forward_ref, back_ref):
    slab = index_ref[0]
    high = slab // 16
    mode = slab % 16
    right = mode // 8
    shift = (8 - mode % 8) * 16
    lane = lax.broadcasted_iota(jnp.int32, (256, 128), 1)
    low_y = jnp.where(right == 0, w_ref[high, :, 0:128], w_ref[high, :, 128:256])
    high_y = jnp.where(right == 0, w_ref[high + 2, :, 0:128], w_ref[high + 2, :, 128:256])
    low_y = pltpu.roll(low_y, shift % 128, 1)
    high_y = pltpu.roll(high_y, (shift + 16) % 128, 1)
    o_ref[...] = jnp.where(lane < 16, low_y, jnp.where(lane < 32, high_y, 0.0))
    same_y = iota(128, 128, 0) % 8 == iota(128, 128, 1) % 8
    rows = (iota(128, 16, 0) // 8 == iota(128, 16, 1)).astype(F32)
    cols = (iota(16, 128, 1) // 8 == iota(16, 128, 0)).astype(F32)
    point = pw_ref[...]
    for ref, matrix in ((forward_ref, point.T), (back_ref, point)):
        wide = jnp.where(same_y, exact_dot(exact_dot(rows, matrix), cols), 0.0)
        upper, lower = split(wide)
        ref[...] = side_by_side([upper, lower, upper])


def iota(rows, cols, axis):
    return lax.broadcasted_iota(jnp.int32, (rows, cols), axis)


def column_bands(v_ref, q_ref, half):
    value = v_ref[:, half].reshape(256, 128)
    return lax.dot_general(
        value.T, q_ref[...], (((1,), (0,)), ((), ())), precision=HIGHEST,
        preferred_element_type=F32,
    )


def column_changes(d_scr, q_ref, o_ref):
    for half in range(2):
        value = lax.dot_general(
            q_ref[...], d_scr[half * 128 : (half + 1) * 128, :], (((1,), (1,)), ((), ())),
            precision=HIGHEST, preferred_element_type=F32,
        )
        o_ref[:, half] = value.reshape(32, 8, 128)


def mix_kernel(v_ref, q_ref, w_ref, o_ref, y_ref, d_scr):
    for half in range(2):
        y_ref[half * 128 : (half + 1) * 128, :] = column_bands(v_ref, q_ref, half)

    def body(o, carry):
        total = -y_ref[pl.ds(pl.multiple_of(o * 16, 16), 16), :]
        for i in range(16):
            total = total + y_ref[i * 16 : (i + 1) * 16, :] * w_ref[pl.ds(i * 16 + o, 1), :]
        d_scr[pl.ds(pl.multiple_of(o * 16, 16), 16), :] = total
        return carry

    lax.fori_loop(0, 16, body, 0)
    column_changes(d_scr, q_ref, o_ref)


def grad_bands_kernel(v_ref, q_ref, y_ref, b_ref, g_ref, p_ref, g_scr):
    for half in range(2):
        b_ref[half * 128 : (half + 1) * 128, :] = column_bands(v_ref, q_ref, half)

    def body(i, carry):
        flow = y_ref[pl.ds(pl.multiple_of(i * 16, 16), 16), :]
        for o in range(16):
            grad = b_ref[o * 16 : (o + 1) * 16, :]
            g_scr[pl.ds(i * 16 + o, 1), :] = jnp.sum(flow * grad, axis=0, keepdims=True)
        return carry

    lax.fori_loop(0, 16, body, 0)
    lane = lax.broadcasted_iota(jnp.int32, (8, 128), 1)
    for group in range(8):
        packed = g_scr[group * 32 : group * 32 + 8, :]
        for k in range(1, 4):
            rows = g_scr[group * 32 + k * 8 : group * 32 + k * 8 + 8, :]
            packed = jnp.where(lane // 32 == k, pltpu.roll(rows, 32 * k, 1), packed)
        for copy in range(group // 4, 8, 2):
            g_ref[copy, group % 4] = packed
    first = v_ref[0, 0, 7:8, :]
    second = v_ref[0, 1, 7:8, :]
    for slab in range(1, 32):
        first = first + v_ref[slab, 0, 7:8, :]
        second = second + v_ref[slab, 1, 7:8, :]
    p_ref[...] = jnp.zeros((8, 128), F32)
    p_ref[0:1, :] = first
    p_ref[1:2, :] = second


def mix_grad_kernel(b_ref, q_ref, w_ref, bias_ref, o_ref, d_scr):
    def body(i, carry):
        total = -b_ref[pl.ds(pl.multiple_of(i * 16, 16), 16), :]
        for o in range(16):
            total = total + b_ref[o * 16 : (o + 1) * 16, :] * w_ref[pl.ds(i * 16 + o, 1), :]
        d_scr[pl.ds(pl.multiple_of(i * 16, 16), 16), :] = total
        return carry

    lax.fori_loop(0, 16, body, 0)
    column_changes(d_scr, q_ref, o_ref)
    for slab in range(32):
        o_ref[slab, 0, 7:8, :] = bias_ref[0:1, :]


def join_kernel(v_ref, g_ref, o_ref):
    for quarter in range(4):
        total = g_ref[0, quarter]
        for i in range(1, 8):
            total = total + g_ref[i, quarter]
        total = total * (1.0 / math.sqrt(128.0))
        for slab in range(8 * quarter, 8 * quarter + 8):
            o_ref[slab, 0:2] = v_ref[slab]
            o_ref[slab, 2] = total


def spread_body(v_ref, l_scr, s_ref):
    def lift(mode, carry):
        for half in range(2):
            low = [v_ref[(mode + 16 - d) % 16, half] for d in range(4)]
            high = [v_ref[16 + (mode + 16 - d) % 16, half] for d in range(4)]
            for p in range(2):
                pairs = [(LOW_PASS[2 * d + p], low[d]) for d in range(4)]
                pairs += [(HIGH_PASS[2 * d + p], high[d]) for d in range(4)]
                l_scr[2 * mode + p, half] = gather_sum(pairs)
        return carry

    lax.fori_loop(0, 16, lift, 0)

    def send(i, carry):
        for half in range(2):
            s_ref[i, half, 64:72, :] = jnp.zeros((8, 128), F32)
            for a in range(10):
                s_ref[i, half, 7 * a : 7 * a + 8, :] = l_scr[(4 * i + 26 + a) % 32, half]
        return carry

    lax.fori_loop(0, 8, send, 0)


def spread_kernel(v_ref, s_ref, l_scr):
    spread_body(v_ref, l_scr, s_ref)


def spread_grad_kernel(v_ref, s_ref, bias_ref, l_scr):
    spread_body(v_ref, l_scr, s_ref)
    bias = v_ref[0, 0, 7:8, :]
    for slab in range(1, 32):
        bias = bias + v_ref[slab, 0, 7:8, :]
    bias_ref[...] = jnp.broadcast_to(bias, (8, 128))


def point_mix(w_ref, first, second):
    high, low = split(side_by_side([first, second]))
    return dot(w_ref[...], jnp.concatenate([high, high, low], axis=0)), high, low


def centre_kernel(
    r_ref, flow_hbm, cot_hbm, w_ref, bias_ref, down_ref, up_ref, out_hbm, g_hbm, s_ref,
    f_scr, c_scr, v_scr, g_scr, d_scr, p_scr, sum_scr, pt_scr, sems,
):
    load_flow = pltpu.make_async_copy(flow_hbm, f_scr, sems.at[0])
    load_cot = pltpu.make_async_copy(cot_hbm, c_scr, sems.at[1])
    load_flow.start()
    load_cot.start()
    unpack_planes(r_ref, d_scr)
    sum_scr[...] = jnp.zeros((128, 128), F32)
    pt_scr[...] = jnp.zeros((128, 128), F32)
    load_flow.wait()
    for pair in range(8):
        change = lift_pair(d_scr, pair, up_ref)
        for k in range(2):
            c = 2 * pair + k
            v_scr[c] = f_scr[c] + (change[:, 128 * k : 128 * k + 128] + bias_ref[c])
    load_cot.wait()
    stores = []
    for chunk in range(4):

        def body(step, carry):
            start = pl.multiple_of((chunk * 4 + step) * 16, 16)
            spans = [pl.ds(start, 8), pl.ds(pl.multiple_of(start + 8, 8), 8)]
            fields = [f_scr[:, span, :].reshape(128, 128) for span in spans]
            mixed, f_high, f_low = point_mix(w_ref, fields[0], fields[1])
            grads = []
            for k in range(2):
                value = v_scr[:, spans[k], :].reshape(128, 128) + mixed[:, 128 * k : 128 * k + 128]
                square = value * value
                tangent = jnp.tanh(value * (GELU_SCALE + (GELU_SCALE * GELU_CUBE) * square))
                half_up = 0.5 + 0.5 * tangent
                v_scr[:, spans[k], :] = (value * half_up).reshape(16, 8, 128)
                bend = value * ((0.5 * GELU_SCALE) + (1.5 * GELU_SCALE * GELU_CUBE) * square)
                slope = half_up + bend * (1.0 - tangent * tangent)
                grad = c_scr[:, spans[k], :].reshape(128, 128) * slope
                g_scr[:, spans[k], :] = grad.reshape(16, 8, 128)
                grads.append(grad)
            sum_scr[...] += grads[0] + grads[1]
            g_high, g_low = split(side_by_side(grads))
            pt_scr[...] += lax.dot_general(
                side_by_side([f_high, f_low, f_high]), side_by_side([g_high, g_high, g_low]),
                (((1,), (1,)), ((), ())), preferred_element_type=F32,
            )
            return carry

        lax.fori_loop(0, 4, body, 0, unroll=True)
        part = pl.ds(chunk * 64, 64)
        for k, (scr, hbm) in enumerate(((v_scr, out_hbm), (g_scr, g_hbm))):
            store = pltpu.make_async_copy(
                scr.at[:, part], hbm.at[:, part], sems.at[2 + 2 * chunk + k]
            )
            store.start()
            stores.append(store)
    for pair in range(8):
        analyse_pair(g_scr, pair, down_ref, p_scr)
    pack_planes(p_scr, s_ref)
    same_y = iota(128, 128, 0) % 8 == iota(128, 128, 1) % 8
    gather = (iota(16, 128, 1) // 8 == iota(16, 128, 0)).astype(F32)
    fold = (iota(128, 128, 0) // 8 == iota(128, 128, 1) % 16).astype(F32)
    wide = exact_dot(exact_dot(gather, jnp.where(same_y, pt_scr[...], 0.0)), fold)
    lane, row = iota(16, 128, 1), iota(16, 128, 0)
    wide = jnp.where(lane // 16 == row % 8, wide, 0.0)
    first = jnp.sum(wide[0:8], axis=0, keepdims=True)
    second = jnp.sum(wide[8:16], axis=0, keepdims=True)
    totals = jnp.sum(exact_dot(gather, sum_scr[...]), axis=1, keepdims=True)
    bias_row = jnp.sum(jnp.where(lane == row, totals, 0.0), axis=0, keepdims=True)
    for group in range(8):
        s_ref[group, 0, 70:71, :] = first
        s_ref[group, 0, 71:72, :] = second
        s_ref[group, 1, 70:71, :] = bias_row
    for store in stores:
        store.wait()


def finish_kernel(r_ref, g_hbm, w_ref, up_ref, out_hbm, g_scr, v_scr, d_scr, sems):
    load = pltpu.make_async_copy(g_hbm, g_scr, sems.at[0])
    load.start()
    unpack_planes(r_ref, d_scr)
    load.wait()
    for pair in range(8):
        change = lift_pair(d_scr, pair, up_ref)
        for k in range(2):
            v_scr[2 * pair + k] = g_scr[2 * pair + k] + change[:, 128 * k : 128 * k + 128]
    stores = []
    for chunk in range(4):

        def body(step, carry):
            start = pl.multiple_of((chunk * 4 + step) * 16, 16)
            spans = [pl.ds(start, 8), pl.ds(pl.multiple_of(start + 8, 8), 8)]
            fields = [g_scr[:, span, :].reshape(128, 128) for span in spans]
            mixed = point_mix(w_ref, fields[0], fields[1])[0]
            for k in range(2):
                value = v_scr[:, spans[k], :].reshape(128, 128) + mixed[:, 128 * k : 128 * k + 128]
                v_scr[:, spans[k], :] = value.reshape(16, 8, 128)
            return carry

        lax.fori_loop(0, 4, body, 0, unroll=True)
        part = pl.ds(chunk * 64, 64)
        store = pltpu.make_async_copy(v_scr.at[:, part], out_hbm.at[:, part], sems.at[1 + chunk])
        store.start()
        stores.append(store)
    for store in stores:
        store.wait()


def modes_place_kernel(m_ref, o_ref):
    for high in range(2):
        for right in range(2):
            rows = swap_blocks([m_ref[high * 16 + right * 8 + m, 2] for m in range(8)])
            for k in range(4):
                for up in range(2):
                    o_ref[
                        high + 2 * up, k * 8 : k * 8 + 8, right * 128 : (right + 1) * 128
                    ] = rows[2 * k + up]


def gather_kernel(index_ref, *refs):
    parts, out_hbm, sems = refs[:8], refs[8], refs[9]
    copies = []
    for flip in range(2):
        for shift in range(4):
            core = (index_ref[1] + flip) % 2
            owner = core * 4 + (index_ref[0] // 8 + 4 - shift) % 4
            to = out_hbm.at[:, pl.ds(pl.multiple_of(owner * 32, 32), 32), :]
            k = flip * 4 + shift
            copies.append(pltpu.make_async_copy(parts[k], to, sems.at[k]))
    for copy in copies:
        copy.start()
    for copy in copies:
        copy.wait()


def call(kernel, ins, outs, scratch=(), sems=0, mib=8):
    spaces = {"v": pltpu.VMEM, "s": pltpu.SMEM, "a": pltpu.HBM}
    structs = [jax.ShapeDtypeStruct(o[0], o[2] if len(o) > 2 else F32) for o in outs]
    scratches = [pltpu.VMEM(shape, F32) for shape in scratch]
    if sems:
        scratches.append(pltpu.SemaphoreType.DMA((sems,)))
    return pl.pallas_call(
        kernel,
        out_shape=structs,
        in_specs=[pl.BlockSpec(memory_space=spaces[k]) for k in ins],
        out_specs=[pl.BlockSpec(memory_space=spaces[o[1]]) for o in outs],
        scratch_shapes=scratches,
        compiler_params=pltpu.CompilerParams(vmem_limit_bytes=mib * 1024 * 1024),
    )


def local(flow_field, cotangent, mode_weights, point_weights, point_bias):
    swap_x = lambda v: lax.all_to_all(v, "gx", 0, 0, tiled=False)
    swap_y = lambda v: lax.all_to_all(v, "gy", 0, 0, tiled=False)
    packed = ((8, 2, 72, 128), "v")
    coefs = ((32, 2, 8, 128), "v")
    square = ((256, 128), "v")
    row = ((8, 128), "v")
    cells = (16, 256, 128)
    parts = (16, 80, 128)
    rows3 = [(32, 2, 8, 128)]
    table = jnp.asarray(y_table())
    down, up = (jnp.asarray(t) for t in cell_tables())
    slab = lax.axis_index("gy").astype(jnp.int32).reshape(1)
    flow_cells = flow_field.reshape(cells)
    kron = ((128, 384), "v", BF16)

    weights, mix_forward, mix_back = call(weights_kernel, "svv", [square, kron, kron])(
        slab, mode_weights.reshape(4, 256, 256), point_weights
    )
    (sent,) = call(analyse_kernel, "av", [packed], [cells, parts], 4, 58)(flow_cells, down)
    (got,) = call(rows_kernel, "v", [coefs], rows3)(swap_x(sent))
    back, bands_flow = call(mix_kernel, "vvv", [coefs, square], [(256, 128)])(
        swap_y(got), table, weights
    )
    (spread,) = call(spread_kernel, "v", [packed], rows3)(swap_y(back))
    output_field, grads, sent = call(
        centre_kernel, "vaavsvv", [(cells, "a"), (cells, "a"), packed],
        [cells] * 4 + [parts] * 2 + [(128, 128)] * 2, 10, 52,
    )(
        swap_x(spread), flow_cells, cotangent.reshape(cells), mix_forward, point_bias, down, up
    )
    got, bias_part = call(rows_grad_kernel, "v", [coefs, row], rows3)(swap_x(sent))
    bands_grad, mode_part, point_total = call(
        grad_bands_kernel, "vvv", [square, ((8, 4, 8, 128), "v"), row], [(256, 128)]
    )(swap_y(got), table, bands_flow)
    (back,) = call(mix_grad_kernel, "vvvv", [coefs], [(256, 128)])(
        bands_grad, table, weights, bias_part
    )
    (joined,) = call(join_kernel, "vv", [((32, 3, 8, 128), "v")])(back, swap_x(mode_part))
    joined = swap_y(joined)
    spread, bias_total = call(spread_grad_kernel, "v", [packed, row], rows3)(joined)
    (grad_field,) = call(
        finish_kernel, "vavv", [(cells, "a")], [cells] * 2 + [parts], 5, 52
    )(swap_x(spread), grads, mix_back, up)
    (placed,) = call(modes_place_kernel, "v", [((4, 32, 256), "v")])(joined)
    parts = [placed]
    for flip, shift in [(f, k) for f in range(2) for k in range(4)][1:]:
        routes = [
            (i * 32 + j, (i ^ flip) * 32 + (j + 8 * shift) % 32)
            for i in range(8)
            for j in range(32)
        ]
        parts.append(lax.ppermute(placed, ("gx", "gy"), routes))
    place, grad_field = lax.optimization_barrier(
        (jnp.stack([lax.axis_index("gy"), lax.axis_index("gx")]).astype(jnp.int32), grad_field)
    )
    (modes,) = call(gather_kernel, "s" + "a" * 8, [((4, 256, 256), "a")], (), 8)(place, *parts)

    cell_count = flow_field.shape[3] * 256 * 256
    return (
        output_field.reshape(flow_field.shape),
        grad_field.reshape(flow_field.shape),
        modes.reshape(4, 16, 16, 256),
        point_total[0:2].reshape(16, 16) / math.sqrt(cell_count),
        bias_total[0, :16] / math.sqrt(cell_count),
    )


def solution(mesh):
    in_specs = (P(None, "gx", "gy", None), P(None, "gx", "gy", None), P(), P(), P())
    out_specs = (P(None, "gx", "gy", None), P(None, "gx", "gy", None), P(), P(), P())
    return jax.shard_map(local, mesh=mesh, in_specs=in_specs, out_specs=out_specs, check_vma=False)
```

```python
import math

import jax
import jax.numpy as jnp
import ml_dtypes
import numpy as np
from jax import lax
from jax.experimental import pallas as pl
from jax.experimental.pallas import tpu as pltpu
from jax.sharding import PartitionSpec as P

LOW_PASS = [
    0.23037781330885523,
    0.7148465705525415,
    0.6308807679295904,
    -0.02798376941698385,
    -0.18703481171888114,
    0.030841381835986965,
    0.032883011666982945,
    -0.010597401784997278,
]
HIGH_PASS = [(-1) ** position * LOW_PASS[7 - position] for position in range(8)]
GELU_SCALE = 0.7978845608028654
GELU_CUBE = 0.044715


def triple_low():
    taps = np.zeros(50)
    for p, hp in enumerate(LOW_PASS):
        for q, hq in enumerate(LOW_PASS):
            for r, hr in enumerate(LOW_PASS):
                taps[p + 2 * q + 4 * r] += hp * hq * hr
    return [float(t) for t in taps]


TRIPLE = triple_low()
HIGHEST = lax.Precision.HIGHEST
F32 = jnp.float32
BF16 = jnp.bfloat16


def cell_tables():
    table = np.zeros((80, 256))
    for a in range(10):
        for b in range(7):
            for x in range(32):
                for y in range(8):
                    at_x, at_y = x + 48 - 8 * a, y + 48 - 8 * b
                    if 0 <= at_x < 50 and 0 <= at_y < 50:
                        table[a * 7 + b, x * 8 + y] = TRIPLE[at_x] * TRIPLE[at_y]
    table = table.astype(np.float32)
    high = table.astype(ml_dtypes.bfloat16)
    low = (table - high.astype(np.float32)).astype(ml_dtypes.bfloat16)
    down = np.concatenate([high, low])
    pad = np.zeros((256, 16), ml_dtypes.bfloat16)
    up = np.concatenate([high.T, low.T, high.T, pad], 1)
    return down, up


def y_table():
    table = np.zeros((32, 8, 128), np.float32)
    for slab in range(32):
        for b in range(7):
            ky = (slab - 6 + b) % 32
            for mode in range(16):
                at = (ky - 2 * mode) % 32
                if at < 8:
                    table[slab, b, mode] = LOW_PASS[at]
                    table[slab, b, 16 + mode] = HIGH_PASS[at]
    return table.reshape(256, 128)


def gather_sum(pairs):
    total = None
    for weight, value in pairs:
        term = value * weight
        total = term if total is None else total + term
    return total


def swap_blocks(rows):
    lane = lax.broadcasted_iota(jnp.int32, (8, 128), 1)
    rows = [rows[0]] + [pltpu.roll(rows[c], 16 * c, 1) for c in range(1, 8)]
    for bit in range(3):
        step = 1 << bit
        chosen = (lane & (16 * step)) != 0
        rows = [jnp.where(chosen, rows[(m + step) % 8], rows[m]) for m in range(8)]
    rows = [rows[(8 - k) % 8] for k in range(8)]
    return [rows[0]] + [pltpu.roll(rows[k], 128 - 16 * k, 1) for k in range(1, 8)]


def split(value):
    high = value.astype(BF16)
    return high, (value - high.astype(F32)).astype(BF16)


def dot(left, right):
    return lax.dot_general(left, right, (((1,), (0,)), ((), ())), preferred_element_type=F32)


def exact_dot(left, right):
    return lax.dot_general(
        left, right, (((1,), (0,)), ((), ())), precision=HIGHEST, preferred_element_type=F32
    )


def side_by_side(values):
    return jnp.concatenate(values, axis=1)


def analyse_pair(field, pair, down_ref, p_scr):
    high, low = split(side_by_side([field[2 * pair], field[2 * pair + 1]]))
    wide = dot(down_ref[...], high)
    total = wide[0:80] + wide[80:160] + dot(down_ref[0:80, :], low)
    p_scr[2 * pair] = total[:, 0:128]
    p_scr[2 * pair + 1] = total[:, 128:256]


def pack_planes(p_scr, s_ref, half):
    for octet in range(9):
        at = slice(octet * 8, octet * 8 + 8)
        rows = swap_blocks([p_scr[half * 8 + c, at, :] for c in range(8)])
        for group in range(8):
            s_ref[group, half, at, :] = rows[group]


def unpack_planes(r_ref, d_scr, half):
    for octet in range(9):
        at = slice(octet * 8, octet * 8 + 8)
        rows = swap_blocks([r_ref[group, half, at, :] for group in range(8)])
        for c in range(8):
            d_scr[half * 8 + c, at, :] = rows[c]
    for c in range(8):
        d_scr[half * 8 + c, 72:80, :] = jnp.zeros((8, 128), F32)


def lift_pair(d_scr, pair, up_ref):
    high, low = split(side_by_side([d_scr[2 * pair], d_scr[2 * pair + 1]]))
    stacked = jnp.concatenate([high, high, low, jnp.zeros((16, 256), BF16)], axis=0)
    return dot(up_ref[...], stacked)


def analyse_kernel(flow_hbm, down_ref, s_ref, f_scr, p_scr, sems):
    copies = [
        pltpu.make_async_copy(flow_hbm.at[pl.ds(4 * k, 4)], f_scr.at[pl.ds(4 * k, 4)], sems.at[k])
        for k in range(4)
    ]
    for copy in copies:
        copy.start()
    for pair in range(8):
        if pair % 2 == 0:
            copies[pair // 2].wait()
        analyse_pair(f_scr, pair, down_ref, p_scr)
        if pair % 4 == 3:
            pack_planes(p_scr, s_ref, pair // 4)


def rows_body(r_ref, l_scr, v_ref):
    def collect(q, carry):
        one = (q + 1) % 8
        two = (q + 2) % 8
        for t in range(4):
            for half in range(2):
                total = r_ref[q, half, 7 * (6 + t) : 7 * (6 + t) + 8, :]
                total = total + r_ref[one, half, 7 * (2 + t) : 7 * (2 + t) + 8, :]
                if t >= 2:
                    total = total + r_ref[two, half, 7 * (t - 2) : 7 * (t - 2) + 8, :]
                l_scr[q * 4 + t, half] = total
        return carry

    lax.fori_loop(0, 8, collect, 0)

    def bands(mode, carry):
        for half in range(2):
            parts = [l_scr[(2 * mode + n) % 32, half] for n in range(8)]
            v_ref[mode, half] = gather_sum(list(zip(LOW_PASS, parts)))
            v_ref[mode + 16, half] = gather_sum(list(zip(HIGH_PASS, parts)))
        return carry

    lax.fori_loop(0, 16, bands, 0)


def rows_kernel(r_ref, v_ref, l_scr):
    rows_body(r_ref, l_scr, v_ref)


def rows_grad_kernel(r_ref, v_ref, bias_ref, l_scr):
    rows_body(r_ref, l_scr, v_ref)
    first = r_ref[0, 0, 70:71, :]
    second = r_ref[0, 0, 71:72, :]
    bias = r_ref[0, 1, 70:71, :]
    for i in range(1, 8):
        first = first + r_ref[i, 0, 70:71, :]
        second = second + r_ref[i, 0, 71:72, :]
        bias = bias + r_ref[i, 1, 70:71, :]

    def put(coef, carry):
        v_ref[coef, 0, 7:8, :] = first
        v_ref[coef, 1, 7:8, :] = second
        return carry

    lax.fori_loop(0, 32, put, 0)
    bias_ref[...] = jnp.broadcast_to(bias, (8, 128))


def weights_kernel(index_ref, w_ref, pw_ref, o_ref, forward_ref, back_ref):
    slab = index_ref[0]
    high = slab // 16
    mode = slab % 16
    right = mode // 8
    shift = (8 - mode % 8) * 16
    lane = lax.broadcasted_iota(jnp.int32, (256, 128), 1)
    low_y = jnp.where(right == 0, w_ref[high, :, 0:128], w_ref[high, :, 128:256])
    high_y = jnp.where(right == 0, w_ref[high + 2, :, 0:128], w_ref[high + 2, :, 128:256])
    low_y = pltpu.roll(low_y, shift % 128, 1)
    high_y = pltpu.roll(high_y, (shift + 16) % 128, 1)
    o_ref[...] = jnp.where(lane < 16, low_y, jnp.where(lane < 32, high_y, 0.0))
    same_y = iota(128, 128, 0) % 8 == iota(128, 128, 1) % 8
    rows = (iota(128, 16, 0) // 8 == iota(128, 16, 1)).astype(F32)
    cols = (iota(16, 128, 1) // 8 == iota(16, 128, 0)).astype(F32)
    point = pw_ref[...]
    for ref, matrix in ((forward_ref, point.T), (back_ref, point)):
        wide = jnp.where(same_y, exact_dot(exact_dot(rows, matrix), cols), 0.0)
        upper, lower = split(wide)
        ref[...] = side_by_side([upper, lower, upper])


def iota(rows, cols, axis):
    return lax.broadcasted_iota(jnp.int32, (rows, cols), axis)


def column_bands(v_ref, q_ref, half):
    value = v_ref[:, half].reshape(256, 128)
    return lax.dot_general(
        value.T, q_ref[...], (((1,), (0,)), ((), ())), precision=HIGHEST,
        preferred_element_type=F32,
    )


def column_changes(d_scr, q_ref, o_ref):
    for half in range(2):
        value = lax.dot_general(
            q_ref[...], d_scr[half * 128 : (half + 1) * 128, :], (((1,), (1,)), ((), ())),
            precision=HIGHEST, preferred_element_type=F32,
        )
        o_ref[:, half] = value.reshape(32, 8, 128)


def mix_kernel(v_ref, q_ref, w_ref, o_ref, y_ref, d_scr):
    for half in range(2):
        y_ref[half * 128 : (half + 1) * 128, :] = column_bands(v_ref, q_ref, half)

    def body(o, carry):
        total = -y_ref[pl.ds(pl.multiple_of(o * 16, 16), 16), :]
        for i in range(16):
            total = total + y_ref[i * 16 : (i + 1) * 16, :] * w_ref[pl.ds(i * 16 + o, 1), :]
        d_scr[pl.ds(pl.multiple_of(o * 16, 16), 16), :] = total
        return carry

    lax.fori_loop(0, 16, body, 0)
    column_changes(d_scr, q_ref, o_ref)


def grad_bands_kernel(v_ref, q_ref, y_ref, b_ref, g_ref, p_ref, g_scr):
    for half in range(2):
        b_ref[half * 128 : (half + 1) * 128, :] = column_bands(v_ref, q_ref, half)

    def body(i, carry):
        flow = y_ref[pl.ds(pl.multiple_of(i * 16, 16), 16), :]
        for o in range(16):
            grad = b_ref[o * 16 : (o + 1) * 16, :]
            g_scr[pl.ds(i * 16 + o, 1), :] = jnp.sum(flow * grad, axis=0, keepdims=True)
        return carry

    lax.fori_loop(0, 16, body, 0)
    lane = lax.broadcasted_iota(jnp.int32, (8, 128), 1)
    for group in range(8):
        packed = g_scr[group * 32 : group * 32 + 8, :]
        for k in range(1, 4):
            rows = g_scr[group * 32 + k * 8 : group * 32 + k * 8 + 8, :]
            packed = jnp.where(lane // 32 == k, pltpu.roll(rows, 32 * k, 1), packed)
        for copy in range(group // 4, 8, 2):
            g_ref[copy, group % 4] = packed
    first = v_ref[0, 0, 7:8, :]
    second = v_ref[0, 1, 7:8, :]
    for slab in range(1, 32):
        first = first + v_ref[slab, 0, 7:8, :]
        second = second + v_ref[slab, 1, 7:8, :]
    p_ref[...] = jnp.zeros((8, 128), F32)
    p_ref[0:1, :] = first
    p_ref[1:2, :] = second


def mix_grad_kernel(b_ref, q_ref, w_ref, bias_ref, o_ref, d_scr):
    def body(i, carry):
        total = -b_ref[pl.ds(pl.multiple_of(i * 16, 16), 16), :]
        for o in range(16):
            total = total + b_ref[o * 16 : (o + 1) * 16, :] * w_ref[pl.ds(i * 16 + o, 1), :]
        d_scr[pl.ds(pl.multiple_of(i * 16, 16), 16), :] = total
        return carry

    lax.fori_loop(0, 16, body, 0)
    column_changes(d_scr, q_ref, o_ref)
    for slab in range(32):
        o_ref[slab, 0, 7:8, :] = bias_ref[0:1, :]


def join_kernel(v_ref, g_ref, o_ref):
    for quarter in range(4):
        total = g_ref[0, quarter]
        for i in range(1, 8):
            total = total + g_ref[i, quarter]
        total = total * (1.0 / math.sqrt(128.0))
        for slab in range(8 * quarter, 8 * quarter + 8):
            o_ref[slab, 0:2] = v_ref[slab]
            o_ref[slab, 2] = total


def spread_body(v_ref, l_scr, s_ref):
    def lift(mode, carry):
        for half in range(2):
            low = [v_ref[(mode + 16 - d) % 16, half] for d in range(4)]
            high = [v_ref[16 + (mode + 16 - d) % 16, half] for d in range(4)]
            for p in range(2):
                pairs = [(LOW_PASS[2 * d + p], low[d]) for d in range(4)]
                pairs += [(HIGH_PASS[2 * d + p], high[d]) for d in range(4)]
                l_scr[2 * mode + p, half] = gather_sum(pairs)
        return carry

    lax.fori_loop(0, 16, lift, 0)

    def send(i, carry):
        for half in range(2):
            s_ref[i, half, 64:72, :] = jnp.zeros((8, 128), F32)
            for a in range(10):
                s_ref[i, half, 7 * a : 7 * a + 8, :] = l_scr[(4 * i + 26 + a) % 32, half]
        return carry

    lax.fori_loop(0, 8, send, 0)


def spread_kernel(v_ref, s_ref, l_scr):
    spread_body(v_ref, l_scr, s_ref)


def spread_grad_kernel(v_ref, s_ref, bias_ref, l_scr):
    spread_body(v_ref, l_scr, s_ref)
    bias = v_ref[0, 0, 7:8, :]
    for slab in range(1, 32):
        bias = bias + v_ref[slab, 0, 7:8, :]
    bias_ref[...] = jnp.broadcast_to(bias, (8, 128))


def point_mix(w_ref, first, second):
    high, low = split(side_by_side([first, second]))
    return dot(w_ref[...], jnp.concatenate([high, high, low], axis=0)), high, low


def centre_kernel(
    r_ref, flow_hbm, cot_hbm, w_ref, bias_ref, down_ref, up_ref, out_hbm, g_hbm, s_ref,
    f_scr, c_scr, v_scr, g_scr, d_scr, p_scr, sum_scr, pt_scr, sems,
):
    load_flow = pltpu.make_async_copy(flow_hbm, f_scr, sems.at[0])
    load_cot = pltpu.make_async_copy(cot_hbm, c_scr, sems.at[1])
    load_flow.start()
    load_cot.start()
    unpack_planes(r_ref, d_scr, 0)
    sum_scr[...] = jnp.zeros((128, 128), F32)
    pt_scr[...] = jnp.zeros((128, 128), F32)
    load_flow.wait()
    for pair in range(8):
        if pair == 1:
            unpack_planes(r_ref, d_scr, 1)
        change = lift_pair(d_scr, pair, up_ref)
        for k in range(2):
            c = 2 * pair + k
            v_scr[c] = f_scr[c] + (change[:, 128 * k : 128 * k + 128] + bias_ref[c])
    load_cot.wait()
    stores = []
    for chunk in range(4):

        def body(step, carry):
            start = pl.multiple_of((chunk * 4 + step) * 16, 16)
            spans = [pl.ds(start, 8), pl.ds(pl.multiple_of(start + 8, 8), 8)]
            fields = [f_scr[:, span, :].reshape(128, 128) for span in spans]
            mixed, f_high, f_low = point_mix(w_ref, fields[0], fields[1])
            grads = []
            for k in range(2):
                value = v_scr[:, spans[k], :].reshape(128, 128) + mixed[:, 128 * k : 128 * k + 128]
                square = value * value
                tangent = jnp.tanh(value * (GELU_SCALE + (GELU_SCALE * GELU_CUBE) * square))
                half_up = 0.5 + 0.5 * tangent
                v_scr[:, spans[k], :] = (value * half_up).reshape(16, 8, 128)
                bend = value * ((0.5 * GELU_SCALE) + (1.5 * GELU_SCALE * GELU_CUBE) * square)
                slope = half_up + bend * (1.0 - tangent * tangent)
                grad = c_scr[:, spans[k], :].reshape(128, 128) * slope
                g_scr[:, spans[k], :] = grad.reshape(16, 8, 128)
                grads.append(grad)
            sum_scr[...] += grads[0] + grads[1]
            g_high, g_low = split(side_by_side(grads))
            pt_scr[...] += lax.dot_general(
                side_by_side([f_high, f_low, f_high]), side_by_side([g_high, g_high, g_low]),
                (((1,), (1,)), ((), ())), preferred_element_type=F32,
            )
            return carry

        lax.fori_loop(0, 4, body, 0, unroll=True)
        part = pl.ds(chunk * 64, 64)
        for k, (scr, hbm) in enumerate(((v_scr, out_hbm), (g_scr, g_hbm))):
            store = pltpu.make_async_copy(
                scr.at[:, part], hbm.at[:, part], sems.at[2 + 2 * chunk + k]
            )
            store.start()
            stores.append(store)
    for pair in range(8):
        analyse_pair(g_scr, pair, down_ref, p_scr)
        if pair % 4 == 3:
            pack_planes(p_scr, s_ref, pair // 4)
    same_y = iota(128, 128, 0) % 8 == iota(128, 128, 1) % 8
    gather = (iota(16, 128, 1) // 8 == iota(16, 128, 0)).astype(F32)
    fold = (iota(128, 128, 0) // 8 == iota(128, 128, 1) % 16).astype(F32)
    wide = exact_dot(exact_dot(gather, jnp.where(same_y, pt_scr[...], 0.0)), fold)
    lane, row = iota(16, 128, 1), iota(16, 128, 0)
    wide = jnp.where(lane // 16 == row % 8, wide, 0.0)
    first = jnp.sum(wide[0:8], axis=0, keepdims=True)
    second = jnp.sum(wide[8:16], axis=0, keepdims=True)
    totals = jnp.sum(exact_dot(gather, sum_scr[...]), axis=1, keepdims=True)
    bias_row = jnp.sum(jnp.where(lane == row, totals, 0.0), axis=0, keepdims=True)
    for group in range(8):
        s_ref[group, 0, 70:71, :] = first
        s_ref[group, 0, 71:72, :] = second
        s_ref[group, 1, 70:71, :] = bias_row
    for store in stores:
        store.wait()


def finish_kernel(r_ref, g_hbm, w_ref, up_ref, out_hbm, g_scr, v_scr, d_scr, sems):
    load = pltpu.make_async_copy(g_hbm, g_scr, sems.at[0])
    load.start()
    unpack_planes(r_ref, d_scr, 0)
    load.wait()
    for pair in range(8):
        if pair == 1:
            unpack_planes(r_ref, d_scr, 1)
        change = lift_pair(d_scr, pair, up_ref)
        for k in range(2):
            v_scr[2 * pair + k] = g_scr[2 * pair + k] + change[:, 128 * k : 128 * k + 128]
    stores = []
    for chunk in range(4):

        def body(step, carry):
            start = pl.multiple_of((chunk * 4 + step) * 16, 16)
            spans = [pl.ds(start, 8), pl.ds(pl.multiple_of(start + 8, 8), 8)]
            fields = [g_scr[:, span, :].reshape(128, 128) for span in spans]
            mixed = point_mix(w_ref, fields[0], fields[1])[0]
            for k in range(2):
                value = v_scr[:, spans[k], :].reshape(128, 128) + mixed[:, 128 * k : 128 * k + 128]
                v_scr[:, spans[k], :] = value.reshape(16, 8, 128)
            return carry

        lax.fori_loop(0, 4, body, 0, unroll=True)
        part = pl.ds(chunk * 64, 64)
        store = pltpu.make_async_copy(v_scr.at[:, part], out_hbm.at[:, part], sems.at[1 + chunk])
        store.start()
        stores.append(store)
    for store in stores:
        store.wait()


def modes_place_kernel(m_ref, o_ref):
    for high in range(2):
        for right in range(2):
            rows = swap_blocks([m_ref[high * 16 + right * 8 + m, 2] for m in range(8)])
            for k in range(4):
                for up in range(2):
                    o_ref[
                        high + 2 * up, k * 8 : k * 8 + 8, right * 128 : (right + 1) * 128
                    ] = rows[2 * k + up]


def gather_kernel(index_ref, *refs):
    parts, out_hbm, sems = refs[:8], refs[8], refs[9]
    copies = []
    for flip in range(2):
        for shift in range(4):
            core = (index_ref[1] + flip) % 2
            owner = core * 4 + (index_ref[0] // 8 + 4 - shift) % 4
            to = out_hbm.at[:, pl.ds(pl.multiple_of(owner * 32, 32), 32), :]
            k = flip * 4 + shift
            copies.append(pltpu.make_async_copy(parts[k], to, sems.at[k]))
    for copy in copies:
        copy.start()
    for copy in copies:
        copy.wait()


def call(kernel, ins, outs, scratch=(), sems=0, mib=8):
    spaces = {"v": pltpu.VMEM, "s": pltpu.SMEM, "a": pltpu.HBM}
    structs = [jax.ShapeDtypeStruct(o[0], o[2] if len(o) > 2 else F32) for o in outs]
    scratches = [pltpu.VMEM(shape, F32) for shape in scratch]
    if sems:
        scratches.append(pltpu.SemaphoreType.DMA((sems,)))
    return pl.pallas_call(
        kernel,
        out_shape=structs,
        in_specs=[pl.BlockSpec(memory_space=spaces[k]) for k in ins],
        out_specs=[pl.BlockSpec(memory_space=spaces[o[1]]) for o in outs],
        scratch_shapes=scratches,
        compiler_params=pltpu.CompilerParams(vmem_limit_bytes=mib * 1024 * 1024),
    )


def local(flow_field, cotangent, mode_weights, point_weights, point_bias):
    swap_x = lambda v: lax.all_to_all(v, "gx", 0, 0, tiled=False)
    swap_y = lambda v: lax.all_to_all(v, "gy", 0, 0, tiled=False)
    packed = ((8, 2, 72, 128), "v")
    coefs = ((32, 2, 8, 128), "v")
    square = ((256, 128), "v")
    row = ((8, 128), "v")
    cells = (16, 256, 128)
    parts = (16, 80, 128)
    rows3 = [(32, 2, 8, 128)]
    table = jnp.asarray(y_table())
    down, up = (jnp.asarray(t) for t in cell_tables())
    slab = lax.axis_index("gy").astype(jnp.int32).reshape(1)
    flow_cells = flow_field.reshape(cells)
    kron = ((128, 384), "v", BF16)

    weights, mix_forward, mix_back = call(weights_kernel, "svv", [square, kron, kron])(
        slab, mode_weights.reshape(4, 256, 256), point_weights
    )
    (sent,) = call(analyse_kernel, "av", [packed], [cells, parts], 4, 52)(flow_cells, down)
    (got,) = call(rows_kernel, "v", [coefs], rows3)(swap_x(sent))
    back, bands_flow = call(mix_kernel, "vvv", [coefs, square], [(256, 128)])(
        swap_y(got), table, weights
    )
    (spread,) = call(spread_kernel, "v", [packed], rows3)(swap_y(back))
    output_field, grads, sent = call(
        centre_kernel, "vaavsvv", [(cells, "a"), (cells, "a"), packed],
        [cells] * 4 + [parts] * 2 + [(128, 128)] * 2, 10, 52,
    )(
        swap_x(spread), flow_cells, cotangent.reshape(cells), mix_forward, point_bias, down, up
    )
    got, bias_part = call(rows_grad_kernel, "v", [coefs, row], rows3)(swap_x(sent))
    bands_grad, mode_part, point_total = call(
        grad_bands_kernel, "vvv", [square, ((8, 4, 8, 128), "v"), row], [(256, 128)]
    )(swap_y(got), table, bands_flow)
    (back,) = call(mix_grad_kernel, "vvvv", [coefs], [(256, 128)])(
        bands_grad, table, weights, bias_part
    )
    (joined,) = call(join_kernel, "vv", [((32, 3, 8, 128), "v")])(back, swap_x(mode_part))
    joined = swap_y(joined)
    spread, bias_total = call(spread_grad_kernel, "v", [packed, row], rows3)(joined)
    (grad_field,) = call(
        finish_kernel, "vavv", [(cells, "a")], [cells] * 2 + [parts], 5, 52
    )(swap_x(spread), grads, mix_back, up)
    (placed,) = call(modes_place_kernel, "v", [((4, 32, 256), "v")])(joined)
    parts = [placed]
    for flip, shift in [(f, k) for f in range(2) for k in range(4)][1:]:
        routes = [
            (i * 32 + j, (i ^ flip) * 32 + (j + 8 * shift) % 32)
            for i in range(8)
            for j in range(32)
        ]
        parts.append(lax.ppermute(placed, ("gx", "gy"), routes))
    place, grad_field = lax.optimization_barrier(
        (jnp.stack([lax.axis_index("gy"), lax.axis_index("gx")]).astype(jnp.int32), grad_field)
    )
    (modes,) = call(gather_kernel, "s" + "a" * 8, [((4, 256, 256), "a")], (), 8)(place, *parts)

    cell_count = flow_field.shape[3] * 256 * 256
    return (
        output_field.reshape(flow_field.shape),
        grad_field.reshape(flow_field.shape),
        modes.reshape(4, 16, 16, 256),
        point_total[0:2].reshape(16, 16) / math.sqrt(cell_count),
        bias_total[0, :16] / math.sqrt(cell_count),
    )


def solution(mesh):
    in_specs = (P(None, "gx", "gy", None), P(None, "gx", "gy", None), P(), P(), P())
    out_specs = (P(None, "gx", "gy", None), P(None, "gx", "gy", None), P(), P(), P())
    return jax.shard_map(local, mesh=mesh, in_specs=in_specs, out_specs=out_specs, check_vma=False)
```

```python
import math

import jax
import jax.numpy as jnp
import ml_dtypes
import numpy as np
from jax import lax
from jax.experimental import pallas as pl
from jax.experimental.pallas import tpu as pltpu
from jax.sharding import PartitionSpec as P

LOW_PASS = [
    0.23037781330885523,
    0.7148465705525415,
    0.6308807679295904,
    -0.02798376941698385,
    -0.18703481171888114,
    0.030841381835986965,
    0.032883011666982945,
    -0.010597401784997278,
]
HIGH_PASS = [(-1) ** position * LOW_PASS[7 - position] for position in range(8)]
GELU_SCALE = 0.7978845608028654
GELU_CUBE = 0.044715


def triple_low():
    taps = np.zeros(50)
    for p, hp in enumerate(LOW_PASS):
        for q, hq in enumerate(LOW_PASS):
            for r, hr in enumerate(LOW_PASS):
                taps[p + 2 * q + 4 * r] += hp * hq * hr
    return [float(t) for t in taps]


TRIPLE = triple_low()
HIGHEST = lax.Precision.HIGHEST
F32 = jnp.float32
BF16 = jnp.bfloat16
MODE_ROUTES = [(1, 0), (0, 1), (0, 2), (1, 2), (0, 3), (1, 3), (1, 1)]


def cell_tables():
    table = np.zeros((80, 256))
    for a in range(10):
        for b in range(7):
            for x in range(32):
                for y in range(8):
                    at_x, at_y = x + 48 - 8 * a, y + 48 - 8 * b
                    if 0 <= at_x < 50 and 0 <= at_y < 50:
                        table[a * 7 + b, x * 8 + y] = TRIPLE[at_x] * TRIPLE[at_y]
    table = table.astype(np.float32)
    high = table.astype(ml_dtypes.bfloat16)
    low = (table - high.astype(np.float32)).astype(ml_dtypes.bfloat16)
    down = np.concatenate([high, low])
    pad = np.zeros((256, 16), ml_dtypes.bfloat16)
    up = np.concatenate([high.T, low.T, high.T, pad], 1)
    return down, up


def y_table():
    table = np.zeros((32, 8, 128), np.float32)
    for slab in range(32):
        for b in range(7):
            ky = (slab - 6 + b) % 32
            for mode in range(16):
                at = (ky - 2 * mode) % 32
                if at < 8:
                    table[slab, b, mode] = LOW_PASS[at]
                    table[slab, b, 16 + mode] = HIGH_PASS[at]
    return table.reshape(256, 128)


def gather_sum(pairs):
    total = None
    for weight, value in pairs:
        term = value * weight
        total = term if total is None else total + term
    return total


def swap_blocks(rows):
    lane = lax.broadcasted_iota(jnp.int32, (8, 128), 1)
    rows = [rows[0]] + [pltpu.roll(rows[c], 16 * c, 1) for c in range(1, 8)]
    for bit in range(3):
        step = 1 << bit
        chosen = (lane & (16 * step)) != 0
        rows = [jnp.where(chosen, rows[(m + step) % 8], rows[m]) for m in range(8)]
    rows = [rows[(8 - k) % 8] for k in range(8)]
    return [rows[0]] + [pltpu.roll(rows[k], 128 - 16 * k, 1) for k in range(1, 8)]


def split(value):
    high = value.astype(BF16)
    return high, (value - high.astype(F32)).astype(BF16)


def dot(left, right):
    return lax.dot_general(left, right, (((1,), (0,)), ((), ())), preferred_element_type=F32)


def exact_dot(left, right):
    return lax.dot_general(
        left, right, (((1,), (0,)), ((), ())), precision=HIGHEST, preferred_element_type=F32
    )


def side_by_side(values):
    return jnp.concatenate(values, axis=1)


def analyse_pair(field, pair, down_ref, p_scr):
    high, low = split(side_by_side([field[2 * pair], field[2 * pair + 1]]))
    wide = dot(down_ref[...], high)
    total = wide[0:80] + wide[80:160] + dot(down_ref[0:80, :], low)
    p_scr[2 * pair] = total[:, 0:128]
    p_scr[2 * pair + 1] = total[:, 128:256]


def pack_planes(p_scr, s_ref, half):
    for octet in range(9):
        at = slice(octet * 8, octet * 8 + 8)
        rows = swap_blocks([p_scr[half * 8 + c, at, :] for c in range(8)])
        for group in range(8):
            s_ref[group, half, at, :] = rows[group]


def unpack_planes(r_ref, d_scr, half):
    for octet in range(9):
        at = slice(octet * 8, octet * 8 + 8)
        rows = swap_blocks([r_ref[group, half, at, :] for group in range(8)])
        for c in range(8):
            d_scr[half * 8 + c, at, :] = rows[c]
    for c in range(8):
        d_scr[half * 8 + c, 72:80, :] = jnp.zeros((8, 128), F32)


def lift_pair(d_scr, pair, up_ref):
    high, low = split(side_by_side([d_scr[2 * pair], d_scr[2 * pair + 1]]))
    stacked = jnp.concatenate([high, high, low, jnp.zeros((16, 256), BF16)], axis=0)
    return dot(up_ref[...], stacked)


def analyse_kernel(flow_hbm, down_ref, s_ref, f_scr, p_scr, sems):
    copies = [
        pltpu.make_async_copy(flow_hbm.at[pl.ds(4 * k, 4)], f_scr.at[pl.ds(4 * k, 4)], sems.at[k])
        for k in range(4)
    ]
    for copy in copies:
        copy.start()
    for pair in range(8):
        if pair % 2 == 0:
            copies[pair // 2].wait()
        analyse_pair(f_scr, pair, down_ref, p_scr)
        if pair % 4 == 3:
            pack_planes(p_scr, s_ref, pair // 4)


def rows_body(r_ref, l_scr, v_ref):
    def collect(q, carry):
        one = (q + 1) % 8
        two = (q + 2) % 8
        for t in range(4):
            for half in range(2):
                total = r_ref[q, half, 7 * (6 + t) : 7 * (6 + t) + 8, :]
                total = total + r_ref[one, half, 7 * (2 + t) : 7 * (2 + t) + 8, :]
                if t >= 2:
                    total = total + r_ref[two, half, 7 * (t - 2) : 7 * (t - 2) + 8, :]
                l_scr[q * 4 + t, half] = total
        return carry

    lax.fori_loop(0, 8, collect, 0)

    def bands(mode, carry):
        for half in range(2):
            parts = [l_scr[(2 * mode + n) % 32, half] for n in range(8)]
            v_ref[mode, half] = gather_sum(list(zip(LOW_PASS, parts)))
            v_ref[mode + 16, half] = gather_sum(list(zip(HIGH_PASS, parts)))
        return carry

    lax.fori_loop(0, 16, bands, 0)


def rows_kernel(r_ref, v_ref, l_scr):
    rows_body(r_ref, l_scr, v_ref)


def rows_grad_kernel(r_ref, v_ref, bias_ref, l_scr):
    rows_body(r_ref, l_scr, v_ref)
    first = r_ref[0, 0, 70:71, :]
    second = r_ref[0, 0, 71:72, :]
    bias = r_ref[0, 1, 70:71, :]
    for i in range(1, 8):
        first = first + r_ref[i, 0, 70:71, :]
        second = second + r_ref[i, 0, 71:72, :]
        bias = bias + r_ref[i, 1, 70:71, :]

    def put(coef, carry):
        v_ref[coef, 0, 7:8, :] = first
        v_ref[coef, 1, 7:8, :] = second
        return carry

    lax.fori_loop(0, 32, put, 0)
    bias_ref[...] = jnp.broadcast_to(bias, (8, 128))


def weights_kernel(index_ref, w_ref, pw_ref, o_ref, forward_ref, back_ref):
    slab = index_ref[0]
    high = slab // 16
    mode = slab % 16
    right = mode // 8
    shift = (8 - mode % 8) * 16
    lane = lax.broadcasted_iota(jnp.int32, (256, 128), 1)
    low_y = jnp.where(right == 0, w_ref[high, :, 0:128], w_ref[high, :, 128:256])
    high_y = jnp.where(right == 0, w_ref[high + 2, :, 0:128], w_ref[high + 2, :, 128:256])
    low_y = pltpu.roll(low_y, shift % 128, 1)
    high_y = pltpu.roll(high_y, (shift + 16) % 128, 1)
    o_ref[...] = jnp.where(lane < 16, low_y, jnp.where(lane < 32, high_y, 0.0))
    same_y = iota(128, 128, 0) % 8 == iota(128, 128, 1) % 8
    rows = (iota(128, 16, 0) // 8 == iota(128, 16, 1)).astype(F32)
    cols = (iota(16, 128, 1) // 8 == iota(16, 128, 0)).astype(F32)
    point = pw_ref[...]
    for ref, matrix in ((forward_ref, point.T), (back_ref, point)):
        wide = jnp.where(same_y, exact_dot(exact_dot(rows, matrix), cols), 0.0)
        upper, lower = split(wide)
        ref[...] = side_by_side([upper, lower, upper])


def iota(rows, cols, axis):
    return lax.broadcasted_iota(jnp.int32, (rows, cols), axis)


def column_bands(v_ref, q_ref, half):
    value = v_ref[:, half].reshape(256, 128)
    return lax.dot_general(
        value.T, q_ref[...], (((1,), (0,)), ((), ())), precision=HIGHEST,
        preferred_element_type=F32,
    )


def column_changes(d_scr, q_ref, o_ref):
    for half in range(2):
        value = lax.dot_general(
            q_ref[...], d_scr[half * 128 : (half + 1) * 128, :], (((1,), (1,)), ((), ())),
            precision=HIGHEST, preferred_element_type=F32,
        )
        o_ref[:, half] = value.reshape(32, 8, 128)


def mix_kernel(v_ref, q_ref, w_ref, o_ref, y_ref, d_scr):
    for half in range(2):
        y_ref[half * 128 : (half + 1) * 128, :] = column_bands(v_ref, q_ref, half)

    def body(o, carry):
        total = -y_ref[pl.ds(pl.multiple_of(o * 16, 16), 16), :]
        for i in range(16):
            total = total + y_ref[i * 16 : (i + 1) * 16, :] * w_ref[pl.ds(i * 16 + o, 1), :]
        d_scr[pl.ds(pl.multiple_of(o * 16, 16), 16), :] = total
        return carry

    lax.fori_loop(0, 16, body, 0)
    column_changes(d_scr, q_ref, o_ref)


def grad_bands_kernel(v_ref, q_ref, y_ref, b_ref, g_ref, p_ref, g_scr):
    for half in range(2):
        b_ref[half * 128 : (half + 1) * 128, :] = column_bands(v_ref, q_ref, half)

    def body(i, carry):
        flow = y_ref[pl.ds(pl.multiple_of(i * 16, 16), 16), :]
        for o in range(16):
            grad = b_ref[o * 16 : (o + 1) * 16, :]
            g_scr[pl.ds(i * 16 + o, 1), :] = jnp.sum(flow * grad, axis=0, keepdims=True)
        return carry

    lax.fori_loop(0, 16, body, 0)
    lane = lax.broadcasted_iota(jnp.int32, (8, 128), 1)
    for group in range(8):
        packed = g_scr[group * 32 : group * 32 + 8, :]
        for k in range(1, 4):
            rows = g_scr[group * 32 + k * 8 : group * 32 + k * 8 + 8, :]
            packed = jnp.where(lane // 32 == k, pltpu.roll(rows, 32 * k, 1), packed)
        for copy in range(group // 4, 8, 2):
            g_ref[copy, group % 4] = packed
    first = v_ref[0, 0, 7:8, :]
    second = v_ref[0, 1, 7:8, :]
    for slab in range(1, 32):
        first = first + v_ref[slab, 0, 7:8, :]
        second = second + v_ref[slab, 1, 7:8, :]
    p_ref[...] = jnp.zeros((8, 128), F32)
    p_ref[0:1, :] = first
    p_ref[1:2, :] = second


def mix_grad_kernel(b_ref, q_ref, w_ref, bias_ref, o_ref, d_scr):
    def body(i, carry):
        total = -b_ref[pl.ds(pl.multiple_of(i * 16, 16), 16), :]
        for o in range(16):
            total = total + b_ref[o * 16 : (o + 1) * 16, :] * w_ref[pl.ds(i * 16 + o, 1), :]
        d_scr[pl.ds(pl.multiple_of(i * 16, 16), 16), :] = total
        return carry

    lax.fori_loop(0, 16, body, 0)
    column_changes(d_scr, q_ref, o_ref)
    for slab in range(32):
        o_ref[slab, 0, 7:8, :] = bias_ref[0:1, :]


def join_kernel(v_ref, g_ref, o_ref):
    for quarter in range(4):
        total = g_ref[0, quarter]
        for i in range(1, 8):
            total = total + g_ref[i, quarter]
        total = total * (1.0 / math.sqrt(128.0))
        for slab in range(8 * quarter, 8 * quarter + 8):
            o_ref[slab, 0:2] = v_ref[slab]
            o_ref[slab, 2] = total


def spread_body(v_ref, l_scr, s_ref):
    def lift(mode, carry):
        for half in range(2):
            low = [v_ref[(mode + 16 - d) % 16, half] for d in range(4)]
            high = [v_ref[16 + (mode + 16 - d) % 16, half] for d in range(4)]
            for p in range(2):
                pairs = [(LOW_PASS[2 * d + p], low[d]) for d in range(4)]
                pairs += [(HIGH_PASS[2 * d + p], high[d]) for d in range(4)]
                l_scr[2 * mode + p, half] = gather_sum(pairs)
        return carry

    lax.fori_loop(0, 16, lift, 0)

    def send(i, carry):
        for half in range(2):
            s_ref[i, half, 64:72, :] = jnp.zeros((8, 128), F32)
            for a in range(10):
                s_ref[i, half, 7 * a : 7 * a + 8, :] = l_scr[(4 * i + 26 + a) % 32, half]
        return carry

    lax.fori_loop(0, 8, send, 0)


def spread_kernel(v_ref, s_ref, l_scr):
    spread_body(v_ref, l_scr, s_ref)


def spread_grad_kernel(v_ref, s_ref, bias_ref, l_scr):
    spread_body(v_ref, l_scr, s_ref)
    bias = v_ref[0, 0, 7:8, :]
    for slab in range(1, 32):
        bias = bias + v_ref[slab, 0, 7:8, :]
    bias_ref[...] = jnp.broadcast_to(bias, (8, 128))


def point_mix(w_ref, first, second):
    high, low = split(side_by_side([first, second]))
    return dot(w_ref[...], jnp.concatenate([high, high, low], axis=0)), high, low


def centre_kernel(
    r_ref, flow_hbm, cot_hbm, w_ref, bias_ref, down_ref, up_ref, out_hbm, g_hbm, s_ref,
    f_scr, c_scr, v_scr, g_scr, d_scr, p_scr, sum_scr, pt_scr, sems,
):
    load_flow = pltpu.make_async_copy(flow_hbm, f_scr, sems.at[0])
    load_cot = pltpu.make_async_copy(cot_hbm, c_scr, sems.at[1])
    load_flow.start()
    load_cot.start()
    unpack_planes(r_ref, d_scr, 0)
    sum_scr[...] = jnp.zeros((128, 128), F32)
    pt_scr[...] = jnp.zeros((128, 128), F32)
    load_flow.wait()
    for pair in range(8):
        if pair == 1:
            unpack_planes(r_ref, d_scr, 1)
        change = lift_pair(d_scr, pair, up_ref)
        for k in range(2):
            c = 2 * pair + k
            v_scr[c] = f_scr[c] + (change[:, 128 * k : 128 * k + 128] + bias_ref[c])
    load_cot.wait()
    stores = []
    for chunk in range(4):

        def body(step, carry):
            start = pl.multiple_of((chunk * 4 + step) * 16, 16)
            spans = [pl.ds(start, 8), pl.ds(pl.multiple_of(start + 8, 8), 8)]
            fields = [f_scr[:, span, :].reshape(128, 128) for span in spans]
            mixed, f_high, f_low = point_mix(w_ref, fields[0], fields[1])
            grads = []
            for k in range(2):
                value = v_scr[:, spans[k], :].reshape(128, 128) + mixed[:, 128 * k : 128 * k + 128]
                square = value * value
                tangent = jnp.tanh(value * (GELU_SCALE + (GELU_SCALE * GELU_CUBE) * square))
                half_up = 0.5 + 0.5 * tangent
                v_scr[:, spans[k], :] = (value * half_up).reshape(16, 8, 128)
                bend = value * ((0.5 * GELU_SCALE) + (1.5 * GELU_SCALE * GELU_CUBE) * square)
                slope = half_up + bend * (1.0 - tangent * tangent)
                grad = c_scr[:, spans[k], :].reshape(128, 128) * slope
                g_scr[:, spans[k], :] = grad.reshape(16, 8, 128)
                grads.append(grad)
            sum_scr[...] += grads[0] + grads[1]
            g_high, g_low = split(side_by_side(grads))
            pt_scr[...] += lax.dot_general(
                side_by_side([f_high, f_low, f_high]), side_by_side([g_high, g_high, g_low]),
                (((1,), (1,)), ((), ())), preferred_element_type=F32,
            )
            return carry

        lax.fori_loop(0, 4, body, 0, unroll=True)
        part = pl.ds(chunk * 64, 64)
        for k, (scr, hbm) in enumerate(((v_scr, out_hbm), (g_scr, g_hbm))):
            store = pltpu.make_async_copy(
                scr.at[:, part], hbm.at[:, part], sems.at[2 + 2 * chunk + k]
            )
            store.start()
            stores.append(store)
    for pair in range(8):
        analyse_pair(g_scr, pair, down_ref, p_scr)
        if pair % 4 == 3:
            pack_planes(p_scr, s_ref, pair // 4)
    same_y = iota(128, 128, 0) % 8 == iota(128, 128, 1) % 8
    gather = (iota(16, 128, 1) // 8 == iota(16, 128, 0)).astype(F32)
    fold = (iota(128, 128, 0) // 8 == iota(128, 128, 1) % 16).astype(F32)
    wide = exact_dot(exact_dot(gather, jnp.where(same_y, pt_scr[...], 0.0)), fold)
    lane, row = iota(16, 128, 1), iota(16, 128, 0)
    wide = jnp.where(lane // 16 == row % 8, wide, 0.0)
    first = jnp.sum(wide[0:8], axis=0, keepdims=True)
    second = jnp.sum(wide[8:16], axis=0, keepdims=True)
    totals = jnp.sum(exact_dot(gather, sum_scr[...]), axis=1, keepdims=True)
    bias_row = jnp.sum(jnp.where(lane == row, totals, 0.0), axis=0, keepdims=True)
    for group in range(8):
        s_ref[group, 0, 70:71, :] = first
        s_ref[group, 0, 71:72, :] = second
        s_ref[group, 1, 70:71, :] = bias_row
    for store in stores:
        store.wait()


def finish_kernel(r_ref, g_hbm, w_ref, up_ref, out_hbm, g_scr, v_scr, d_scr, sems):
    load = pltpu.make_async_copy(g_hbm, g_scr, sems.at[0])
    load.start()
    unpack_planes(r_ref, d_scr, 0)
    load.wait()
    for pair in range(8):
        if pair == 1:
            unpack_planes(r_ref, d_scr, 1)
        change = lift_pair(d_scr, pair, up_ref)
        for k in range(2):
            v_scr[2 * pair + k] = g_scr[2 * pair + k] + change[:, 128 * k : 128 * k + 128]
    stores = []
    for chunk in range(4):

        def body(step, carry):
            start = pl.multiple_of((chunk * 4 + step) * 16, 16)
            spans = [pl.ds(start, 8), pl.ds(pl.multiple_of(start + 8, 8), 8)]
            fields = [g_scr[:, span, :].reshape(128, 128) for span in spans]
            mixed = point_mix(w_ref, fields[0], fields[1])[0]
            for k in range(2):
                value = v_scr[:, spans[k], :].reshape(128, 128) + mixed[:, 128 * k : 128 * k + 128]
                v_scr[:, spans[k], :] = value.reshape(16, 8, 128)
            return carry

        lax.fori_loop(0, 4, body, 0, unroll=True)
        part = pl.ds(chunk * 64, 64)
        store = pltpu.make_async_copy(v_scr.at[:, part], out_hbm.at[:, part], sems.at[1 + chunk])
        store.start()
        stores.append(store)
    for store in stores:
        store.wait()


def modes_place_kernel(m_ref, o_ref):
    for high in range(2):
        for right in range(2):
            rows = swap_blocks([m_ref[high * 16 + right * 8 + m, 2] for m in range(8)])
            for k in range(4):
                for up in range(2):
                    o_ref[
                        high + 2 * up, k * 8 : k * 8 + 8, right * 128 : (right + 1) * 128
                    ] = rows[2 * k + up]


def gather_kernel(index_ref, *refs):
    parts, out_hbm, sems = refs[:8], refs[8], refs[9]
    copies = []
    for k, (flip, shift) in enumerate(MODE_ROUTES + [(0, 0)]):
        core = (index_ref[1] + flip) % 2
        owner = core * 4 + (index_ref[0] // 8 + 4 - shift) % 4
        to = out_hbm.at[:, pl.ds(pl.multiple_of(owner * 32, 32), 32), :]
        copies.append(pltpu.make_async_copy(parts[k], to, sems.at[k]))
    for copy in copies:
        copy.start()
    for copy in copies:
        copy.wait()


def call(kernel, ins, outs, scratch=(), sems=0, mib=8):
    spaces = {"v": pltpu.VMEM, "s": pltpu.SMEM, "a": pltpu.HBM}
    structs = [jax.ShapeDtypeStruct(o[0], o[2] if len(o) > 2 else F32) for o in outs]
    scratches = [pltpu.VMEM(shape, F32) for shape in scratch]
    if sems:
        scratches.append(pltpu.SemaphoreType.DMA((sems,)))
    return pl.pallas_call(
        kernel,
        out_shape=structs,
        in_specs=[pl.BlockSpec(memory_space=spaces[k]) for k in ins],
        out_specs=[pl.BlockSpec(memory_space=spaces[o[1]]) for o in outs],
        scratch_shapes=scratches,
        compiler_params=pltpu.CompilerParams(vmem_limit_bytes=mib * 1024 * 1024),
    )


def local(flow_field, cotangent, mode_weights, point_weights, point_bias):
    swap_x = lambda v: lax.all_to_all(v, "gx", 0, 0, tiled=False)
    swap_y = lambda v: lax.all_to_all(v, "gy", 0, 0, tiled=False)
    packed = ((8, 2, 72, 128), "v")
    coefs = ((32, 2, 8, 128), "v")
    square = ((256, 128), "v")
    row = ((8, 128), "v")
    cells = (16, 256, 128)
    parts = (16, 80, 128)
    rows3 = [(32, 2, 8, 128)]
    table = jnp.asarray(y_table())
    down, up = (jnp.asarray(t) for t in cell_tables())
    slab = lax.axis_index("gy").astype(jnp.int32).reshape(1)
    flow_cells = flow_field.reshape(cells)
    kron = ((128, 384), "v", BF16)

    weights, mix_forward, mix_back = call(weights_kernel, "svv", [square, kron, kron])(
        slab, mode_weights.reshape(4, 256, 256), point_weights
    )
    (sent,) = call(analyse_kernel, "av", [packed], [cells, parts], 4, 52)(flow_cells, down)
    (got,) = call(rows_kernel, "v", [coefs], rows3)(swap_x(sent))
    back, bands_flow = call(mix_kernel, "vvv", [coefs, square], [(256, 128)])(
        swap_y(got), table, weights
    )
    (spread,) = call(spread_kernel, "v", [packed], rows3)(swap_y(back))
    output_field, grads, sent = call(
        centre_kernel, "vaavsvv", [(cells, "a"), (cells, "a"), packed],
        [cells] * 4 + [parts] * 2 + [(128, 128)] * 2, 10, 52,
    )(
        swap_x(spread), flow_cells, cotangent.reshape(cells), mix_forward, point_bias, down, up
    )
    got, bias_part = call(rows_grad_kernel, "v", [coefs, row], rows3)(swap_x(sent))
    bands_grad, mode_part, point_total = call(
        grad_bands_kernel, "vvv", [square, ((8, 4, 8, 128), "v"), row], [(256, 128)]
    )(swap_y(got), table, bands_flow)
    (back,) = call(mix_grad_kernel, "vvvv", [coefs], [(256, 128)])(
        bands_grad, table, weights, bias_part
    )
    (joined,) = call(join_kernel, "vv", [((32, 3, 8, 128), "v")])(back, swap_x(mode_part))
    joined = swap_y(joined)
    spread, bias_total = call(spread_grad_kernel, "v", [packed, row], rows3)(joined)
    (grad_field,) = call(
        finish_kernel, "vavv", [(cells, "a")], [cells] * 2 + [parts], 5, 52
    )(swap_x(spread), grads, mix_back, up)
    (placed,) = call(modes_place_kernel, "v", [((4, 32, 256), "v")])(joined)
    parts = []
    for flip, shift in MODE_ROUTES:
        routes = [
            (i * 32 + j, (i ^ flip) * 32 + (j + 8 * shift) % 32)
            for i in range(8)
            for j in range(32)
        ]
        parts.append(lax.ppermute(placed, ("gx", "gy"), routes))
    place, grad_field = lax.optimization_barrier(
        (jnp.stack([lax.axis_index("gy"), lax.axis_index("gx")]).astype(jnp.int32), grad_field)
    )
    (modes,) = call(gather_kernel, "s" + "a" * 8, [((4, 256, 256), "a")], (), 8)(
        place, *parts, placed
    )

    cell_count = flow_field.shape[3] * 256 * 256
    return (
        output_field.reshape(flow_field.shape),
        grad_field.reshape(flow_field.shape),
        modes.reshape(4, 16, 16, 256),
        point_total[0:2].reshape(16, 16) / math.sqrt(cell_count),
        bias_total[0, :16] / math.sqrt(cell_count),
    )


def solution(mesh):
    in_specs = (P(None, "gx", "gy", None), P(None, "gx", "gy", None), P(), P(), P())
    out_specs = (P(None, "gx", "gy", None), P(None, "gx", "gy", None), P(), P(), P())
    return jax.shard_map(local, mesh=mesh, in_specs=in_specs, out_specs=out_specs, check_vma=False)
```

```python
import math

import jax
import jax.numpy as jnp
import ml_dtypes
import numpy as np
from jax import lax
from jax.experimental import pallas as pl
from jax.experimental.pallas import tpu as pltpu
from jax.sharding import PartitionSpec as P

LOW_PASS = [
    0.23037781330885523,
    0.7148465705525415,
    0.6308807679295904,
    -0.02798376941698385,
    -0.18703481171888114,
    0.030841381835986965,
    0.032883011666982945,
    -0.010597401784997278,
]
HIGH_PASS = [(-1) ** position * LOW_PASS[7 - position] for position in range(8)]
GELU_SCALE = 0.7978845608028654
GELU_CUBE = 0.044715


def triple_low():
    taps = np.zeros(50)
    for p, hp in enumerate(LOW_PASS):
        for q, hq in enumerate(LOW_PASS):
            for r, hr in enumerate(LOW_PASS):
                taps[p + 2 * q + 4 * r] += hp * hq * hr
    return [float(t) for t in taps]


TRIPLE = triple_low()
HIGHEST = lax.Precision.HIGHEST
F32 = jnp.float32
BF16 = jnp.bfloat16
MODE_ROUTES = [(0, 1), (0, 2), (0, 3), (1, 0), (1, 1), (1, 2), (1, 3)]


def cell_tables():
    table = np.zeros((80, 256))
    for a in range(10):
        for b in range(7):
            for x in range(32):
                for y in range(8):
                    at_x, at_y = x + 48 - 8 * a, y + 48 - 8 * b
                    if 0 <= at_x < 50 and 0 <= at_y < 50:
                        table[a * 7 + b, x * 8 + y] = TRIPLE[at_x] * TRIPLE[at_y]
    table = table.astype(np.float32)
    high = table.astype(ml_dtypes.bfloat16)
    low = (table - high.astype(np.float32)).astype(ml_dtypes.bfloat16)
    down = np.concatenate([high, low])
    pad = np.zeros((256, 16), ml_dtypes.bfloat16)
    up = np.concatenate([high.T, low.T, high.T, pad], 1)
    return down, up


def y_table():
    table = np.zeros((32, 8, 128), np.float32)
    for slab in range(32):
        for b in range(7):
            ky = (slab - 6 + b) % 32
            for mode in range(16):
                at = (ky - 2 * mode) % 32
                if at < 8:
                    table[slab, b, mode] = LOW_PASS[at]
                    table[slab, b, 16 + mode] = HIGH_PASS[at]
    return table.reshape(256, 128)


def gather_sum(pairs):
    total = None
    for weight, value in pairs:
        term = value * weight
        total = term if total is None else total + term
    return total


def swap_blocks(rows):
    lane = lax.broadcasted_iota(jnp.int32, (8, 128), 1)
    rows = [rows[0]] + [pltpu.roll(rows[c], 16 * c, 1) for c in range(1, 8)]
    for bit in range(3):
        step = 1 << bit
        chosen = (lane & (16 * step)) != 0
        rows = [jnp.where(chosen, rows[(m + step) % 8], rows[m]) for m in range(8)]
    rows = [rows[(8 - k) % 8] for k in range(8)]
    return [rows[0]] + [pltpu.roll(rows[k], 128 - 16 * k, 1) for k in range(1, 8)]


def split(value):
    high = value.astype(BF16)
    return high, (value - high.astype(F32)).astype(BF16)


def dot(left, right):
    return lax.dot_general(left, right, (((1,), (0,)), ((), ())), preferred_element_type=F32)


def exact_dot(left, right):
    return lax.dot_general(
        left, right, (((1,), (0,)), ((), ())), precision=HIGHEST, preferred_element_type=F32
    )


def side_by_side(values):
    return jnp.concatenate(values, axis=1)


def analyse_pair(field, pair, down_ref, p_scr):
    high, low = split(side_by_side([field[2 * pair], field[2 * pair + 1]]))
    wide = dot(down_ref[...], high)
    total = wide[0:80] + wide[80:160] + dot(down_ref[0:80, :], low)
    p_scr[2 * pair] = total[:, 0:128]
    p_scr[2 * pair + 1] = total[:, 128:256]


def pack_planes(p_scr, s_ref, half):
    for octet in range(9):
        at = slice(octet * 8, octet * 8 + 8)
        rows = swap_blocks([p_scr[half * 8 + c, at, :] for c in range(8)])
        for group in range(8):
            s_ref[group, half, at, :] = rows[group]


def unpack_planes(r_ref, d_scr, half):
    for octet in range(9):
        at = slice(octet * 8, octet * 8 + 8)
        rows = swap_blocks([r_ref[group, half, at, :] for group in range(8)])
        for c in range(8):
            d_scr[half * 8 + c, at, :] = rows[c]
    for c in range(8):
        d_scr[half * 8 + c, 72:80, :] = jnp.zeros((8, 128), F32)


def lift_pair(d_scr, pair, up_ref):
    high, low = split(side_by_side([d_scr[2 * pair], d_scr[2 * pair + 1]]))
    stacked = jnp.concatenate([high, high, low, jnp.zeros((16, 256), BF16)], axis=0)
    return dot(up_ref[...], stacked)


def analyse_kernel(flow_hbm, down_ref, s_ref, f_scr, p_scr, sems):
    copies = [
        pltpu.make_async_copy(flow_hbm.at[pl.ds(4 * k, 4)], f_scr.at[pl.ds(4 * k, 4)], sems.at[k])
        for k in range(4)
    ]
    for copy in copies:
        copy.start()
    for pair in range(8):
        if pair % 2 == 0:
            copies[pair // 2].wait()
        analyse_pair(f_scr, pair, down_ref, p_scr)
        if pair % 4 == 3:
            pack_planes(p_scr, s_ref, pair // 4)


def rows_body(r_ref, l_scr, v_ref):
    def collect(q, carry):
        one = (q + 1) % 8
        two = (q + 2) % 8
        for t in range(4):
            for half in range(2):
                total = r_ref[q, half, 7 * (6 + t) : 7 * (6 + t) + 8, :]
                total = total + r_ref[one, half, 7 * (2 + t) : 7 * (2 + t) + 8, :]
                if t >= 2:
                    total = total + r_ref[two, half, 7 * (t - 2) : 7 * (t - 2) + 8, :]
                l_scr[q * 4 + t, half] = total
        return carry

    lax.fori_loop(0, 8, collect, 0)

    def bands(mode, carry):
        for half in range(2):
            parts = [l_scr[(2 * mode + n) % 32, half] for n in range(8)]
            v_ref[mode, half] = gather_sum(list(zip(LOW_PASS, parts)))
            v_ref[mode + 16, half] = gather_sum(list(zip(HIGH_PASS, parts)))
        return carry

    lax.fori_loop(0, 16, bands, 0)


def rows_kernel(r_ref, v_ref, l_scr):
    rows_body(r_ref, l_scr, v_ref)


def rows_grad_kernel(r_ref, v_ref, bias_ref, l_scr):
    rows_body(r_ref, l_scr, v_ref)
    first = r_ref[0, 0, 70:71, :]
    second = r_ref[0, 0, 71:72, :]
    bias = r_ref[0, 1, 70:71, :]
    for i in range(1, 8):
        first = first + r_ref[i, 0, 70:71, :]
        second = second + r_ref[i, 0, 71:72, :]
        bias = bias + r_ref[i, 1, 70:71, :]

    def put(coef, carry):
        v_ref[coef, 0, 7:8, :] = first
        v_ref[coef, 1, 7:8, :] = second
        return carry

    lax.fori_loop(0, 32, put, 0)
    bias_ref[...] = jnp.broadcast_to(bias, (8, 128))


def weights_kernel(index_ref, w_ref, pw_ref, o_ref, forward_ref, back_ref):
    slab = index_ref[0]
    high = slab // 16
    mode = slab % 16
    right = mode // 8
    shift = (8 - mode % 8) * 16
    lane = lax.broadcasted_iota(jnp.int32, (256, 128), 1)
    low_y = jnp.where(right == 0, w_ref[high, :, 0:128], w_ref[high, :, 128:256])
    high_y = jnp.where(right == 0, w_ref[high + 2, :, 0:128], w_ref[high + 2, :, 128:256])
    low_y = pltpu.roll(low_y, shift % 128, 1)
    high_y = pltpu.roll(high_y, (shift + 16) % 128, 1)
    o_ref[...] = jnp.where(lane < 16, low_y, jnp.where(lane < 32, high_y, 0.0))
    same_y = iota(128, 128, 0) % 8 == iota(128, 128, 1) % 8
    rows = (iota(128, 16, 0) // 8 == iota(128, 16, 1)).astype(F32)
    cols = (iota(16, 128, 1) // 8 == iota(16, 128, 0)).astype(F32)
    point = pw_ref[...]
    for ref, matrix in ((forward_ref, point.T), (back_ref, point)):
        wide = jnp.where(same_y, exact_dot(exact_dot(rows, matrix), cols), 0.0)
        upper, lower = split(wide)
        ref[...] = side_by_side([upper, lower, upper])


def iota(rows, cols, axis):
    return lax.broadcasted_iota(jnp.int32, (rows, cols), axis)


def column_bands(v_ref, q_ref, half):
    value = v_ref[:, half].reshape(256, 128)
    return lax.dot_general(
        value.T, q_ref[...], (((1,), (0,)), ((), ())), precision=HIGHEST,
        preferred_element_type=F32,
    )


def column_changes(d_scr, q_ref, o_ref):
    for half in range(2):
        value = lax.dot_general(
            q_ref[...], d_scr[half * 128 : (half + 1) * 128, :], (((1,), (1,)), ((), ())),
            precision=HIGHEST, preferred_element_type=F32,
        )
        o_ref[:, half] = value.reshape(32, 8, 128)


def mix_kernel(v_ref, q_ref, w_ref, o_ref, y_ref, d_scr):
    for half in range(2):
        y_ref[half * 128 : (half + 1) * 128, :] = column_bands(v_ref, q_ref, half)

    def body(o, carry):
        total = -y_ref[pl.ds(pl.multiple_of(o * 16, 16), 16), :]
        for i in range(16):
            total = total + y_ref[i * 16 : (i + 1) * 16, :] * w_ref[pl.ds(i * 16 + o, 1), :]
        d_scr[pl.ds(pl.multiple_of(o * 16, 16), 16), :] = total
        return carry

    lax.fori_loop(0, 16, body, 0)
    column_changes(d_scr, q_ref, o_ref)


def grad_bands_kernel(v_ref, q_ref, y_ref, b_ref, g_ref, p_ref, g_scr):
    for half in range(2):
        b_ref[half * 128 : (half + 1) * 128, :] = column_bands(v_ref, q_ref, half)

    def body(i, carry):
        flow = y_ref[pl.ds(pl.multiple_of(i * 16, 16), 16), :]
        for o in range(16):
            grad = b_ref[o * 16 : (o + 1) * 16, :]
            g_scr[pl.ds(i * 16 + o, 1), :] = jnp.sum(flow * grad, axis=0, keepdims=True)
        return carry

    lax.fori_loop(0, 16, body, 0)
    lane = lax.broadcasted_iota(jnp.int32, (8, 128), 1)
    for group in range(8):
        packed = g_scr[group * 32 : group * 32 + 8, :]
        for k in range(1, 4):
            rows = g_scr[group * 32 + k * 8 : group * 32 + k * 8 + 8, :]
            packed = jnp.where(lane // 32 == k, pltpu.roll(rows, 32 * k, 1), packed)
        for copy in range(group // 4, 8, 2):
            g_ref[copy, group % 4] = packed
    first = v_ref[0, 0, 7:8, :]
    second = v_ref[0, 1, 7:8, :]
    for slab in range(1, 32):
        first = first + v_ref[slab, 0, 7:8, :]
        second = second + v_ref[slab, 1, 7:8, :]
    p_ref[...] = jnp.zeros((8, 128), F32)
    p_ref[0:1, :] = first
    p_ref[1:2, :] = second


def mix_grad_kernel(b_ref, q_ref, w_ref, bias_ref, o_ref, d_scr):
    def body(i, carry):
        total = -b_ref[pl.ds(pl.multiple_of(i * 16, 16), 16), :]
        for o in range(16):
            total = total + b_ref[o * 16 : (o + 1) * 16, :] * w_ref[pl.ds(i * 16 + o, 1), :]
        d_scr[pl.ds(pl.multiple_of(i * 16, 16), 16), :] = total
        return carry

    lax.fori_loop(0, 16, body, 0)
    column_changes(d_scr, q_ref, o_ref)
    for slab in range(32):
        o_ref[slab, 0, 7:8, :] = bias_ref[0:1, :]


def join_kernel(v_ref, g_ref, o_ref):
    for quarter in range(4):
        total = g_ref[0, quarter]
        for i in range(1, 8):
            total = total + g_ref[i, quarter]
        total = total * (1.0 / math.sqrt(128.0))
        for slab in range(8 * quarter, 8 * quarter + 8):
            o_ref[slab, 0:2] = v_ref[slab]
            o_ref[slab, 2] = total


def spread_body(v_ref, l_scr, s_ref):
    def lift(mode, carry):
        for half in range(2):
            low = [v_ref[(mode + 16 - d) % 16, half] for d in range(4)]
            high = [v_ref[16 + (mode + 16 - d) % 16, half] for d in range(4)]
            for p in range(2):
                pairs = [(LOW_PASS[2 * d + p], low[d]) for d in range(4)]
                pairs += [(HIGH_PASS[2 * d + p], high[d]) for d in range(4)]
                l_scr[2 * mode + p, half] = gather_sum(pairs)
        return carry

    lax.fori_loop(0, 16, lift, 0)

    def send(i, carry):
        for half in range(2):
            s_ref[i, half, 64:72, :] = jnp.zeros((8, 128), F32)
            for a in range(10):
                s_ref[i, half, 7 * a : 7 * a + 8, :] = l_scr[(4 * i + 26 + a) % 32, half]
        return carry

    lax.fori_loop(0, 8, send, 0)


def spread_kernel(v_ref, s_ref, l_scr):
    spread_body(v_ref, l_scr, s_ref)


def spread_grad_kernel(v_ref, s_ref, bias_ref, l_scr):
    spread_body(v_ref, l_scr, s_ref)
    bias = v_ref[0, 0, 7:8, :]
    for slab in range(1, 32):
        bias = bias + v_ref[slab, 0, 7:8, :]
    bias_ref[...] = jnp.broadcast_to(bias, (8, 128))


def point_mix(w_ref, first, second):
    high, low = split(side_by_side([first, second]))
    return dot(w_ref[...], jnp.concatenate([high, high, low], axis=0)), high, low


def centre_kernel(
    r_ref, flow_hbm, cot_hbm, w_ref, bias_ref, down_ref, up_ref, out_hbm, g_hbm, s_ref,
    f_scr, c_scr, v_scr, g_scr, d_scr, p_scr, sum_scr, pt_scr, sems,
):
    load_flow = pltpu.make_async_copy(flow_hbm, f_scr, sems.at[0])
    load_cot = pltpu.make_async_copy(cot_hbm, c_scr, sems.at[1])
    load_flow.start()
    load_cot.start()
    unpack_planes(r_ref, d_scr, 0)
    sum_scr[...] = jnp.zeros((128, 128), F32)
    pt_scr[...] = jnp.zeros((128, 128), F32)
    load_flow.wait()
    for pair in range(8):
        if pair == 1:
            unpack_planes(r_ref, d_scr, 1)
        change = lift_pair(d_scr, pair, up_ref)
        for k in range(2):
            c = 2 * pair + k
            v_scr[c] = f_scr[c] + (change[:, 128 * k : 128 * k + 128] + bias_ref[c])
    load_cot.wait()
    stores = []
    for chunk in range(4):

        def body(step, carry):
            start = pl.multiple_of((chunk * 4 + step) * 16, 16)
            spans = [pl.ds(start, 8), pl.ds(pl.multiple_of(start + 8, 8), 8)]
            fields = [f_scr[:, span, :].reshape(128, 128) for span in spans]
            mixed, f_high, f_low = point_mix(w_ref, fields[0], fields[1])
            grads = []
            for k in range(2):
                value = v_scr[:, spans[k], :].reshape(128, 128) + mixed[:, 128 * k : 128 * k + 128]
                square = value * value
                tangent = jnp.tanh(value * (GELU_SCALE + (GELU_SCALE * GELU_CUBE) * square))
                half_up = 0.5 + 0.5 * tangent
                v_scr[:, spans[k], :] = (value * half_up).reshape(16, 8, 128)
                bend = value * ((0.5 * GELU_SCALE) + (1.5 * GELU_SCALE * GELU_CUBE) * square)
                slope = half_up + bend * (1.0 - tangent * tangent)
                grad = c_scr[:, spans[k], :].reshape(128, 128) * slope
                g_scr[:, spans[k], :] = grad.reshape(16, 8, 128)
                grads.append(grad)
            sum_scr[...] += grads[0] + grads[1]
            g_high, g_low = split(side_by_side(grads))
            pt_scr[...] += lax.dot_general(
                side_by_side([f_high, f_low, f_high]), side_by_side([g_high, g_high, g_low]),
                (((1,), (1,)), ((), ())), preferred_element_type=F32,
            )
            return carry

        lax.fori_loop(0, 4, body, 0, unroll=True)
        part = pl.ds(chunk * 64, 64)
        for k, (scr, hbm) in enumerate(((v_scr, out_hbm), (g_scr, g_hbm))):
            store = pltpu.make_async_copy(
                scr.at[:, part], hbm.at[:, part], sems.at[2 + 2 * chunk + k]
            )
            store.start()
            stores.append(store)
    for pair in range(8):
        analyse_pair(g_scr, pair, down_ref, p_scr)
        if pair % 4 == 3:
            pack_planes(p_scr, s_ref, pair // 4)
    same_y = iota(128, 128, 0) % 8 == iota(128, 128, 1) % 8
    gather = (iota(16, 128, 1) // 8 == iota(16, 128, 0)).astype(F32)
    fold = (iota(128, 128, 0) // 8 == iota(128, 128, 1) % 16).astype(F32)
    wide = exact_dot(exact_dot(gather, jnp.where(same_y, pt_scr[...], 0.0)), fold)
    lane, row = iota(16, 128, 1), iota(16, 128, 0)
    wide = jnp.where(lane // 16 == row % 8, wide, 0.0)
    first = jnp.sum(wide[0:8], axis=0, keepdims=True)
    second = jnp.sum(wide[8:16], axis=0, keepdims=True)
    totals = jnp.sum(exact_dot(gather, sum_scr[...]), axis=1, keepdims=True)
    bias_row = jnp.sum(jnp.where(lane == row, totals, 0.0), axis=0, keepdims=True)
    for group in range(8):
        s_ref[group, 0, 70:71, :] = first
        s_ref[group, 0, 71:72, :] = second
        s_ref[group, 1, 70:71, :] = bias_row
    for store in stores:
        store.wait()


def finish_kernel(r_ref, g_hbm, w_ref, up_ref, out_hbm, g_scr, v_scr, d_scr, sems):
    load = pltpu.make_async_copy(g_hbm, g_scr, sems.at[0])
    load.start()
    unpack_planes(r_ref, d_scr, 0)
    load.wait()
    for pair in range(8):
        if pair == 1:
            unpack_planes(r_ref, d_scr, 1)
        change = lift_pair(d_scr, pair, up_ref)
        for k in range(2):
            v_scr[2 * pair + k] = g_scr[2 * pair + k] + change[:, 128 * k : 128 * k + 128]
    stores = []
    for chunk in range(4):

        def body(step, carry):
            start = pl.multiple_of((chunk * 4 + step) * 16, 16)
            spans = [pl.ds(start, 8), pl.ds(pl.multiple_of(start + 8, 8), 8)]
            fields = [g_scr[:, span, :].reshape(128, 128) for span in spans]
            mixed = point_mix(w_ref, fields[0], fields[1])[0]
            for k in range(2):
                value = v_scr[:, spans[k], :].reshape(128, 128) + mixed[:, 128 * k : 128 * k + 128]
                v_scr[:, spans[k], :] = value.reshape(16, 8, 128)
            return carry

        lax.fori_loop(0, 4, body, 0, unroll=True)
        part = pl.ds(chunk * 64, 64)
        store = pltpu.make_async_copy(v_scr.at[:, part], out_hbm.at[:, part], sems.at[1 + chunk])
        store.start()
        stores.append(store)
    for store in stores:
        store.wait()


def modes_place_kernel(m_ref, o_ref):
    for high in range(2):
        for right in range(2):
            rows = swap_blocks([m_ref[high * 16 + right * 8 + m, 2] for m in range(8)])
            for k in range(4):
                for up in range(2):
                    o_ref[
                        high + 2 * up, k * 8 : k * 8 + 8, right * 128 : (right + 1) * 128
                    ] = rows[2 * k + up]


def gather_kernel(index_ref, *refs):
    parts, out_hbm, sems = refs[:8], refs[8], refs[9]
    copies = []
    for k, (flip, shift) in enumerate(MODE_ROUTES + [(0, 0)]):
        core = (index_ref[1] + flip) % 2
        owner = core * 4 + (index_ref[0] // 8 + 4 - shift) % 4
        to = out_hbm.at[:, pl.ds(pl.multiple_of(owner * 32, 32), 32), :]
        copies.append(pltpu.make_async_copy(parts[k], to, sems.at[k]))
    for copy in copies:
        copy.start()
    for copy in copies:
        copy.wait()


def call(kernel, ins, outs, scratch=(), sems=0, mib=8):
    spaces = {"v": pltpu.VMEM, "s": pltpu.SMEM, "a": pltpu.HBM}
    structs = [jax.ShapeDtypeStruct(o[0], o[2] if len(o) > 2 else F32) for o in outs]
    scratches = [pltpu.VMEM(shape, F32) for shape in scratch]
    if sems:
        scratches.append(pltpu.SemaphoreType.DMA((sems,)))
    return pl.pallas_call(
        kernel,
        out_shape=structs,
        in_specs=[pl.BlockSpec(memory_space=spaces[k]) for k in ins],
        out_specs=[pl.BlockSpec(memory_space=spaces[o[1]]) for o in outs],
        scratch_shapes=scratches,
        compiler_params=pltpu.CompilerParams(vmem_limit_bytes=mib * 1024 * 1024),
    )


def local(flow_field, cotangent, mode_weights, point_weights, point_bias):
    swap_x = lambda v: lax.all_to_all(v, "gx", 0, 0, tiled=False)
    swap_y = lambda v: lax.all_to_all(v, "gy", 0, 0, tiled=False)
    packed = ((8, 2, 72, 128), "v")
    coefs = ((32, 2, 8, 128), "v")
    square = ((256, 128), "v")
    row = ((8, 128), "v")
    cells = (16, 256, 128)
    parts = (16, 80, 128)
    rows3 = [(32, 2, 8, 128)]
    table = jnp.asarray(y_table())
    down, up = (jnp.asarray(t) for t in cell_tables())
    slab = lax.axis_index("gy").astype(jnp.int32).reshape(1)
    flow_cells = flow_field.reshape(cells)
    kron = ((128, 384), "v", BF16)

    weights, mix_forward, mix_back = call(weights_kernel, "svv", [square, kron, kron])(
        slab, mode_weights.reshape(4, 256, 256), point_weights
    )
    (sent,) = call(analyse_kernel, "av", [packed], [cells, parts], 4, 52)(flow_cells, down)
    (got,) = call(rows_kernel, "v", [coefs], rows3)(swap_x(sent))
    back, bands_flow = call(mix_kernel, "vvv", [coefs, square], [(256, 128)])(
        swap_y(got), table, weights
    )
    (spread,) = call(spread_kernel, "v", [packed], rows3)(swap_y(back))
    output_field, grads, sent = call(
        centre_kernel, "vaavsvv", [(cells, "a"), (cells, "a"), packed],
        [cells] * 4 + [parts] * 2 + [(128, 128)] * 2, 10, 52,
    )(
        swap_x(spread), flow_cells, cotangent.reshape(cells), mix_forward, point_bias, down, up
    )
    got, bias_part = call(rows_grad_kernel, "v", [coefs, row], rows3)(swap_x(sent))
    bands_grad, mode_part, point_total = call(
        grad_bands_kernel, "vvv", [square, ((8, 4, 8, 128), "v"), row], [(256, 128)]
    )(swap_y(got), table, bands_flow)
    (back,) = call(mix_grad_kernel, "vvvv", [coefs], [(256, 128)])(
        bands_grad, table, weights, bias_part
    )
    (joined,) = call(join_kernel, "vv", [((32, 3, 8, 128), "v")])(back, swap_x(mode_part))
    joined = swap_y(joined)
    spread, bias_total = call(spread_grad_kernel, "v", [packed, row], rows3)(joined)
    (grad_field,) = call(
        finish_kernel, "vavv", [(cells, "a")], [cells] * 2 + [parts], 5, 52
    )(swap_x(spread), grads, mix_back, up)
    (placed,) = call(modes_place_kernel, "v", [((4, 32, 256), "v")])(joined)
    parts = [placed]
    for shift in (1, 2, 3):
        routes = [(j, (j + 8 * shift) % 32) for j in range(32)]
        parts.append(lax.ppermute(placed, "gy", routes))
    parts += [lax.ppermute(part, "gx", [(i, i ^ 1) for i in range(8)]) for part in parts]
    parts = parts[1:]
    place, grad_field = lax.optimization_barrier(
        (jnp.stack([lax.axis_index("gy"), lax.axis_index("gx")]).astype(jnp.int32), grad_field)
    )
    (modes,) = call(gather_kernel, "s" + "a" * 8, [((4, 256, 256), "a")], (), 8)(
        place, *parts, placed
    )

    cell_count = flow_field.shape[3] * 256 * 256
    return (
        output_field.reshape(flow_field.shape),
        grad_field.reshape(flow_field.shape),
        modes.reshape(4, 16, 16, 256),
        point_total[0:2].reshape(16, 16) / math.sqrt(cell_count),
        bias_total[0, :16] / math.sqrt(cell_count),
    )


def solution(mesh):
    in_specs = (P(None, "gx", "gy", None), P(None, "gx", "gy", None), P(), P(), P())
    out_specs = (P(None, "gx", "gy", None), P(None, "gx", "gy", None), P(), P(), P())
    return jax.shard_map(local, mesh=mesh, in_specs=in_specs, out_specs=out_specs, check_vma=False)
```
